32 devices in a mesh: ctx: 8 (over y, x, core), dp: 4 (over z).
Axes of the slice: x: 2, y: 2, z: 4, core: 2. Of those that a mesh axis runs over, the one named last changes fastest.
Arguments:
- ids: int32 [3072], P('ctx'), may hold values from 0 to 511
- embed_table: bfloat16 [512, 4096], P(None, 'dp'), may hold values from -6 to 6
- norm_gain: bfloat16 [4096], P('dp'), may hold values from 0.25 to 1.75
- w_query: bfloat16 [4096, 4096], P('ctx', 'dp'), may hold values from -0.09375 to 0.09375
- w_key: bfloat16 [4096, 4096], P('ctx', 'dp'), may hold values from -0.09375 to 0.09375
- w_value: bfloat16 [4096, 4096], P('ctx', 'dp'), may hold values from -0.09375 to 0.09375
- short_filter: float32 [3, 3, 4096], P(None, None, 'dp'), may hold values from -4 to 4
- pole_rate: float32 [4096, 16], P('dp'), may hold values from 1.6276042e-05 to 0.05
- residue: float32 [4096, 16], P('dp'), may hold values from -2 to 2
- skip_gain: float32 [4096], P('dp'), may hold values from -4 to 4
- w_out: bfloat16 [4096, 4096], P('ctx', 'dp'), may hold values from -0.09375 to 0.09375
Outputs:
- block_out: bfloat16 [3072, 4096], P('ctx', 'dp')
The draws below stay inside these ranges and needn't reach their ends.
All inputs are finite; a program needn't handle non-finite values.
Results may differ from the reference program's by a relative error of at most 0.0082.
Values may be sent and summed in bfloat16 or wider, within the bound.
A program may use at most 128 MiB of HBM per device.

```python
import math
import jax
import jax.numpy as jnp
import numpy as np
from jax import lax

D = 4096
VOCAB = 512
MODES = 16
TAPS = 3
TOKENS = 3072


def draw_pole_rate(key, part):
    key_pick = jax.random.fold_in(key, 11)
    key_fast = jax.random.fold_in(key, 12)
    key_slow = jax.random.fold_in(key, 13)
    selector = jax.random.uniform(key_pick, (D, MODES), jnp.float32)
    fast_rates = jnp.exp(jax.random.uniform(key_fast, (D, MODES), jnp.float32, math.log(0.02), math.log(0.05)))
    slow_rates = jnp.exp(jax.random.uniform(key_slow, (D, MODES), jnp.float32, math.log(0.05), math.log(2.0))) / TOKENS
    share_fast = 0.5
    return jnp.where(selector < share_fast, fast_rates, slow_rates)


def with_ends(array, key, least, top_value):
    extent = array.shape
    spot = [jax.random.randint(jax.random.fold_in(key, axis), (), 0, extent[axis]) for axis in range(len(extent))]
    array = array.at[tuple(spot)].set(least)
    longest = extent.index(max(extent))
    spot[longest] = (spot[longest] + 1) % extent[longest]
    return array.at[tuple(spot)].set(top_value)


def shard_levels(key, dims, shards, least, top_value):
    gain, own = 1.0, jax.random.fold_in(key, 6)
    for axis_at, blocks in shards:
        steps = jnp.exp(jax.random.uniform(jax.random.fold_in(own, axis_at), (blocks,), jnp.float32, least / len(shards), top_value / len(shards)))
        gain = gain * jnp.repeat(steps, dims[axis_at] // blocks).reshape([-1 if axis == axis_at else 1 for axis in range(len(dims))])
    return gain


def cumulative_ranks(count, skew):
    loads = [(1 << 20) // math.isqrt(grade ** skew) + 1 for grade in range(1, count + 1)]
    width = 1 + sum(loads) // (1 << 30)
    return np.cumsum(np.array([max(1, weight // width) for weight in loads]))


def ranked_ids(stream_key, extent, amount, lean):
    grid = cumulative_ranks(amount, lean)
    pick = jax.random.randint(jax.random.fold_in(stream_key, 1), extent, 0, int(grid[amount - 1]))
    grade = jnp.searchsorted(jnp.asarray(grid, jnp.int32), pick, side="right")
    return jax.random.permutation(jax.random.fold_in(stream_key, 2), amount)[grade].astype(jnp.int32)


def gaussian(key, shape, deviation, bound, split=(), held_as=jnp.bfloat16):
    result = jax.random.normal(key, shape, jnp.float32) * deviation
    if len(split) > 0:
        result = shard_levels(key, shape, split, -0.22, 0.18) * result
    return jnp.clip(result, min=-bound, max=bound).astype(held_as)


def setup_inputs(seed: int = 0) -> dict:
    arg_keys = jax.random.split(jax.random.key(seed), 12)
    return {
        "ids": with_ends(ranked_ids(arg_keys[0], (TOKENS,), VOCAB, 2), jax.random.fold_in(arg_keys[0], 3), 0, VOCAB - 1).astype(jnp.int32),
        "embed_table": gaussian(arg_keys[1], (VOCAB, D), 1.0, 6.0, ((1, 4),)),
        "norm_gain": jnp.clip(1.0 + 0.15 * jax.random.normal(arg_keys[2], (D,), jnp.float32), 0.25, 1.75).astype(jnp.bfloat16),
        "w_query": gaussian(arg_keys[3], (D, D), D ** -0.5, 0.09375, ((0, 8), (1, 4))),
        "w_key": gaussian(arg_keys[4], (D, D), D ** -0.5, 0.09375, ((0, 8), (1, 4))),
        "w_value": gaussian(arg_keys[5], (D, D), D ** -0.5, 0.09375, ((0, 8), (1, 4))),
        "short_filter": gaussian(arg_keys[6], (TAPS, 3, D), 0.6, 4.0, ((2, 4),), jnp.float32),
        "pole_rate": draw_pole_rate(jax.random.fold_in(arg_keys[11], 71), 0),
        "residue": gaussian(arg_keys[8], (D, MODES), 0.3, 2.0, ((0, 4),), jnp.float32),
        "skip_gain": gaussian(arg_keys[9], (D,), 1.0, 4.0, ((0, 4),), jnp.float32),
        "w_out": gaussian(arg_keys[10], (D, D), D ** -0.5, 0.09375, ((0, 8), (1, 4))),
    }


def reference(ids, embed_table, norm_gain, w_query, w_key, w_value, short_filter, pole_rate, residue, skip_gain, w_out):
    embedded = embed_table[ids]
    floated = embedded.astype(jnp.float32)
    scale = lax.rsqrt(lax.optimization_barrier(jnp.mean(floated * floated, axis=1, keepdims=True)) + 1e-06)
    normed = (floated * scale * norm_gain.astype(jnp.float32)[None, :]).astype(jnp.bfloat16)
    convs = []
    for index, weight in enumerate((w_query, w_key, w_value)):
        proj = jnp.dot(normed, weight, preferred_element_type=jnp.float32).astype(jnp.bfloat16)
        padded = jnp.pad(proj.astype(jnp.float32), ((TAPS - 1, 0), (0, 0)))
        conv = jnp.zeros((TOKENS, D), jnp.float32)
        for tap in range(TAPS):
            conv = conv + short_filter[tap, index][None, :] * padded[TAPS - 1 - tap:TAPS - 1 - tap + TOKENS]
        convs.append(conv)
    query_conv, key_conv, value_conv = convs
    gated = key_conv * value_conv
    decay = jnp.exp(-pole_rate)
    strength = residue * jnp.sqrt(2.0 * pole_rate)

    def advance(state, row):
        state = decay * state + row[:, None]
        return (state, lax.optimization_barrier(jnp.sum(strength * state, axis=1)))
    final_state, filtered = lax.scan(advance, jnp.zeros((D, MODES), jnp.float32), gated)
    long_conv = filtered + skip_gain[None, :] * gated
    mixed = (query_conv * long_conv).astype(jnp.bfloat16)
    output = jnp.dot(mixed, w_out, preferred_element_type=jnp.float32)
    return (floated + output).astype(jnp.bfloat16)
```

```python
import math

import jax
import jax.numpy as jnp
from jax import lax

from jax.experimental import pallas as pl
from jax.experimental.pallas import tpu as pltpu
from jax.sharding import PartitionSpec as P

MESH = pl.DeviceIdType.MESH
LANES = 128
SUBLANES = 8
VMEM_BYTES = 36 << 20


def shifted(value, axis, steps):
    count = lax.axis_size(axis)
    initial, last = (max(0, -steps), min(count, count - steps))
    return lax.ppermute(value, axis, [(source, source + steps) for source in range(initial, last)])


def entering_2(value, axis, combine, identity):
    peers, index = (lax.axis_size(axis), lax.axis_index(axis))
    everything = jax.tree.map(lambda part: lax.all_gather(part, axis), value)
    start = jax.tree.map(
        lambda part, zero: jnp.broadcast_to(jnp.asarray(zero, part.dtype), part.shape),
        value,
        identity,
    )

    def turn(k, before):
        reached = k < index
        new = combine(before, jax.tree.map(lambda part: part[k], everything))
        return jax.tree.map(lambda a, b: jnp.where(reached, a, b), new, before)

    return lax.fori_loop(0, peers, turn, start)


def shards(
    ids,
    embed_table,
    norm_gain,
    w_query,
    w_key,
    w_value,
    short_filter,
    pole_rate,
    residue,
    skip_gain,
    w_out,
):
    highest = lax.Precision.HIGHEST
    vocab = embed_table.shape[0]
    channels = w_query.shape[1]
    one_hot = (ids[:, None] == jnp.arange(vocab, dtype=jnp.int32)[None, :]).astype(jnp.bfloat16)
    embedded = jnp.dot(one_hot, embed_table, preferred_element_type=jnp.float32).astype(
        jnp.bfloat16
    )
    full_rows, full_gain = (
        lax.all_gather(embedded, "dp", axis=1, tiled=True),
        lax.all_gather(norm_gain, "dp", axis=0, tiled=True),
    )
    floated = full_rows.astype(jnp.float32)
    scale = lax.rsqrt(jnp.mean(floated * floated, axis=1, keepdims=True) + 1e-06)
    normed = (floated * scale * full_gain.astype(jnp.float32)[None, :]).astype(jnp.bfloat16)
    tok_rows = normed.shape[0]

    def add_rows(piece):
        return jnp.dot(normed, piece, preferred_element_type=jnp.float32)

    query_proj = add_rows(lax.all_gather(w_query, "ctx", axis=0, tiled=True))
    key_proj = add_rows(lax.all_gather(w_key, "ctx", axis=0, tiled=True))
    value_proj = add_rows(lax.all_gather(w_value, "ctx", axis=0, tiled=True))
    projected = jnp.concatenate([query_proj, key_proj, value_proj], axis=1).astype(jnp.bfloat16)
    taps = short_filter.shape[0]
    previous = shifted(projected[tok_rows - (taps - 1) :], "ctx", 1)
    extended = jnp.concatenate([previous, projected], axis=0).astype(jnp.float32)
    filt_rows = short_filter.reshape(taps, 3 * channels)
    convolved = jnp.zeros((tok_rows, 3 * channels), jnp.float32)
    for tap in range(taps):
        convolved = (
            convolved
            + filt_rows[tap][None, :] * extended[taps - 1 - tap : taps - 1 - tap + tok_rows]
        )
    query_conv = convolved[:, :channels]
    gated = convolved[:, channels : 2 * channels] * convolved[:, 2 * channels :]
    sub_len = math.gcd(tok_rows, 64)
    blocks = tok_rows // sub_len
    lag_index = jnp.arange(sub_len, dtype=jnp.int32)
    lags = lag_index.astype(jnp.float32)
    strength = residue * jnp.sqrt(2.0 * pole_rate)
    kernel = jnp.einsum(
        "lck,ck->lc", jnp.exp(-pole_rate[None] * lags[:, None, None]), strength, precision=highest
    )
    offsets = lag_index[:, None] - lag_index[None, :]
    toeplitz = jnp.where((offsets >= 0)[:, :, None], kernel[jnp.maximum(offsets, 0)], 0.0)
    pieces = gated.reshape(blocks, sub_len, channels)
    inside = jnp.einsum("tsc,bsc->btc", toeplitz, pieces, precision=highest)
    tail_decay = jnp.exp(-pole_rate[None] * (sub_len - 1.0 - lags)[:, None, None])
    block_ends = jnp.einsum("sck,bsc->bck", tail_decay, pieces, precision=highest)
    step_decay = jnp.exp(-pole_rate * float(sub_len))

    def advance(state, block_end):
        return (step_decay * state + block_end, state)

    device_end, entering = lax.scan(advance, jnp.zeros_like(step_decay), block_ends)
    device_decay = jnp.exp(-pole_rate * float(tok_rows))

    def combine(earlier, later):
        return (earlier[0] * later[0], later[0] * earlier[1] + later[1])

    decay_total, incoming = entering_2(
        (device_decay, device_end),
        "ctx",
        combine,
        (jnp.ones_like(device_decay), jnp.zeros_like(device_end)),
    )
    block_pos = jnp.arange(blocks, dtype=jnp.float32) * float(sub_len)
    states_in = entering + jnp.exp(-pole_rate[None] * block_pos[:, None, None]) * incoming[None]
    lead = jnp.exp(-pole_rate[None] * (lags + 1.0)[:, None, None]) * strength[None]
    carried = jnp.einsum("tck,bck->btc", lead, states_in, precision=highest)
    long_conv = (inside + carried).reshape(tok_rows, channels) + skip_gain[None, :] * gated
    mixed = (query_conv * long_conv).astype(jnp.bfloat16)
    all_mixed = lax.all_gather(mixed, "dp", axis=1, tiled=True)
    output = jnp.dot(
        all_mixed,
        lax.all_gather(w_out, "ctx", axis=0, tiled=True),
        preferred_element_type=jnp.float32,
    )
    return (embedded.astype(jnp.float32) + output).astype(jnp.bfloat16)


def remote(src, dst, send, recv, **where):
    return pltpu.make_async_remote_copy(
        src_ref=src,
        dst_ref=dst,
        send_sem=send,
        recv_sem=recv,
        device_id=where,
        device_id_type=MESH,
    )


def greet(ctx_peers, dp_peers):
    barrier = pltpu.get_barrier_semaphore()
    for peer in ctx_peers:
        pl.semaphore_signal(barrier, inc=1, device_id={"ctx": peer}, device_id_type=MESH)
    for peer in dp_peers:
        pl.semaphore_signal(barrier, inc=1, device_id={"dp": peer}, device_id_type=MESH)
    pl.semaphore_wait(barrier, len(ctx_peers) + len(dp_peers))


def flip(index, bit):
    return index + bit - 2 * bit * (lax.rem(index // bit, 2))


def project_kernel(
    n_ctx,
    n_dp,
    ids_ref,
    gain_ref,
    table_ref,
    wq_ref,
    wk_ref,
    wv_ref,
    ids_out,
    rows_out,
    tab,
    own,
    weights,
    part,
    land,
    mine,
    sums,
    scales,
    gains,
    z_send,
    z_recv,
    core_send,
    core_recv,
    w_send,
    w_recv,
    id_send,
    id_recv,
    sum_send,
    sum_recv,
    gain_send,
    gain_recv,
    rs_send,
    rs_recv,
    local,
):
    me, at = lax.axis_index("ctx"), lax.axis_index("dp")
    vocab, width = table_ref.shape
    depth = wq_ref.shape[0]
    chips = n_ctx // 2
    lanes = wq_ref.shape[1] // n_ctx
    chunks = z_send.shape[1]
    part_rows = vocab // chunks
    half_rows = part_rows // 2
    chip, core = me // 2, lax.rem(me, 2)
    partner = flip(me, 1)
    relatives = [me, flip(me, 2), flip(me, 4), flip(flip(me, 2), 4)]
    ctx_peers = [lax.rem(me + d, n_ctx) for d in range(1, n_ctx)]
    dp_peers = [lax.rem(at + d, n_dp) for d in range(1, n_dp)]
    source, above, below = at == chip, at > chip, at < chip

    loads = [pltpu.make_async_copy(table_ref, own, local.at[0])]
    for r, peer in enumerate(relatives):
        for w, weight in enumerate((wq_ref, wk_ref, wv_ref)):
            column = pl.multiple_of(peer * lanes, lanes)
            loads.append(
                pltpu.make_async_copy(
                    weight.at[:, pl.ds(column, lanes)],
                    weights.at[
                        pl.ds(pl.multiple_of(core * depth, depth), depth),
                        pl.ds((r * 3 + w) * lanes, lanes),
                    ],
                    local.at[1 + r * 3 + w],
                )
            )
    for copy in loads:
        copy.start()
    id_rows = ids_ref.shape[0]
    ids_out[me] = jnp.concatenate(
        [ids_ref[...], jnp.zeros((SUBLANES - id_rows, LANES), ids_ref.dtype)], axis=0
    )
    greet(ctx_peers, dp_peers)

    def half(k, which):
        return pl.ds(pl.multiple_of(k * part_rows + which * half_rows, half_rows), half_rows)

    def z_copy(src, k, way, peer):
        piece = half(k, core)
        return remote(src.at[piece], tab.at[piece], z_send.at[way, k], z_recv.at[k], dp=peer)

    def core_copy(k):
        piece = half(k, core)
        return remote(tab.at[piece], tab.at[piece], core_send.at[k], core_recv.at[k], ctx=partner)

    def core_arrival(k):
        piece = half(k, 1 - core)
        return remote(tab.at[piece], tab.at[piece], core_send.at[k], core_recv.at[k], ctx=partner)

    can_up, can_down = at < n_dp - 1, at > 0
    for k in range(chunks):

        @pl.when(source & can_up)
        def _():
            z_copy(table_ref, k, 0, at + 1).start()

        @pl.when(source & can_down)
        def _():
            z_copy(table_ref, k, 1, at - 1).start()

    swaps = []
    for r, peer in enumerate(relatives):
        for w, weight in enumerate((wq_ref, wk_ref, wv_ref)):
            column = pl.multiple_of(flip(peer, 1) * lanes, lanes)
            swaps.append(
                remote(
                    weight.at[:, pl.ds(column, lanes)],
                    weights.at[
                        pl.ds(pl.multiple_of(core * depth, depth), depth),
                        pl.ds((r * 3 + w) * lanes, lanes),
                    ],
                    w_send.at[r * 3 + w],
                    w_recv.at[r * 3 + w],
                    ctx=partner,
                )
            )
    for copy in swaps:
        copy.start()
    sends = []
    for d, peer in enumerate(ctx_peers):
        sends.append(remote(ids_out.at[me], ids_out.at[me], id_send.at[d], id_recv.at[me], ctx=peer))
        sends[-1].start()

    loads[0].wait()
    groups = vocab // LANES
    lines = []
    for g in range(groups):
        block = own[g * LANES : (g + 1) * LANES, :].astype(jnp.float32)
        total = jnp.sum(block * block, axis=1, keepdims=True)
        lines.append(jnp.broadcast_to(total, (LANES, LANES)).T[:1, :])
    lines.append(jnp.zeros((SUBLANES - groups, LANES), jnp.float32))
    sums[at] = jnp.concatenate(lines, axis=0)
    for d, peer in enumerate(dp_peers):
        sends.append(remote(sums.at[at], sums.at[at], sum_send.at[d], sum_recv.at[at], dp=peer))
        sends[-1].start()

    def gain_copy(d):
        return remote(gains, gains, gain_send.at[d], gain_recv.at[0], dp=dp_peers[d])

    @pl.when(source)
    def _():
        gains[...] = jnp.broadcast_to(gain_ref[...].astype(jnp.float32), gains.shape)
        for d in range(n_dp - 1):
            gain_copy(d).start()
        tab[...] = own[...]

    for peer in dp_peers:
        remote(sums.at[peer], sums.at[peer], sum_send.at[0], sum_recv.at[peer], dp=peer).wait_recv()
    total = sums[0]
    for b in range(1, n_dp):
        total = total + sums[b]
    scale = lax.rsqrt(total / (n_dp * width) + 1e-06)
    for g in range(groups):
        scales[g * LANES : (g + 1) * LANES, :] = jnp.broadcast_to(
            scale[g : g + 1, :], (LANES, LANES)
        ).T

    @pl.when(jnp.logical_not(source))
    def _():
        gain_copy(0).wait_recv()

    for copy in loads[1:]:
        copy.wait()
    for copy in swaps:
        copy.wait_recv()

    def rs_copy(r, k):
        piece = pl.ds(k * part_rows, part_rows)
        return remote(
            part.at[r - 1, piece],
            land.at[r - 1, piece],
            rs_send.at[r - 1, k],
            rs_recv.at[r - 1, k],
            ctx=relatives[r],
        )

    span = 3 * lanes
    for k in range(chunks):

        @pl.when(above)
        def _():
            z_copy(tab, k, 0, at).wait_recv()

            @pl.when(can_up)
            def _():
                z_copy(tab, k, 0, at + 1).start()

        @pl.when(below)
        def _():
            z_copy(tab, k, 1, at).wait_recv()

            @pl.when(can_down)
            def _():
                z_copy(tab, k, 1, at - 1).start()

        @pl.when(jnp.logical_not(source))
        def _():
            core_copy(k).start()
            core_arrival(k).wait_recv()

        piece = slice(k * part_rows, (k + 1) * part_rows)
        by_row = jnp.concatenate([scales[piece, :]] * (width // LANES), axis=1)
        normed = (tab[piece, :].astype(jnp.float32) * by_row * gains[:1, :]).astype(jnp.bfloat16)
        for r in range(1, chips):
            part[r - 1, piece, :] = jnp.dot(
                normed,
                weights[:, r * span : (r + 1) * span],
                preferred_element_type=jnp.float32,
            ).astype(jnp.bfloat16)
            rs_copy(r, k).start()
        mine[piece, :] = jnp.dot(normed, weights[:, :span], preferred_element_type=jnp.float32)

    for k in range(chunks):
        piece = slice(k * part_rows, (k + 1) * part_rows)
        total = mine[piece, :]
        for r in range(1, chips):
            rs_copy(r, k).wait_recv()
            total = total + land[r - 1, piece, :].astype(jnp.float32)
        rows_out[piece, :] = total.astype(jnp.bfloat16)

    for peer in ctx_peers:
        remote(ids_out.at[peer], ids_out.at[peer], id_send.at[0], id_recv.at[peer], ctx=peer).wait_recv()
    for copy in sends + swaps:
        copy.wait_send()

    @pl.when(source)
    def _():
        for d in range(n_dp - 1):
            gain_copy(d).wait_send()

    for k in range(chunks):

        @pl.when((source | above) & can_up)
        def _():
            z_copy(tab, k, 0, at).wait_send()

        @pl.when((source | below) & can_down)
        def _():
            z_copy(tab, k, 1, at).wait_send()

        @pl.when(jnp.logical_not(source))
        def _():
            core_copy(k).wait_send()

        for r in range(1, chips):
            rs_copy(r, k).wait_send()


def project(n_ctx, n_dp, ids, gain, table, w_query, w_key, w_value):
    vocab, width = table.shape
    depth, lanes = w_query.shape[0], w_query.shape[1] // n_ctx
    chips = n_ctx // 2
    chunks = vocab // LANES
    anywhere = pl.BlockSpec(memory_space=pl.ANY)
    whole = pl.BlockSpec(memory_space=pltpu.VMEM)
    dma = pltpu.SemaphoreType.DMA
    return pl.pallas_call(
        lambda *refs: project_kernel(n_ctx, n_dp, *refs),
        name="project",
        out_shape=(
            jax.ShapeDtypeStruct((n_ctx, SUBLANES, LANES), ids.dtype),
            jax.ShapeDtypeStruct((vocab, 3 * lanes), w_query.dtype),
        ),
        in_specs=[whole] * 2 + [anywhere] * 4,
        out_specs=[whole] * 2,
        scratch_shapes=[
            pltpu.VMEM((vocab, width), table.dtype),
            pltpu.VMEM((vocab, width), table.dtype),
            pltpu.VMEM((2 * depth, chips * 3 * lanes), w_query.dtype),
            pltpu.VMEM((chips - 1, vocab, 3 * lanes), w_query.dtype),
            pltpu.VMEM((chips - 1, vocab, 3 * lanes), w_query.dtype),
            pltpu.VMEM((vocab, 3 * lanes), jnp.float32),
            pltpu.VMEM((n_dp, SUBLANES, LANES), jnp.float32),
            pltpu.VMEM((vocab, LANES), jnp.float32),
            pltpu.VMEM((SUBLANES, width), jnp.float32),
            dma((2, chunks)),
            dma((chunks,)),
            dma((chunks,)),
            dma((chunks,)),
            dma((chips * 3,)),
            dma((chips * 3,)),
            dma((n_ctx - 1,)),
            dma((n_ctx,)),
            dma((n_dp - 1,)),
            dma((n_dp,)),
            dma((n_dp - 1,)),
            dma((1,)),
            dma((chips - 1, chunks)),
            dma((chips - 1, chunks)),
            dma((1 + chips * 3,)),
        ],
        compiler_params=pltpu.CompilerParams(
            collective_id=0, has_side_effects=True, vmem_limit_bytes=VMEM_BYTES
        ),
    )(ids, gain, table, w_query, w_key, w_value)


def mix_kernel(
    me_ref,
    ids_ref,
    rows_ref,
    filt_ref,
    rate_ref,
    residue_ref,
    skip_ref,
    out_ref,
    proj,
    gated,
    query,
):
    vocab = rows_ref.shape[0]
    taps = filt_ref.shape[0]
    modes = rate_ref.shape[0]
    segments, steps, lanes = out_ref.shape
    lead = proj.shape[1] - segments * steps
    mine = pl.ds(pl.multiple_of(me_ref[0] * lanes, lanes), lanes)
    rows = rows_ref[...]
    pieces = steps // lanes
    per_segment = ids_ref.shape[1]
    names = lax.broadcasted_iota(jnp.int32, (lanes, vocab), 1)
    for s in range(segments):
        by_lane = ids_ref[s].astype(jnp.float32)
        square = jnp.concatenate(
            [by_lane, jnp.zeros((lanes - per_segment, lanes), jnp.float32)], axis=0
        )
        columns = square.T.astype(jnp.int32)
        one_hot = jnp.concatenate(
            [
                (columns[:, p : p + 1] == names).astype(jnp.float32).astype(jnp.bfloat16)
                for p in range(pieces)
            ],
            axis=0,
        )
        picked = jnp.dot(one_hot, rows, preferred_element_type=jnp.float32)
        for w in range(3):
            proj[w, pl.ds(lead + s, steps, stride=segments), :] = picked[:, w * lanes : (w + 1) * lanes]
    place_of = lax.broadcasted_iota(jnp.int32, (segments, lanes), 0)

    def later(value, by):
        return jnp.where(place_of >= by, pltpu.roll(value, by, 0), 0.0)

    end = proj.shape[1]
    for tap in range(1, taps):
        for w in range(3):
            tail = proj[w, end - tap * segments : end - (tap - 1) * segments, :]
            proj[w, lead - tap * segments : lead - (tap - 1) * segments, :] = later(tail, 1)
    size = lanes

    def convolve(n, carry):
        start = n * size + lead
        conv = [jnp.zeros((size, lanes), jnp.float32) for _ in range(3)]
        for tap in range(taps):
            here = pl.ds(pl.multiple_of(start - tap * segments, segments), size)
            for w in range(3):
                conv[w] = conv[w] + filt_ref[tap, w : w + 1, mine] * proj[w, here, :]
        there = pl.ds(pl.multiple_of(n * size, size), size)
        query[there, :] = conv[0]
        gated[there, :] = conv[1] * conv[2]
        return carry

    lax.fori_loop(0, segments * steps // size, convolve, 0)

    def spread_rows(row):
        return jnp.broadcast_to(row, (segments, lanes))

    rate, residue = rate_ref[:, mine], residue_ref[:, mine]
    decay = [spread_rows(jnp.exp(-rate[m : m + 1, :])) for m in range(modes)]
    unroll = 4

    def ends(n, state):
        for u in range(unroll):
            row = gated[pl.ds(pl.multiple_of((n * unroll + u) * segments, segments), segments), :]
            state = tuple(d * s + row for d, s in zip(decay, state))
        return state

    zero = jnp.zeros((segments, lanes), jnp.float32)
    state = lax.fori_loop(0, steps // unroll, ends, (zero,) * modes)
    entering = []
    for m in range(modes):
        value = later(state[m], 1)
        by = 1
        while by < segments:
            jump = jnp.exp(-rate[m : m + 1, :] * float(steps * by))
            value = value + jump * later(value, by)
            by *= 2
        entering.append(value)
    strength = [
        spread_rows(residue[m : m + 1, :] * jnp.sqrt(2.0 * rate[m : m + 1, :])) for m in range(modes)
    ]
    skip = spread_rows(skip_ref[:, mine])

    def advance(n, state):
        for u in range(unroll):
            here = pl.ds(pl.multiple_of((n * unroll + u) * segments, segments), segments)
            row = gated[here, :]
            sums = [skip * row, None]
            new = []
            for m in range(modes):
                now = decay[m] * state[m] + row
                new.append(now)
                term = strength[m] * now
                sums[m % 2] = term if sums[m % 2] is None else sums[m % 2] + term
            state = tuple(new)
            query[here, :] = query[here, :] * (sums[0] + sums[1])
        return state

    lax.fori_loop(0, steps // unroll, advance, tuple(entering))
    for s in range(segments):
        out_ref[s] = query[pl.ds(s, steps, stride=segments), :].astype(jnp.bfloat16)


def mix(me, ids, rows, filt, rate, residue, skip, segments, steps):
    whole = pl.BlockSpec(memory_space=pltpu.VMEM)
    lanes = rows.shape[1] // 3
    lead = segments * (filt.shape[0] - 1)
    return pl.pallas_call(
        mix_kernel,
        name="mix",
        out_shape=jax.ShapeDtypeStruct((segments, steps, lanes), jnp.bfloat16),
        in_specs=[pl.BlockSpec(memory_space=pltpu.SMEM)] + [whole] * 6,
        out_specs=whole,
        scratch_shapes=[
            pltpu.VMEM((3, lead + segments * steps, lanes), jnp.float32),
            pltpu.VMEM((segments * steps, lanes), jnp.float32),
            pltpu.VMEM((segments * steps, lanes), jnp.float32),
        ],
        compiler_params=pltpu.CompilerParams(vmem_limit_bytes=VMEM_BYTES),
    )(me, ids, rows, filt, rate, residue, skip)


def collect_kernel(
    n_ctx,
    n_dp,
    mixed_ref,
    weight_ref,
    mixed_out,
    weight_out,
    own_mixed,
    own_weight,
    a_send,
    slot_recv,
    z_send,
    w_send,
    w_recv,
    core_send,
    core_recv,
    local,
):
    me, at = lax.axis_index("ctx"), lax.axis_index("dp")
    depth, lanes = weight_ref.shape[0], mixed_ref.shape[2]
    bits = [1 << b for b in range(n_ctx.bit_length() - 1)]
    ctx_peers = [lax.rem(me + d, n_ctx) for d in range(1, n_ctx)]
    near = [(at - 1, at > 0), (at + 1, at < n_dp - 1)]
    barrier = pltpu.get_barrier_semaphore()
    dp_peers = [lax.rem(at + d, n_dp) for d in range(1, n_dp)]
    greet(ctx_peers, dp_peers)
    partner, side, up = flip(me, 1), flip(me, 2), flip(me, 4)
    across = flip(side, 4)
    half = depth // 2

    def slot(source, k):
        start = (source * n_ctx + k) * lanes
        return mixed_out.at[:, pl.ds(pl.multiple_of(start, lanes), lanes)]

    def turn(d, peer):
        return remote(mixed_ref.at[peer], slot(at, me), a_send.at[d - 1], slot_recv.at[at, me], ctx=peer)

    def block(owner, first=0, count=None):
        count = depth if count is None else count
        start = pl.multiple_of(owner * depth + first, half)
        return weight_out.at[pl.ds(start, count)]

    for d, peer in enumerate(ctx_peers):
        turn(d + 1, peer).start()
    into = [
        pltpu.make_async_copy(mixed_ref.at[me], own_mixed, local.at[0]),
        pltpu.make_async_copy(weight_ref, own_weight, local.at[1]),
    ]
    for copy in into:
        copy.start()

    def z_copy(source, d, way, hop, peer):
        k = lax.rem(me + d, n_ctx)
        src = mixed_ref.at[me] if hop == 0 and d == 0 else slot(source, k)
        return remote(src, slot(source, k), z_send.at[way, hop, d], slot_recv.at[source, k], dp=peer)

    def recv(source, d):
        k = lax.rem(me + d, n_ctx)
        z_copy_like = remote(slot(source, k), slot(source, k), z_send.at[0, 0, d], slot_recv.at[source, k], ctx=partner)
        z_copy_like.wait_recv()

    def first_hop(d):
        @pl.when(at < n_dp - 1)
        def _():
            z_copy(at, d, 0, 0, at + 1).start()

        @pl.when(at > 0)
        def _():
            z_copy(at, d, 1, 0, at - 1).start()

    first_hop(0)
    own = [
        remote(weight_ref, block(me), w_send.at[0], w_recv.at[0], ctx=side),
        remote(weight_ref, block(me), w_send.at[1], w_recv.at[1], ctx=up),
        remote(weight_ref, block(me), w_send.at[2], w_recv.at[2], ctx=partner),
    ]
    own[2].start()
    for copy in into:
        copy.wait()
    out = [
        pltpu.make_async_copy(own_mixed, slot(at, me), local.at[0]),
        pltpu.make_async_copy(own_weight, block(me), local.at[1]),
    ]
    for copy in out:
        copy.start()
    for d in range(1, n_ctx):
        recv(at, d)
        first_hop(d)
    own[0].start()
    own[1].start()

    for hop in range(1, n_dp):
        for d in range(n_ctx):

            @pl.when(at - hop >= 0)
            def _():
                recv(at - hop, d)

                if hop < n_dp - 1:

                    @pl.when(at < n_dp - 1)
                    def _():
                        z_copy(at - hop, d, 0, hop, at + 1).start()

            @pl.when(at + hop <= n_dp - 1)
            def _():
                recv(at + hop, d)

                if hop < n_dp - 1:

                    @pl.when(at > 0)
                    def _():
                        z_copy(at + hop, d, 1, hop, at - 1).start()

        if hop == 1:
            own[0].wait_recv()
            own[1].wait_recv()
            passed = [
                remote(block(side, 0, half), block(side, 0, half), w_send.at[3], w_recv.at[3], ctx=up),
                remote(block(up, half, half), block(up, half, half), w_send.at[4], w_recv.at[4], ctx=side),
                remote(block(side), block(side), core_send.at[0], core_recv.at[0], ctx=partner),
                remote(block(up), block(up), core_send.at[1], core_recv.at[1], ctx=partner),
            ]
            for copy in passed:
                copy.start()
    passed[0].wait_recv()
    passed[1].wait_recv()
    last = [
        remote(block(across, 0, half), block(across, 0, half), core_send.at[2], core_recv.at[2], ctx=partner),
        remote(block(across, half, half), block(across, half, half), core_send.at[3], core_recv.at[3], ctx=partner),
    ]
    for copy in last:
        copy.start()
    own[2].wait_recv()
    passed[2].wait_recv()
    passed[3].wait_recv()
    for copy in last:
        copy.wait_recv()
    for copy in own + passed + last:
        copy.wait_send()
    for d, peer in enumerate(ctx_peers):
        turn(d + 1, peer).wait_send()
    for hop in range(n_dp - 1):
        for d in range(n_ctx):

            @pl.when((at - hop >= 0) & (at < n_dp - 1))
            def _():
                z_copy(at - hop, d, 0, hop, at + 1).wait_send()

            @pl.when((at + hop <= n_dp - 1) & (at > 0))
            def _():
                z_copy(at + hop, d, 1, hop, at - 1).wait_send()

    for copy in out:
        copy.wait()


def collect(n_ctx, n_dp, mixed, weight):
    depth, columns = weight.shape
    steps, lanes = mixed.shape[1:]
    anywhere = pl.BlockSpec(memory_space=pl.ANY)
    dma = pltpu.SemaphoreType.DMA
    return pl.pallas_call(
        lambda *refs: collect_kernel(n_ctx, n_dp, *refs),
        name="collect",
        out_shape=(
            jax.ShapeDtypeStruct((steps, n_dp * n_ctx * lanes), mixed.dtype),
            jax.ShapeDtypeStruct((n_ctx * depth, columns), weight.dtype),
        ),
        in_specs=[anywhere] * 2,
        out_specs=[anywhere] * 2,
        scratch_shapes=[
            pltpu.VMEM((steps, lanes), mixed.dtype),
            pltpu.VMEM((depth, columns), weight.dtype),
            dma((n_ctx - 1,)),
            dma((n_dp, n_ctx)),
            dma((2, n_dp - 1, n_ctx)),
            dma((5,)),
            dma((5,)),
            dma((4,)),
            dma((4,)),
            dma((2,)),
        ],
        compiler_params=pltpu.CompilerParams(
            collective_id=1, has_side_effects=True, vmem_limit_bytes=8 << 20
        ),
    )(mixed, weight)


def by_channel(
    n_ctx,
    n_dp,
    ids,
    embed_table,
    norm_gain,
    w_query,
    w_key,
    w_value,
    short_filter,
    pole_rate,
    residue,
    skip_gain,
    w_out,
):
    vocab = embed_table.shape[0]
    tok_rows = ids.shape[0]
    all_ids, rows = project(
        n_ctx,
        n_dp,
        ids.reshape(-1, LANES),
        norm_gain[None, :],
        embed_table,
        w_query,
        w_key,
        w_value,
    )
    mixed = mix(
        lax.axis_index("ctx").astype(jnp.int32).reshape(1),
        all_ids,
        rows,
        short_filter,
        pole_rate.T,
        residue.T,
        skip_gain[None, :],
        n_ctx,
        tok_rows,
    )
    all_mixed, all_rows = collect(n_ctx, n_dp, mixed, w_out)
    one_hot = (ids[:, None] == jnp.arange(vocab, dtype=jnp.int32)[None, :]).astype(jnp.bfloat16)
    embedded = jnp.dot(one_hot, embed_table, preferred_element_type=jnp.float32)
    output = jnp.dot(all_mixed, all_rows, preferred_element_type=jnp.float32)
    return (embedded + output).astype(jnp.bfloat16)


def solution(mesh):
    placed = (
        P("ctx"),
        P(None, "dp"),
        P("dp"),
        P("ctx", "dp"),
        P("ctx", "dp"),
        P("ctx", "dp"),
        P(None, None, "dp"),
        P("dp", None),
        P("dp", None),
        P("dp"),
        P("ctx", "dp"),
    )
    n_ctx, n_dp = mesh.shape["ctx"], mesh.shape["dp"]

    def body(*args):
        ids, table, w_query = args[0], args[1], args[3]
        fits = (
            n_ctx == SUBLANES
            and n_ctx == 2 * n_dp
            and w_query.shape[1] == n_ctx * LANES
            and table.shape[1] == 2 * w_query.shape[0]
            and table.shape[0] % LANES == 0
            and table.shape[0] < SUBLANES * LANES
            and ids.shape[0] % LANES == 0
            and ids.shape[0] < SUBLANES * LANES
        )
        if fits:
            return by_channel(n_ctx, n_dp, *args)
        return shards(*args)

    return jax.shard_map(
        body, mesh=mesh, in_specs=placed, out_specs=P("ctx", "dp"), check_vma=False
    )
```

```python
import math

import jax
import jax.numpy as jnp
from jax import lax

from jax.experimental import pallas as pl
from jax.experimental.pallas import tpu as pltpu
from jax.sharding import PartitionSpec as P

MESH = pl.DeviceIdType.MESH
LANES = 128
SUBLANES = 8
VMEM_BYTES = 36 << 20


def shifted(value, axis, steps):
    count = lax.axis_size(axis)
    initial, last = (max(0, -steps), min(count, count - steps))
    return lax.ppermute(value, axis, [(source, source + steps) for source in range(initial, last)])


def entering_2(value, axis, combine, identity):
    peers, index = (lax.axis_size(axis), lax.axis_index(axis))
    everything = jax.tree.map(lambda part: lax.all_gather(part, axis), value)
    start = jax.tree.map(
        lambda part, zero: jnp.broadcast_to(jnp.asarray(zero, part.dtype), part.shape),
        value,
        identity,
    )

    def turn(k, before):
        reached = k < index
        new = combine(before, jax.tree.map(lambda part: part[k], everything))
        return jax.tree.map(lambda a, b: jnp.where(reached, a, b), new, before)

    return lax.fori_loop(0, peers, turn, start)


def shards(
    ids,
    embed_table,
    norm_gain,
    w_query,
    w_key,
    w_value,
    short_filter,
    pole_rate,
    residue,
    skip_gain,
    w_out,
):
    highest = lax.Precision.HIGHEST
    vocab = embed_table.shape[0]
    channels = w_query.shape[1]
    one_hot = (ids[:, None] == jnp.arange(vocab, dtype=jnp.int32)[None, :]).astype(jnp.bfloat16)
    embedded = jnp.dot(one_hot, embed_table, preferred_element_type=jnp.float32).astype(
        jnp.bfloat16
    )
    full_rows, full_gain = (
        lax.all_gather(embedded, "dp", axis=1, tiled=True),
        lax.all_gather(norm_gain, "dp", axis=0, tiled=True),
    )
    floated = full_rows.astype(jnp.float32)
    scale = lax.rsqrt(jnp.mean(floated * floated, axis=1, keepdims=True) + 1e-06)
    normed = (floated * scale * full_gain.astype(jnp.float32)[None, :]).astype(jnp.bfloat16)
    tok_rows = normed.shape[0]

    def add_rows(piece):
        return jnp.dot(normed, piece, preferred_element_type=jnp.float32)

    query_proj = add_rows(lax.all_gather(w_query, "ctx", axis=0, tiled=True))
    key_proj = add_rows(lax.all_gather(w_key, "ctx", axis=0, tiled=True))
    value_proj = add_rows(lax.all_gather(w_value, "ctx", axis=0, tiled=True))
    projected = jnp.concatenate([query_proj, key_proj, value_proj], axis=1).astype(jnp.bfloat16)
    taps = short_filter.shape[0]
    previous = shifted(projected[tok_rows - (taps - 1) :], "ctx", 1)
    extended = jnp.concatenate([previous, projected], axis=0).astype(jnp.float32)
    filt_rows = short_filter.reshape(taps, 3 * channels)
    convolved = jnp.zeros((tok_rows, 3 * channels), jnp.float32)
    for tap in range(taps):
        convolved = (
            convolved
            + filt_rows[tap][None, :] * extended[taps - 1 - tap : taps - 1 - tap + tok_rows]
        )
    query_conv = convolved[:, :channels]
    gated = convolved[:, channels : 2 * channels] * convolved[:, 2 * channels :]
    sub_len = math.gcd(tok_rows, 64)
    blocks = tok_rows // sub_len
    lag_index = jnp.arange(sub_len, dtype=jnp.int32)
    lags = lag_index.astype(jnp.float32)
    strength = residue * jnp.sqrt(2.0 * pole_rate)
    kernel = jnp.einsum(
        "lck,ck->lc", jnp.exp(-pole_rate[None] * lags[:, None, None]), strength, precision=highest
    )
    offsets = lag_index[:, None] - lag_index[None, :]
    toeplitz = jnp.where((offsets >= 0)[:, :, None], kernel[jnp.maximum(offsets, 0)], 0.0)
    pieces = gated.reshape(blocks, sub_len, channels)
    inside = jnp.einsum("tsc,bsc->btc", toeplitz, pieces, precision=highest)
    tail_decay = jnp.exp(-pole_rate[None] * (sub_len - 1.0 - lags)[:, None, None])
    block_ends = jnp.einsum("sck,bsc->bck", tail_decay, pieces, precision=highest)
    step_decay = jnp.exp(-pole_rate * float(sub_len))

    def advance(state, block_end):
        return (step_decay * state + block_end, state)

    device_end, entering = lax.scan(advance, jnp.zeros_like(step_decay), block_ends)
    device_decay = jnp.exp(-pole_rate * float(tok_rows))

    def combine(earlier, later):
        return (earlier[0] * later[0], later[0] * earlier[1] + later[1])

    decay_total, incoming = entering_2(
        (device_decay, device_end),
        "ctx",
        combine,
        (jnp.ones_like(device_decay), jnp.zeros_like(device_end)),
    )
    block_pos = jnp.arange(blocks, dtype=jnp.float32) * float(sub_len)
    states_in = entering + jnp.exp(-pole_rate[None] * block_pos[:, None, None]) * incoming[None]
    lead = jnp.exp(-pole_rate[None] * (lags + 1.0)[:, None, None]) * strength[None]
    carried = jnp.einsum("tck,bck->btc", lead, states_in, precision=highest)
    long_conv = (inside + carried).reshape(tok_rows, channels) + skip_gain[None, :] * gated
    mixed = (query_conv * long_conv).astype(jnp.bfloat16)
    all_mixed = lax.all_gather(mixed, "dp", axis=1, tiled=True)
    output = jnp.dot(
        all_mixed,
        lax.all_gather(w_out, "ctx", axis=0, tiled=True),
        preferred_element_type=jnp.float32,
    )
    return (embedded.astype(jnp.float32) + output).astype(jnp.bfloat16)


def remote(src, dst, send, recv, **where):
    return pltpu.make_async_remote_copy(
        src_ref=src,
        dst_ref=dst,
        send_sem=send,
        recv_sem=recv,
        device_id=where,
        device_id_type=MESH,
    )


def greet(ctx_peers, dp_peers):
    barrier = pltpu.get_barrier_semaphore()
    for peer in ctx_peers:
        pl.semaphore_signal(barrier, inc=1, device_id={"ctx": peer}, device_id_type=MESH)
    for peer in dp_peers:
        pl.semaphore_signal(barrier, inc=1, device_id={"dp": peer}, device_id_type=MESH)
    pl.semaphore_wait(barrier, len(ctx_peers) + len(dp_peers))


def flip(index, bit):
    return index + bit - 2 * bit * (lax.rem(index // bit, 2))


def project_kernel(
    n_ctx,
    n_dp,
    ids_ref,
    gain_ref,
    table_ref,
    wq_ref,
    wk_ref,
    wv_ref,
    ids_out,
    rows_out,
    tab,
    own,
    weights,
    part,
    land,
    mine,
    sums,
    scales,
    gains,
    z_send,
    z_recv,
    core_send,
    core_recv,
    w_send,
    w_recv,
    id_send,
    id_recv,
    sum_send,
    sum_recv,
    gain_send,
    gain_recv,
    rs_send,
    rs_recv,
    local,
):
    me, at = lax.axis_index("ctx"), lax.axis_index("dp")
    vocab, width = table_ref.shape
    depth = wq_ref.shape[0]
    chips = n_ctx // 2
    lanes = wq_ref.shape[1] // n_ctx
    chunks = rs_send.shape[1]
    part_rows = vocab // chunks
    hops = z_send.shape[1]
    hop_rows = vocab // hops
    half_rows = hop_rows // 2
    chip, core = me // 2, lax.rem(me, 2)
    partner = flip(me, 1)
    relatives = [me, flip(me, 2), flip(me, 4), flip(flip(me, 2), 4)]
    ctx_peers = [lax.rem(me + d, n_ctx) for d in range(1, n_ctx)]
    dp_peers = [lax.rem(at + d, n_dp) for d in range(1, n_dp)]
    source, above, below = at == chip, at > chip, at < chip

    loads = [pltpu.make_async_copy(table_ref, own, local.at[0])]
    for r, peer in enumerate(relatives):
        for w, weight in enumerate((wq_ref, wk_ref, wv_ref)):
            column = pl.multiple_of(peer * lanes, lanes)
            loads.append(
                pltpu.make_async_copy(
                    weight.at[:, pl.ds(column, lanes)],
                    weights.at[
                        pl.ds(pl.multiple_of(core * depth, depth), depth),
                        pl.ds((r * 3 + w) * lanes, lanes),
                    ],
                    local.at[1 + r * 3 + w],
                )
            )
    for copy in loads:
        copy.start()
    id_rows = ids_ref.shape[0]
    ids_out[me] = jnp.concatenate(
        [ids_ref[...], jnp.zeros((SUBLANES - id_rows, LANES), ids_ref.dtype)], axis=0
    )
    loads[0].wait()
    groups = vocab // LANES
    lines = []
    for g in range(groups):
        block = own[g * LANES : (g + 1) * LANES, :].astype(jnp.float32)
        total = jnp.sum(block * block, axis=1, keepdims=True)
        lines.append(jnp.broadcast_to(total, (LANES, LANES)).T[:1, :])
    lines.append(jnp.zeros((SUBLANES - groups, LANES), jnp.float32))
    sums[at] = jnp.concatenate(lines, axis=0)

    @pl.when(source)
    def _():
        wide = gain_ref[...].astype(jnp.float32)
        gains[...] = jnp.concatenate(
            [wide[:, r * LANES : (r + 1) * LANES] for r in range(width // LANES)], axis=0
        )

    greet(ctx_peers, dp_peers)

    def gain_copy(d):
        return remote(gains, gains, gain_send.at[d], gain_recv.at[0], dp=dp_peers[d])

    @pl.when(source)
    def _():
        for d in range(n_dp - 1):
            gain_copy(d).start()

    sends = []
    for d, peer in enumerate(dp_peers):
        sends.append(remote(sums.at[at], sums.at[at], sum_send.at[d], sum_recv.at[at], dp=peer))
        sends[-1].start()

    def half(k, which):
        return pl.ds(pl.multiple_of(k * hop_rows + which * half_rows, half_rows), half_rows)

    def z_copy(src, k, way, peer):
        piece = half(k, core)
        return remote(src.at[piece], tab.at[piece], z_send.at[way, k], z_recv.at[k], dp=peer)

    def core_copy(k):
        piece = half(k, core)
        return remote(tab.at[piece], tab.at[piece], core_send.at[k], core_recv.at[k], ctx=partner)

    def core_arrival(k):
        piece = half(k, 1 - core)
        return remote(tab.at[piece], tab.at[piece], core_send.at[k], core_recv.at[k], ctx=partner)

    can_up, can_down = at < n_dp - 1, at > 0
    for k in range(hops):

        @pl.when(source & can_up)
        def _():
            z_copy(table_ref, k, 0, at + 1).start()

        @pl.when(source & can_down)
        def _():
            z_copy(table_ref, k, 1, at - 1).start()

    swaps = []
    for r, peer in enumerate(relatives):
        for w, weight in enumerate((wq_ref, wk_ref, wv_ref)):
            column = pl.multiple_of(flip(peer, 1) * lanes, lanes)
            swaps.append(
                remote(
                    weight.at[:, pl.ds(column, lanes)],
                    weights.at[
                        pl.ds(pl.multiple_of(core * depth, depth), depth),
                        pl.ds((r * 3 + w) * lanes, lanes),
                    ],
                    w_send.at[r * 3 + w],
                    w_recv.at[r * 3 + w],
                    ctx=partner,
                )
            )
    for copy in swaps:
        copy.start()
    @pl.when(source)
    def _():
        tab[...] = own[...]

    for d, peer in enumerate(ctx_peers):
        sends.append(remote(ids_out.at[me], ids_out.at[me], id_send.at[d], id_recv.at[me], ctx=peer))
        sends[-1].start()

    def arrive(h):
        @pl.when(above)
        def _():
            z_copy(tab, h, 0, at).wait_recv()

            @pl.when(can_up)
            def _():
                z_copy(tab, h, 0, at + 1).start()

        @pl.when(below)
        def _():
            z_copy(tab, h, 1, at).wait_recv()

            @pl.when(can_down)
            def _():
                z_copy(tab, h, 1, at - 1).start()

        @pl.when(jnp.logical_not(source))
        def _():
            core_copy(h).start()

    def settle():
        for peer in dp_peers:
            remote(sums.at[peer], sums.at[peer], sum_send.at[0], sum_recv.at[peer], dp=peer).wait_recv()
        total = sums[0]
        for b in range(1, n_dp):
            total = total + sums[b]
        scale = lax.rsqrt(total / (n_dp * width) + 1e-06)
        for g in range(groups):
            scales[g * LANES : (g + 1) * LANES, :] = jnp.broadcast_to(
                scale[g : g + 1, :], (LANES, LANES)
            ).T

        @pl.when(jnp.logical_not(source))
        def _():
            gain_copy(0).wait_recv()

        for copy in loads[1:]:
            copy.wait()
        for copy in swaps:
            copy.wait_recv()

    def rs_copy(r, k):
        piece = pl.ds(k * part_rows, part_rows)
        return remote(
            part.at[r - 1, piece],
            land.at[r - 1, piece],
            rs_send.at[r - 1, k],
            rs_recv.at[r - 1, k],
            ctx=relatives[r],
        )

    span = 3 * lanes
    for k in range(chunks):
        for h in range(k * hops // chunks, (k + 1) * hops // chunks):
            arrive(h)
        for h in range(k * hops // chunks, (k + 1) * hops // chunks):

            @pl.when(jnp.logical_not(source))
            def _():
                core_arrival(h).wait_recv()

        if k == 0:
            settle()
            gain = jnp.concatenate(
                [gains[r : r + 1, :] for r in range(width // LANES)], axis=1
            )
        piece = slice(k * part_rows, (k + 1) * part_rows)
        by_row = jnp.concatenate([scales[piece, :]] * (width // LANES), axis=1)
        normed = (tab[piece, :].astype(jnp.float32) * by_row * gain).astype(jnp.bfloat16)
        for r in range(1, chips):
            part[r - 1, piece, :] = jnp.dot(
                normed,
                weights[:, r * span : (r + 1) * span],
                preferred_element_type=jnp.float32,
            ).astype(jnp.bfloat16)
            rs_copy(r, k).start()
        mine[piece, :] = jnp.dot(normed, weights[:, :span], preferred_element_type=jnp.float32)

    for k in range(chunks):
        piece = slice(k * part_rows, (k + 1) * part_rows)
        total = mine[piece, :]
        for r in range(1, chips):
            rs_copy(r, k).wait_recv()
            total = total + land[r - 1, piece, :].astype(jnp.float32)
        rows_out[piece, :] = total.astype(jnp.bfloat16)

    for peer in ctx_peers:
        remote(ids_out.at[peer], ids_out.at[peer], id_send.at[0], id_recv.at[peer], ctx=peer).wait_recv()
    for copy in sends + swaps:
        copy.wait_send()

    @pl.when(source)
    def _():
        for d in range(n_dp - 1):
            gain_copy(d).wait_send()

    for k in range(hops):

        @pl.when((source | above) & can_up)
        def _():
            z_copy(tab, k, 0, at).wait_send()

        @pl.when((source | below) & can_down)
        def _():
            z_copy(tab, k, 1, at).wait_send()

        @pl.when(jnp.logical_not(source))
        def _():
            core_copy(k).wait_send()

    for k in range(chunks):
        for r in range(1, chips):
            rs_copy(r, k).wait_send()


def project(n_ctx, n_dp, ids, gain, table, w_query, w_key, w_value):
    vocab, width = table.shape
    depth, lanes = w_query.shape[0], w_query.shape[1] // n_ctx
    chips = n_ctx // 2
    chunks = vocab // LANES
    hops = 2 * chunks
    anywhere = pl.BlockSpec(memory_space=pl.ANY)
    whole = pl.BlockSpec(memory_space=pltpu.VMEM)
    dma = pltpu.SemaphoreType.DMA
    return pl.pallas_call(
        lambda *refs: project_kernel(n_ctx, n_dp, *refs),
        name="project",
        out_shape=(
            jax.ShapeDtypeStruct((n_ctx, SUBLANES, LANES), ids.dtype),
            jax.ShapeDtypeStruct((vocab, 3 * lanes), w_query.dtype),
        ),
        in_specs=[whole] * 2 + [anywhere] * 4,
        out_specs=[whole] * 2,
        scratch_shapes=[
            pltpu.VMEM((vocab, width), table.dtype),
            pltpu.VMEM((vocab, width), table.dtype),
            pltpu.VMEM((2 * depth, chips * 3 * lanes), w_query.dtype),
            pltpu.VMEM((chips - 1, vocab, 3 * lanes), w_query.dtype),
            pltpu.VMEM((chips - 1, vocab, 3 * lanes), w_query.dtype),
            pltpu.VMEM((vocab, 3 * lanes), jnp.float32),
            pltpu.VMEM((n_dp, SUBLANES, LANES), jnp.float32),
            pltpu.VMEM((vocab, LANES), jnp.float32),
            pltpu.VMEM((width // LANES, LANES), jnp.float32),
            dma((2, hops)),
            dma((hops,)),
            dma((hops,)),
            dma((hops,)),
            dma((chips * 3,)),
            dma((chips * 3,)),
            dma((n_ctx - 1,)),
            dma((n_ctx,)),
            dma((n_dp - 1,)),
            dma((n_dp,)),
            dma((n_dp - 1,)),
            dma((1,)),
            dma((chips - 1, chunks)),
            dma((chips - 1, chunks)),
            dma((1 + chips * 3,)),
        ],
        compiler_params=pltpu.CompilerParams(
            collective_id=0, has_side_effects=True, vmem_limit_bytes=53 << 20
        ),
    )(ids, gain, table, w_query, w_key, w_value)


def mix_kernel(
    me_ref,
    ids_ref,
    rows_ref,
    filt_ref,
    rate_ref,
    residue_ref,
    skip_ref,
    out_ref,
    proj,
    gated,
    query,
):
    vocab = rows_ref.shape[0]
    taps = filt_ref.shape[0]
    modes = rate_ref.shape[0]
    segments, steps, lanes = out_ref.shape
    lead = proj.shape[1] - segments * steps
    mine = pl.ds(pl.multiple_of(me_ref[0] * lanes, lanes), lanes)
    rows = rows_ref[...]
    pieces = steps // lanes
    per_segment = ids_ref.shape[1]
    names = lax.broadcasted_iota(jnp.int32, (lanes, vocab), 1)
    for s in range(segments):
        by_lane = ids_ref[s].astype(jnp.float32)
        square = jnp.concatenate(
            [by_lane, jnp.zeros((lanes - per_segment, lanes), jnp.float32)], axis=0
        )
        columns = square.T.astype(jnp.int32)
        one_hot = jnp.concatenate(
            [
                (columns[:, p : p + 1] == names).astype(jnp.float32).astype(jnp.bfloat16)
                for p in range(pieces)
            ],
            axis=0,
        )
        picked = jnp.dot(one_hot, rows, preferred_element_type=jnp.float32)
        for w in range(3):
            proj[w, pl.ds(lead + s, steps, stride=segments), :] = picked[:, w * lanes : (w + 1) * lanes]
    place_of = lax.broadcasted_iota(jnp.int32, (segments, lanes), 0)

    def later(value, by):
        return jnp.where(place_of >= by, pltpu.roll(value, by, 0), 0.0)

    end = proj.shape[1]
    for tap in range(1, taps):
        for w in range(3):
            tail = proj[w, end - tap * segments : end - (tap - 1) * segments, :]
            proj[w, lead - tap * segments : lead - (tap - 1) * segments, :] = later(tail, 1)
    size = lanes

    def convolve(n, carry):
        start = n * size + lead
        conv = [jnp.zeros((size, lanes), jnp.float32) for _ in range(3)]
        for tap in range(taps):
            here = pl.ds(pl.multiple_of(start - tap * segments, segments), size)
            for w in range(3):
                conv[w] = conv[w] + filt_ref[tap, w : w + 1, mine] * proj[w, here, :]
        there = pl.ds(pl.multiple_of(n * size, size), size)
        query[there, :] = conv[0]
        gated[there, :] = conv[1] * conv[2]
        return carry

    lax.fori_loop(0, segments * steps // size, convolve, 0)

    def spread_rows(row):
        return jnp.broadcast_to(row, (segments, lanes))

    rate, residue = rate_ref[:, mine], residue_ref[:, mine]
    decay = [spread_rows(jnp.exp(-rate[m : m + 1, :])) for m in range(modes)]
    unroll = 4

    def ends(n, state):
        for u in range(unroll):
            row = gated[pl.ds(pl.multiple_of((n * unroll + u) * segments, segments), segments), :]
            state = tuple(d * s + row for d, s in zip(decay, state))
        return state

    zero = jnp.zeros((segments, lanes), jnp.float32)
    state = lax.fori_loop(0, steps // unroll, ends, (zero,) * modes)
    entering = []
    for m in range(modes):
        value = later(state[m], 1)
        by = 1
        while by < segments:
            jump = jnp.exp(-rate[m : m + 1, :] * float(steps * by))
            value = value + jump * later(value, by)
            by *= 2
        entering.append(value)
    strength = [
        spread_rows(residue[m : m + 1, :] * jnp.sqrt(2.0 * rate[m : m + 1, :])) for m in range(modes)
    ]
    skip = spread_rows(skip_ref[:, mine])

    def advance(n, state):
        for u in range(unroll):
            here = pl.ds(pl.multiple_of((n * unroll + u) * segments, segments), segments)
            row = gated[here, :]
            sums = [skip * row, None]
            new = []
            for m in range(modes):
                now = decay[m] * state[m] + row
                new.append(now)
                term = strength[m] * now
                sums[m % 2] = term if sums[m % 2] is None else sums[m % 2] + term
            state = tuple(new)
            query[here, :] = query[here, :] * (sums[0] + sums[1])
        return state

    lax.fori_loop(0, steps // unroll, advance, tuple(entering))
    for s in range(segments):
        out_ref[s] = query[pl.ds(s, steps, stride=segments), :].astype(jnp.bfloat16)


def mix(me, ids, rows, filt, rate, residue, skip, segments, steps):
    whole = pl.BlockSpec(memory_space=pltpu.VMEM)
    lanes = rows.shape[1] // 3
    lead = segments * (filt.shape[0] - 1)
    return pl.pallas_call(
        mix_kernel,
        name="mix",
        out_shape=jax.ShapeDtypeStruct((segments, steps, lanes), jnp.bfloat16),
        in_specs=[pl.BlockSpec(memory_space=pltpu.SMEM)] + [whole] * 6,
        out_specs=whole,
        scratch_shapes=[
            pltpu.VMEM((3, lead + segments * steps, lanes), jnp.float32),
            pltpu.VMEM((segments * steps, lanes), jnp.float32),
            pltpu.VMEM((segments * steps, lanes), jnp.float32),
        ],
        compiler_params=pltpu.CompilerParams(vmem_limit_bytes=VMEM_BYTES),
    )(me, ids, rows, filt, rate, residue, skip)


def collect_kernel(
    n_ctx,
    n_dp,
    mixed_ref,
    weight_ref,
    mixed_out,
    weight_out,
    own_mixed,
    own_weight,
    a_send,
    slot_recv,
    z_send,
    w_send,
    w_recv,
    core_send,
    core_recv,
    local,
):
    me, at = lax.axis_index("ctx"), lax.axis_index("dp")
    depth, lanes = weight_ref.shape[0], mixed_ref.shape[2]
    bits = [1 << b for b in range(n_ctx.bit_length() - 1)]
    ctx_peers = [lax.rem(me + d, n_ctx) for d in range(1, n_ctx)]
    near = [(at - 1, at > 0), (at + 1, at < n_dp - 1)]
    barrier = pltpu.get_barrier_semaphore()
    dp_peers = [lax.rem(at + d, n_dp) for d in range(1, n_dp)]
    greet(ctx_peers, dp_peers)
    partner, side, up = flip(me, 1), flip(me, 2), flip(me, 4)
    across = flip(side, 4)
    half = depth // 2

    def slot(source, k):
        start = (source * n_ctx + k) * lanes
        return mixed_out.at[:, pl.ds(pl.multiple_of(start, lanes), lanes)]

    def turn(d, peer):
        return remote(mixed_ref.at[peer], slot(at, me), a_send.at[d - 1], slot_recv.at[at, me], ctx=peer)

    def block(owner, first=0, count=None):
        count = depth if count is None else count
        start = pl.multiple_of(owner * depth + first, half)
        return weight_out.at[pl.ds(start, count)]

    for d, peer in enumerate(ctx_peers):
        turn(d + 1, peer).start()
    into = [
        pltpu.make_async_copy(mixed_ref.at[me], own_mixed, local.at[0]),
        pltpu.make_async_copy(weight_ref, own_weight, local.at[1]),
    ]
    for copy in into:
        copy.start()

    def z_copy(source, d, way, hop, peer):
        k = lax.rem(me + d, n_ctx)
        src = mixed_ref.at[me] if hop == 0 and d == 0 else slot(source, k)
        return remote(src, slot(source, k), z_send.at[way, hop, d], slot_recv.at[source, k], dp=peer)

    def recv(source, d):
        k = lax.rem(me + d, n_ctx)
        z_copy_like = remote(slot(source, k), slot(source, k), z_send.at[0, 0, d], slot_recv.at[source, k], ctx=partner)
        z_copy_like.wait_recv()

    def first_hop(d):
        @pl.when(at < n_dp - 1)
        def _():
            z_copy(at, d, 0, 0, at + 1).start()

        @pl.when(at > 0)
        def _():
            z_copy(at, d, 1, 0, at - 1).start()

    first_hop(0)
    own = [
        remote(weight_ref, block(me), w_send.at[0], w_recv.at[0], ctx=side),
        remote(weight_ref, block(me), w_send.at[1], w_recv.at[1], ctx=up),
        remote(weight_ref, block(me), w_send.at[2], w_recv.at[2], ctx=partner),
    ]
    own[2].start()
    for copy in into:
        copy.wait()
    out = [
        pltpu.make_async_copy(own_mixed, slot(at, me), local.at[0]),
        pltpu.make_async_copy(own_weight, block(me), local.at[1]),
    ]
    for copy in out:
        copy.start()
    for d in range(1, n_ctx):
        recv(at, d)
        first_hop(d)
    own[0].start()
    own[1].start()

    for hop in range(1, n_dp):
        for d in range(n_ctx):

            @pl.when(at - hop >= 0)
            def _():
                recv(at - hop, d)

                if hop < n_dp - 1:

                    @pl.when(at < n_dp - 1)
                    def _():
                        z_copy(at - hop, d, 0, hop, at + 1).start()

            @pl.when(at + hop <= n_dp - 1)
            def _():
                recv(at + hop, d)

                if hop < n_dp - 1:

                    @pl.when(at > 0)
                    def _():
                        z_copy(at + hop, d, 1, hop, at - 1).start()

        if hop == 1:
            own[0].wait_recv()
            own[1].wait_recv()
            passed = [
                remote(block(side, 0, half), block(side, 0, half), w_send.at[3], w_recv.at[3], ctx=up),
                remote(block(up, half, half), block(up, half, half), w_send.at[4], w_recv.at[4], ctx=side),
                remote(block(side), block(side), core_send.at[0], core_recv.at[0], ctx=partner),
                remote(block(up), block(up), core_send.at[1], core_recv.at[1], ctx=partner),
            ]
            for copy in passed:
                copy.start()
    passed[0].wait_recv()
    passed[1].wait_recv()
    last = [
        remote(block(across, 0, half), block(across, 0, half), core_send.at[2], core_recv.at[2], ctx=partner),
        remote(block(across, half, half), block(across, half, half), core_send.at[3], core_recv.at[3], ctx=partner),
    ]
    for copy in last:
        copy.start()
    own[2].wait_recv()
    passed[2].wait_recv()
    passed[3].wait_recv()
    for copy in last:
        copy.wait_recv()
    for copy in own + passed + last:
        copy.wait_send()
    for d, peer in enumerate(ctx_peers):
        turn(d + 1, peer).wait_send()
    for hop in range(n_dp - 1):
        for d in range(n_ctx):

            @pl.when((at - hop >= 0) & (at < n_dp - 1))
            def _():
                z_copy(at - hop, d, 0, hop, at + 1).wait_send()

            @pl.when((at + hop <= n_dp - 1) & (at > 0))
            def _():
                z_copy(at + hop, d, 1, hop, at - 1).wait_send()

    for copy in out:
        copy.wait()


def collect(n_ctx, n_dp, mixed, weight):
    depth, columns = weight.shape
    steps, lanes = mixed.shape[1:]
    anywhere = pl.BlockSpec(memory_space=pl.ANY)
    dma = pltpu.SemaphoreType.DMA
    return pl.pallas_call(
        lambda *refs: collect_kernel(n_ctx, n_dp, *refs),
        name="collect",
        out_shape=(
            jax.ShapeDtypeStruct((steps, n_dp * n_ctx * lanes), mixed.dtype),
            jax.ShapeDtypeStruct((n_ctx * depth, columns), weight.dtype),
        ),
        in_specs=[anywhere] * 2,
        out_specs=[anywhere] * 2,
        scratch_shapes=[
            pltpu.VMEM((steps, lanes), mixed.dtype),
            pltpu.VMEM((depth, columns), weight.dtype),
            dma((n_ctx - 1,)),
            dma((n_dp, n_ctx)),
            dma((2, n_dp - 1, n_ctx)),
            dma((5,)),
            dma((5,)),
            dma((4,)),
            dma((4,)),
            dma((2,)),
        ],
        compiler_params=pltpu.CompilerParams(
            collective_id=1, has_side_effects=True, vmem_limit_bytes=8 << 20
        ),
    )(mixed, weight)


def by_channel(
    n_ctx,
    n_dp,
    ids,
    embed_table,
    norm_gain,
    w_query,
    w_key,
    w_value,
    short_filter,
    pole_rate,
    residue,
    skip_gain,
    w_out,
):
    vocab = embed_table.shape[0]
    tok_rows = ids.shape[0]
    all_ids, rows = project(
        n_ctx,
        n_dp,
        ids.reshape(-1, LANES),
        norm_gain[None, :],
        embed_table,
        w_query,
        w_key,
        w_value,
    )
    mixed = mix(
        lax.axis_index("ctx").astype(jnp.int32).reshape(1),
        all_ids,
        rows,
        short_filter,
        pole_rate.T,
        residue.T,
        skip_gain[None, :],
        n_ctx,
        tok_rows,
    )
    all_mixed, all_rows = collect(n_ctx, n_dp, mixed, w_out)
    one_hot = (ids[:, None] == jnp.arange(vocab, dtype=jnp.int32)[None, :]).astype(jnp.bfloat16)
    embedded = jnp.dot(one_hot, embed_table, preferred_element_type=jnp.float32)
    output = jnp.dot(all_mixed, all_rows, preferred_element_type=jnp.float32)
    return (embedded + output).astype(jnp.bfloat16)


def solution(mesh):
    placed = (
        P("ctx"),
        P(None, "dp"),
        P("dp"),
        P("ctx", "dp"),
        P("ctx", "dp"),
        P("ctx", "dp"),
        P(None, None, "dp"),
        P("dp", None),
        P("dp", None),
        P("dp"),
        P("ctx", "dp"),
    )
    n_ctx, n_dp = mesh.shape["ctx"], mesh.shape["dp"]

    def body(*args):
        ids, table, w_query = args[0], args[1], args[3]
        fits = (
            n_ctx == SUBLANES
            and n_ctx == 2 * n_dp
            and w_query.shape[1] == n_ctx * LANES
            and table.shape[1] == 2 * w_query.shape[0]
            and table.shape[0] % LANES == 0
            and table.shape[0] < SUBLANES * LANES
            and ids.shape[0] % LANES == 0
            and ids.shape[0] < SUBLANES * LANES
        )
        if fits:
            return by_channel(n_ctx, n_dp, *args)
        return shards(*args)

    return jax.shard_map(
        body, mesh=mesh, in_specs=placed, out_specs=P("ctx", "dp"), check_vma=False
    )
```

```python
import math

import jax
import jax.numpy as jnp
from jax import lax

from jax.experimental import pallas as pl
from jax.experimental.pallas import tpu as pltpu
from jax.sharding import PartitionSpec as P

MESH = pl.DeviceIdType.MESH
LANES = 128
SUBLANES = 8
VMEM_BYTES = 56 << 20


def shifted(value, axis, steps):
    count = lax.axis_size(axis)
    initial, last = (max(0, -steps), min(count, count - steps))
    return lax.ppermute(value, axis, [(source, source + steps) for source in range(initial, last)])


def entering_2(value, axis, combine, identity):
    peers, index = (lax.axis_size(axis), lax.axis_index(axis))
    everything = jax.tree.map(lambda part: lax.all_gather(part, axis), value)
    start = jax.tree.map(
        lambda part, zero: jnp.broadcast_to(jnp.asarray(zero, part.dtype), part.shape),
        value,
        identity,
    )

    def turn(k, before):
        reached = k < index
        new = combine(before, jax.tree.map(lambda part: part[k], everything))
        return jax.tree.map(lambda a, b: jnp.where(reached, a, b), new, before)

    return lax.fori_loop(0, peers, turn, start)


def shards(
    ids,
    embed_table,
    norm_gain,
    w_query,
    w_key,
    w_value,
    short_filter,
    pole_rate,
    residue,
    skip_gain,
    w_out,
):
    highest = lax.Precision.HIGHEST
    vocab = embed_table.shape[0]
    channels = w_query.shape[1]
    one_hot = (ids[:, None] == jnp.arange(vocab, dtype=jnp.int32)[None, :]).astype(jnp.bfloat16)
    embedded = jnp.dot(one_hot, embed_table, preferred_element_type=jnp.float32).astype(
        jnp.bfloat16
    )
    full_rows, full_gain = (
        lax.all_gather(embedded, "dp", axis=1, tiled=True),
        lax.all_gather(norm_gain, "dp", axis=0, tiled=True),
    )
    floated = full_rows.astype(jnp.float32)
    scale = lax.rsqrt(jnp.mean(floated * floated, axis=1, keepdims=True) + 1e-06)
    normed = (floated * scale * full_gain.astype(jnp.float32)[None, :]).astype(jnp.bfloat16)
    tok_rows = normed.shape[0]

    def add_rows(piece):
        return jnp.dot(normed, piece, preferred_element_type=jnp.float32)

    query_proj = add_rows(lax.all_gather(w_query, "ctx", axis=0, tiled=True))
    key_proj = add_rows(lax.all_gather(w_key, "ctx", axis=0, tiled=True))
    value_proj = add_rows(lax.all_gather(w_value, "ctx", axis=0, tiled=True))
    projected = jnp.concatenate([query_proj, key_proj, value_proj], axis=1).astype(jnp.bfloat16)
    taps = short_filter.shape[0]
    previous = shifted(projected[tok_rows - (taps - 1) :], "ctx", 1)
    extended = jnp.concatenate([previous, projected], axis=0).astype(jnp.float32)
    filt_rows = short_filter.reshape(taps, 3 * channels)
    convolved = jnp.zeros((tok_rows, 3 * channels), jnp.float32)
    for tap in range(taps):
        convolved = (
            convolved
            + filt_rows[tap][None, :] * extended[taps - 1 - tap : taps - 1 - tap + tok_rows]
        )
    query_conv = convolved[:, :channels]
    gated = convolved[:, channels : 2 * channels] * convolved[:, 2 * channels :]
    sub_len = math.gcd(tok_rows, 64)
    blocks = tok_rows // sub_len
    lag_index = jnp.arange(sub_len, dtype=jnp.int32)
    lags = lag_index.astype(jnp.float32)
    strength = residue * jnp.sqrt(2.0 * pole_rate)
    kernel = jnp.einsum(
        "lck,ck->lc", jnp.exp(-pole_rate[None] * lags[:, None, None]), strength, precision=highest
    )
    offsets = lag_index[:, None] - lag_index[None, :]
    toeplitz = jnp.where((offsets >= 0)[:, :, None], kernel[jnp.maximum(offsets, 0)], 0.0)
    pieces = gated.reshape(blocks, sub_len, channels)
    inside = jnp.einsum("tsc,bsc->btc", toeplitz, pieces, precision=highest)
    tail_decay = jnp.exp(-pole_rate[None] * (sub_len - 1.0 - lags)[:, None, None])
    block_ends = jnp.einsum("sck,bsc->bck", tail_decay, pieces, precision=highest)
    step_decay = jnp.exp(-pole_rate * float(sub_len))

    def advance(state, block_end):
        return (step_decay * state + block_end, state)

    device_end, entering = lax.scan(advance, jnp.zeros_like(step_decay), block_ends)
    device_decay = jnp.exp(-pole_rate * float(tok_rows))

    def combine(earlier, later):
        return (earlier[0] * later[0], later[0] * earlier[1] + later[1])

    decay_total, incoming = entering_2(
        (device_decay, device_end),
        "ctx",
        combine,
        (jnp.ones_like(device_decay), jnp.zeros_like(device_end)),
    )
    block_pos = jnp.arange(blocks, dtype=jnp.float32) * float(sub_len)
    states_in = entering + jnp.exp(-pole_rate[None] * block_pos[:, None, None]) * incoming[None]
    lead = jnp.exp(-pole_rate[None] * (lags + 1.0)[:, None, None]) * strength[None]
    carried = jnp.einsum("tck,bck->btc", lead, states_in, precision=highest)
    long_conv = (inside + carried).reshape(tok_rows, channels) + skip_gain[None, :] * gated
    mixed = (query_conv * long_conv).astype(jnp.bfloat16)
    all_mixed = lax.all_gather(mixed, "dp", axis=1, tiled=True)
    output = jnp.dot(
        all_mixed,
        lax.all_gather(w_out, "ctx", axis=0, tiled=True),
        preferred_element_type=jnp.float32,
    )
    return (embedded.astype(jnp.float32) + output).astype(jnp.bfloat16)


def remote(src, dst, send, recv, **where):
    return pltpu.make_async_remote_copy(
        src_ref=src,
        dst_ref=dst,
        send_sem=send,
        recv_sem=recv,
        device_id=where,
        device_id_type=MESH,
    )


def greet(ctx_peers, dp_peers):
    barrier = pltpu.get_barrier_semaphore()
    for peer in ctx_peers:
        pl.semaphore_signal(barrier, inc=1, device_id={"ctx": peer}, device_id_type=MESH)
    for peer in dp_peers:
        pl.semaphore_signal(barrier, inc=1, device_id={"dp": peer}, device_id_type=MESH)
    pl.semaphore_wait(barrier, len(ctx_peers) + len(dp_peers))


def flip(index, bit):
    return index + bit - 2 * bit * (lax.rem(index // bit, 2))


def block_kernel(
    n_ctx,
    n_dp,
    ids_ref,
    gain_ref,
    filt_ref,
    rate_ref,
    residue_ref,
    skip_ref,
    table_ref,
    wq_ref,
    wk_ref,
    wv_ref,
    wo_ref,
    out_ref,
    all_ids,
    tab,
    own,
    weights,
    first_out,
    first_in,
    hold,
    second_out,
    second_in,
    mine,
    sums,
    scales,
    gains,
    rows,
    params,
    hot,
    proj,
    gated,
    query,
    mixed,
    gathered,
    w_all,
    acc,
    z_send,
    z_recv,
    core_send,
    core_recv,
    w_send,
    w_recv,
    id_send,
    id_recv,
    sum_send,
    sum_recv,
    gain_send,
    gain_recv,
    first_send,
    first_recv,
    second_send,
    second_recv,
    dup_send,
    dup_recv,
    a_send,
    a_recv,
    y_send,
    y_recv,
    o_send,
    o_recv,
    q_send,
    q_recv,
    c_send,
    c_recv,
    local,
):
    me, at = lax.axis_index("ctx"), lax.axis_index("dp")
    vocab, width = table_ref.shape
    depth = wq_ref.shape[0]
    lanes = wq_ref.shape[1] // n_ctx
    span = 3 * lanes
    chunks = first_send.shape[1]
    part_rows = vocab // chunks
    side_rows = part_rows // 2
    hops = z_send.shape[1]
    hop_rows = vocab // hops
    half_rows = hop_rows // 2
    segments, steps = n_ctx, out_ref.shape[0]
    turns = a_send.shape[1]
    turn_rows = steps // turns
    taps = filt_ref.shape[0]
    modes = rate_ref.shape[0]
    pieces = o_send.shape[1]
    piece_rows = depth // pieces
    chip, core = me // 2, lax.rem(me, 2)
    partner, side, up = flip(me, 1), flip(me, 2), flip(me, 4)
    across = flip(side, 4)
    relatives = [me, side, up, across]
    ctx_peers = [lax.rem(me + d, n_ctx) for d in range(1, n_ctx)]
    dp_peers = [lax.rem(at + d, n_dp) for d in range(1, n_dp)]
    source, above, below = at == chip, at > chip, at < chip
    low = at < n_dp // 2
    outer = (at == 0) | (at == n_dp - 1)
    inner = jnp.logical_not(outer)
    plane_outer = jnp.where(low, 0, n_dp - 1)
    plane_inner = jnp.where(low, 1, n_dp - 2)
    far_inner = jnp.where(low, n_dp - 2, 1)
    far_outer = jnp.where(low, n_dp - 1, 0)
    channels = pl.ds(pl.multiple_of(me * lanes, lanes), lanes)

    loads = [
        pltpu.make_async_copy(table_ref, own, local.at[0]),
        pltpu.make_async_copy(
            wo_ref, w_all.at[pl.ds(pl.multiple_of(me * depth, depth), depth)], local.at[1]
        ),
    ]
    for r, peer in enumerate(relatives):
        for w, weight in enumerate((wq_ref, wk_ref, wv_ref)):
            column = pl.multiple_of(peer * lanes, lanes)
            loads.append(
                pltpu.make_async_copy(
                    weight.at[:, pl.ds(column, lanes)],
                    weights.at[
                        pl.ds(pl.multiple_of(core * depth, depth), depth),
                        pl.ds((r * 3 + w) * lanes, lanes),
                    ],
                    local.at[2 + r * 3 + w],
                )
            )
    for copy in loads:
        copy.start()
    all_ids[me] = jnp.concatenate(
        [ids_ref[...], jnp.zeros((SUBLANES - ids_ref.shape[0], LANES), ids_ref.dtype)], axis=0
    )
    params[0, :modes, :] = rate_ref[:, channels]
    params[0, modes : 2 * modes, :] = residue_ref[:, channels]
    for tap in range(taps):
        params[0, 2 * modes + 3 * tap : 2 * modes + 3 * tap + 3, :] = filt_ref[tap, :, channels]
    skip_row = 2 * modes + 3 * taps
    params[0, skip_row : skip_row + 1, :] = skip_ref[:, channels]

    loads[0].wait()
    groups = vocab // LANES
    lines = []
    for g in range(groups):
        block = own[g * LANES : (g + 1) * LANES, :].astype(jnp.float32)
        total = jnp.sum(block * block, axis=1, keepdims=True)
        lines.append(jnp.broadcast_to(total, (LANES, LANES)).T[:1, :])
    lines.append(jnp.zeros((SUBLANES - groups, LANES), jnp.float32))
    sums[at] = jnp.concatenate(lines, axis=0)

    @pl.when(source)
    def _():
        wide = gain_ref[...].astype(jnp.float32)
        gains[...] = jnp.concatenate(
            [wide[:, r * LANES : (r + 1) * LANES] for r in range(width // LANES)], axis=0
        )

    greet(ctx_peers, dp_peers)

    def gain_copy(d):
        return remote(gains, gains, gain_send.at[d], gain_recv.at[0], dp=dp_peers[d])

    @pl.when(source)
    def _():
        for d in range(n_dp - 1):
            gain_copy(d).start()

    sends = []

    def send(copy):
        copy.start()
        sends.append(copy)

    for d, peer in enumerate(dp_peers):
        send(remote(sums.at[at], sums.at[at], sum_send.at[d], sum_recv.at[at], dp=peer))

    def half(k, which):
        return pl.ds(pl.multiple_of(k * hop_rows + which * half_rows, half_rows), half_rows)

    def z_copy(src, k, way, peer):
        piece = half(k, core)
        return remote(src.at[piece], tab.at[piece], z_send.at[way, k], z_recv.at[k], dp=peer)

    def core_copy(k):
        piece = half(k, core)
        return remote(tab.at[piece], tab.at[piece], core_send.at[k], core_recv.at[k], ctx=partner)

    def core_arrival(k):
        piece = half(k, 1 - core)
        return remote(tab.at[piece], tab.at[piece], core_send.at[k], core_recv.at[k], ctx=partner)

    can_up, can_down = at < n_dp - 1, at > 0
    for k in range(hops):

        @pl.when(source & can_up)
        def _():
            z_copy(table_ref, k, 0, at + 1).start()

        @pl.when(source & can_down)
        def _():
            z_copy(table_ref, k, 1, at - 1).start()

    swaps = []
    for r, peer in enumerate(relatives):
        for w, weight in enumerate((wq_ref, wk_ref, wv_ref)):
            column = pl.multiple_of(flip(peer, 1) * lanes, lanes)
            swaps.append(
                remote(
                    weight.at[:, pl.ds(column, lanes)],
                    weights.at[
                        pl.ds(pl.multiple_of(core * depth, depth), depth),
                        pl.ds((r * 3 + w) * lanes, lanes),
                    ],
                    w_send.at[r * 3 + w],
                    w_recv.at[r * 3 + w],
                    ctx=partner,
                )
            )
            send(swaps[-1])

    @pl.when(source)
    def _():
        tab[...] = own[...]

    for d, peer in enumerate(ctx_peers):
        send(remote(all_ids.at[me], all_ids.at[me], id_send.at[d], id_recv.at[me], ctx=peer))

    def piece_of(owner, p):
        start = pl.multiple_of(owner * depth + p * piece_rows, piece_rows)
        return w_all.at[pl.ds(start, piece_rows)]

    def own_piece(way, p):
        return remote(
            wo_ref.at[pl.ds(p * piece_rows, piece_rows)],
            piece_of(me, p),
            o_send.at[way, p],
            o_recv.at[way, p],
            ctx=(side, up)[way],
        )

    def pass_piece(p):
        owner, peer = ((side, up), (up, side))[p % 2]
        return remote(piece_of(owner, p), piece_of(owner, p), q_send.at[p], q_recv.at[p], ctx=peer)

    def core_piece(which, p):
        owner = (side, up, across)[which]
        return remote(
            piece_of(owner, p), piece_of(owner, p), c_send.at[which, p], c_recv.at[which, p], ctx=partner
        )

    whole_mine = pl.ds(pl.multiple_of(me * depth, depth), depth)
    to_partner = remote(wo_ref, w_all.at[whole_mine], c_send.at[3, 0], c_recv.at[3, 0], ctx=partner)

    def offer(p):
        for way in range(2):
            send(own_piece(way, p))

    offer(0)
    send(to_partner)

    def arrive(h):
        @pl.when(above)
        def _():
            z_copy(tab, h, 0, at).wait_recv()

            @pl.when(can_up)
            def _():
                z_copy(tab, h, 0, at + 1).start()

        @pl.when(below)
        def _():
            z_copy(tab, h, 1, at).wait_recv()

            @pl.when(can_down)
            def _():
                z_copy(tab, h, 1, at - 1).start()

        @pl.when(jnp.logical_not(source))
        def _():
            core_copy(h).start()

    def settle():
        for peer in dp_peers:
            remote(sums.at[peer], sums.at[peer], sum_send.at[0], sum_recv.at[peer], dp=peer).wait_recv()
        total = sums[0]
        for b in range(1, n_dp):
            total = total + sums[b]
        scale = lax.rsqrt(total / (n_dp * width) + 1e-06)
        for g in range(groups):
            scales[g * LANES : (g + 1) * LANES, :] = jnp.broadcast_to(
                scale[g : g + 1, :], (LANES, LANES)
            ).T

        @pl.when(jnp.logical_not(source))
        def _():
            gain_copy(0).wait_recv()

        for copy in loads[2:]:
            copy.wait()
        for copy in swaps:
            copy.wait_recv()

    def sides(k, way):
        start = k * part_rows + way * side_rows
        return slice(start, start + side_rows)

    def first(k, way):
        piece = pl.ds(k * part_rows + way * side_rows, side_rows)
        return remote(
            first_out.at[piece],
            first_in.at[piece],
            first_send.at[way, k],
            first_recv.at[way, k],
            ctx=(side, up)[way],
        )

    def second(k, way):
        piece = pl.ds(k * part_rows + way * side_rows, side_rows)
        return remote(
            second_out.at[piece],
            second_in.at[piece],
            second_send.at[way, k],
            second_recv.at[way, k],
            ctx=(up, side)[way],
        )

    def relay(k):
        for way in range(2):
            first(k, way).wait_recv()
            piece = sides(k, way)
            second_out[piece, :] = (
                hold[piece, :] + first_in[piece, span:].astype(jnp.float32)
            ).astype(jnp.bfloat16)
            send(second(k, way))

    for k in range(chunks):
        for h in range(k * hops // chunks, (k + 1) * hops // chunks):
            arrive(h)
        for h in range(k * hops // chunks, (k + 1) * hops // chunks):

            @pl.when(jnp.logical_not(source))
            def _():
                core_arrival(h).wait_recv()

        if k == 0:
            settle()
            gain = jnp.concatenate([gains[r : r + 1, :] for r in range(width // LANES)], axis=1)
        piece = slice(k * part_rows, (k + 1) * part_rows)
        by_row = jnp.concatenate([scales[piece, :]] * (width // LANES), axis=1)
        normed = (tab[piece, :].astype(jnp.float32) * by_row * gain).astype(jnp.bfloat16)

        def product(r):
            return jnp.dot(
                normed, weights[:, r * span : (r + 1) * span], preferred_element_type=jnp.float32
            )

        ways = [sides(k, 0), sides(k, 1)]
        diagonal = product(3).astype(jnp.bfloat16)
        along_x, along_y = product(1), product(2)
        for way, (here, there) in enumerate(((along_x, along_y), (along_y, along_x))):
            cut = slice(way * side_rows, (way + 1) * side_rows)
            first_out[ways[way], :span] = here[cut, :].astype(jnp.bfloat16)
            first_out[ways[way], span:] = diagonal[cut, :]
            hold[ways[way], :] = there[cut, :]
            send(first(k, way))
        mine[piece, :] = product(0)
        if k > 0:
            relay(k - 1)
    relay(chunks - 1)

    for peer in ctx_peers:
        remote(all_ids.at[peer], all_ids.at[peer], id_send.at[0], id_recv.at[peer], ctx=peer).wait_recv()
    names = lax.broadcasted_iota(jnp.int32, (lanes, vocab), 1)
    for s in range(segments):
        columns = jnp.concatenate(
            [all_ids[s].astype(jnp.float32), jnp.zeros((lanes - SUBLANES, lanes), jnp.float32)], axis=0
        ).T.astype(jnp.int32)
        for p in range(steps // lanes):
            start = s * steps + p * lanes
            hot[start : start + lanes, :] = (
                (columns[:, p : p + 1] == names).astype(jnp.float32).astype(jnp.bfloat16)
            )

    def dup_copy(k):
        piece = pl.ds(k * part_rows, part_rows)
        return remote(
            rows.at[0, piece], rows.at[1, piece], dup_send.at[k], dup_recv.at[k], dp=plane_outer
        )

    dup_params = remote(
        params.at[0], params.at[1], dup_send.at[chunks], dup_recv.at[chunks], dp=plane_outer
    )
    for k in range(chunks):
        for way in range(2):
            second(k, way).wait_recv()
            piece = sides(k, way)
            rows[0, piece, :] = (
                mine[piece, :]
                + first_in[piece, :span].astype(jnp.float32)
                + second_in[piece, :].astype(jnp.float32)
            ).astype(jnp.bfloat16)

        @pl.when(inner)
        def _():
            dup_copy(k).start()
            if k == 0:
                dup_params.start()

    offer(1)

    lead = proj.shape[1] - segments * steps
    place_of = lax.broadcasted_iota(jnp.int32, (segments, lanes), 0)

    def later(value, by):
        return jnp.where(place_of >= by, pltpu.roll(value, by, 0), 0.0)

    def spread_rows(row):
        return jnp.broadcast_to(row, (segments, lanes))

    unroll = 4

    def turn_copy(m, plane, k, d, peer):
        piece = pl.ds(k * turn_rows, turn_rows)
        return remote(
            mixed.at[m, peer, piece],
            gathered.at[plane, piece, channels],
            a_send.at[m, k, d],
            a_recv.at[m, k, me],
            ctx=peer,
        )

    def turn_arrival(m, plane, k, peer):
        piece = pl.ds(k * turn_rows, turn_rows)
        theirs = gathered.at[plane, piece, pl.ds(pl.multiple_of(peer * lanes, lanes), lanes)]
        return remote(theirs, theirs, a_send.at[m, k, 0], a_recv.at[m, k, peer], ctx=peer)

    def mix(m, plane, arrived):
        for s in range(segments):
            picked = jnp.dot(
                hot[s * steps : (s + 1) * steps, :], rows[m], preferred_element_type=jnp.float32
            )
            for w in range(3):
                proj[w, pl.ds(lead + s, steps, stride=segments), :] = picked[
                    :, w * lanes : (w + 1) * lanes
                ]
        end = proj.shape[1]
        for tap in range(1, taps):
            for w in range(3):
                tail = proj[w, end - tap * segments : end - (tap - 1) * segments, :]
                proj[w, lead - tap * segments : lead - (tap - 1) * segments, :] = later(tail, 1)
        size = lanes

        def convolve(n, carry):
            start = n * size + lead
            conv = [jnp.zeros((size, lanes), jnp.float32) for _ in range(3)]
            for tap in range(taps):
                here = pl.ds(pl.multiple_of(start - tap * segments, segments), size)
                for w in range(3):
                    line = 2 * modes + 3 * tap + w
                    conv[w] = conv[w] + params[m, line : line + 1, :] * proj[w, here, :]
            there = pl.ds(pl.multiple_of(n * size, size), size)
            query[there, :] = conv[0]
            gated[there, :] = conv[1] * conv[2]
            return carry

        lax.fori_loop(0, segments * steps // size, convolve, 0)
        rate, residue = params[m, :modes, :], params[m, modes : 2 * modes, :]
        decay = [spread_rows(jnp.exp(-rate[i : i + 1, :])) for i in range(modes)]

        def ends(n, state):
            for u in range(unroll):
                here = pl.ds(pl.multiple_of((n * unroll + u) * segments, segments), segments)
                row = gated[here, :]
                state = tuple(d * s + row for d, s in zip(decay, state))
            return state

        zero = jnp.zeros((segments, lanes), jnp.float32)
        state = lax.fori_loop(0, steps // unroll, ends, (zero,) * modes)
        entering = []
        for i in range(modes):
            value = later(state[i], 1)
            by = 1
            while by < segments:
                jump = jnp.exp(-rate[i : i + 1, :] * float(steps * by))
                value = value + jump * later(value, by)
                by *= 2
            entering.append(value)
        strength = [
            spread_rows(residue[i : i + 1, :] * jnp.sqrt(2.0 * rate[i : i + 1, :]))
            for i in range(modes)
        ]
        skip = spread_rows(params[m, skip_row : skip_row + 1, :])

        def advance(n, state):
            for u in range(unroll):
                here = pl.ds(pl.multiple_of((n * unroll + u) * segments, segments), segments)
                row = gated[here, :]
                total = [skip * row, None]
                new = []
                for i in range(modes):
                    now = decay[i] * state[i] + row
                    new.append(now)
                    term = strength[i] * now
                    total[i % 2] = term if total[i % 2] is None else total[i % 2] + term
                state = tuple(new)
                query[here, :] = query[here, :] * (total[0] + total[1])
            return state

        state = tuple(entering)
        for k in range(turns):
            first_step = k * turn_rows // unroll
            state = lax.fori_loop(first_step, first_step + turn_rows // unroll, advance, state)
            piece = slice(k * turn_rows, (k + 1) * turn_rows)
            for s in range(segments):
                mixed[m, s, piece, :] = query[
                    pl.ds(k * turn_rows * segments + s, turn_rows, stride=segments), :
                ].astype(jnp.bfloat16)
            for d, peer in enumerate(ctx_peers):
                turn_copy(m, plane, k, d, peer).start()
            gathered[plane, piece, channels] = mixed[m, me, piece, :]
            if k > 0:
                arrived(k - 1)
        arrived(turns - 1)

    def y_copy(slot, plane, k, peer):
        block = gathered.at[plane, pl.ds(k * turn_rows, turn_rows)]
        return remote(block, block, y_send.at[slot, k], y_recv.at[slot, k], dp=peer)

    def arrived_own(k):
        for peer in ctx_peers:
            turn_arrival(0, at, k, peer).wait_recv()

        @pl.when(outer)
        def _():
            y_copy(0, plane_outer, k, plane_inner).start()

        @pl.when(inner)
        def _():
            y_copy(1, plane_inner, k, far_inner).start()

    mix(0, at, arrived_own)
    offer(2)

    @pl.when(outer)
    def _():
        dup_params.wait_recv()
        for k in range(chunks):
            dup_copy(k).wait_recv()

        def arrived_twin(k):
            for peer in ctx_peers:
                turn_arrival(1, plane_inner, k, peer).wait_recv()

        mix(1, plane_inner, arrived_twin)

    offer(3)
    acc[...] = jnp.dot(
        hot[pl.ds(pl.multiple_of(me * steps, steps), steps), :],
        own[...],
        preferred_element_type=jnp.float32,
    )

    def take(p):
        for way in range(2):
            own_piece(way, p).wait_recv()
        send(pass_piece(p))
        for way in range(2):
            send(core_piece(way, p))

    @pl.when(inner)
    def _():
        for k in range(turns):
            y_copy(0, plane_outer, k, plane_outer).wait_recv()
            y_copy(2, plane_outer, k, far_inner).start()
            y_copy(1, far_inner, k, far_inner).wait_recv()
            y_copy(3, far_inner, k, plane_outer).start()

    for p in range(pieces):
        take(p)

    @pl.when(inner)
    def _():
        for k in range(turns):
            y_copy(2, far_outer, k, far_inner).wait_recv()
            y_copy(4, far_outer, k, plane_outer).start()

    @pl.when(outer)
    def _():
        for k in range(turns):
            y_copy(3, far_inner, k, plane_inner).wait_recv()

    for p in range(pieces):
        pass_piece(p).wait_recv()
        send(core_piece(2, p))
    loads[1].wait()
    to_partner.wait_recv()
    for p in range(pieces):
        for which in range(3):
            core_piece(which, p).wait_recv()

    def weights_of(plane):
        return w_all[pl.ds(pl.multiple_of(plane * width, width), width), :]

    for plane in (plane_outer, plane_inner, far_inner):
        acc[...] += jnp.dot(
            gathered[plane], weights_of(plane), preferred_element_type=jnp.float32
        )
    for k in range(turns):

        @pl.when(outer)
        def _():
            y_copy(4, far_outer, k, plane_inner).wait_recv()

        piece = slice(k * turn_rows, (k + 1) * turn_rows)
        out_ref[piece, :] = (
            acc[piece, :]
            + jnp.dot(
                gathered[far_outer, piece, :],
                weights_of(far_outer),
                preferred_element_type=jnp.float32,
            )
        ).astype(out_ref.dtype)

    for copy in sends:
        copy.wait_send()

    @pl.when(source)
    def _():
        for d in range(n_dp - 1):
            gain_copy(d).wait_send()

    for k in range(hops):

        @pl.when((source | above) & can_up)
        def _():
            z_copy(tab, k, 0, at).wait_send()

        @pl.when((source | below) & can_down)
        def _():
            z_copy(tab, k, 1, at).wait_send()

        @pl.when(jnp.logical_not(source))
        def _():
            core_copy(k).wait_send()

    @pl.when(inner)
    def _():
        dup_params.wait_send()
        for k in range(chunks):
            dup_copy(k).wait_send()
        for k in range(turns):
            for slot, plane in ((1, plane_inner), (2, plane_outer), (3, far_inner), (4, far_outer)):
                y_copy(slot, plane, k, far_inner).wait_send()

    for k in range(turns):
        for d, peer in enumerate(ctx_peers):
            turn_copy(0, at, k, d, peer).wait_send()

    @pl.when(outer)
    def _():
        for k in range(turns):
            y_copy(0, plane_outer, k, plane_inner).wait_send()
            for d, peer in enumerate(ctx_peers):
                turn_copy(1, plane_inner, k, d, peer).wait_send()


def by_channel(
    n_ctx,
    n_dp,
    ids,
    embed_table,
    norm_gain,
    w_query,
    w_key,
    w_value,
    short_filter,
    pole_rate,
    residue,
    skip_gain,
    w_out,
):
    vocab, width = embed_table.shape
    depth, lanes = w_query.shape[0], w_query.shape[1] // n_ctx
    steps, modes, taps = ids.shape[0], pole_rate.shape[1], short_filter.shape[0]
    tokens, span = n_ctx * steps, 3 * lanes
    chips = n_ctx // 2
    chunks = vocab // LANES
    hops = 2 * chunks
    turns, pieces = 4, 4
    kind = w_query.dtype
    lines = 2 * modes + 3 * taps + 1
    lines += -lines % SUBLANES
    anywhere = pl.BlockSpec(memory_space=pl.ANY)
    whole = pl.BlockSpec(memory_space=pltpu.VMEM)
    dma = pltpu.SemaphoreType.DMA
    vmem = pltpu.VMEM
    f32 = jnp.float32
    return pl.pallas_call(
        lambda *refs: block_kernel(n_ctx, n_dp, *refs),
        name="block",
        out_shape=jax.ShapeDtypeStruct((steps, w_out.shape[1]), embed_table.dtype),
        in_specs=[whole] * 6 + [anywhere] * 5,
        out_specs=whole,
        scratch_shapes=[
            vmem((n_ctx, SUBLANES, LANES), ids.dtype),
            vmem((vocab, width), kind),
            vmem((vocab, width), kind),
            vmem((2 * depth, chips * span), kind),
            vmem((vocab, 2 * span), kind),
            vmem((vocab, 2 * span), kind),
            vmem((vocab, span), f32),
            vmem((vocab, span), kind),
            vmem((vocab, span), kind),
            vmem((vocab, span), f32),
            vmem((n_dp, SUBLANES, LANES), f32),
            vmem((vocab, LANES), f32),
            vmem((width // LANES, LANES), f32),
            vmem((2, vocab, span), kind),
            vmem((2, lines, LANES), f32),
            vmem((tokens, vocab), kind),
            vmem((3, n_ctx * (taps - 1) + tokens, lanes), f32),
            vmem((tokens, lanes), f32),
            vmem((tokens, lanes), f32),
            vmem((2, n_ctx, steps, lanes), kind),
            vmem((n_dp, steps, n_ctx * lanes), kind),
            vmem((n_ctx * depth, w_out.shape[1]), kind),
            vmem((steps, w_out.shape[1]), f32),
            dma((2, hops)),
            dma((hops,)),
            dma((hops,)),
            dma((hops,)),
            dma((chips * 3,)),
            dma((chips * 3,)),
            dma((n_ctx - 1,)),
            dma((n_ctx,)),
            dma((n_dp - 1,)),
            dma((n_dp,)),
            dma((n_dp - 1,)),
            dma((1,)),
            dma((2, chunks)),
            dma((2, chunks)),
            dma((2, chunks)),
            dma((2, chunks)),
            dma((chunks + 1,)),
            dma((chunks + 1,)),
            dma((2, turns, n_ctx - 1)),
            dma((2, turns, n_ctx)),
            dma((5, turns)),
            dma((5, turns)),
            dma((2, pieces)),
            dma((2, pieces)),
            dma((pieces,)),
            dma((pieces,)),
            dma((4, pieces)),
            dma((4, pieces)),
            dma((2 + chips * 3,)),
        ],
        compiler_params=pltpu.CompilerParams(
            collective_id=0, has_side_effects=True, vmem_limit_bytes=VMEM_BYTES
        ),
    )(
        ids.reshape(-1, LANES),
        norm_gain[None, :],
        short_filter,
        pole_rate.T,
        residue.T,
        skip_gain[None, :],
        embed_table,
        w_query,
        w_key,
        w_value,
        w_out,
    )


def solution(mesh):
    placed = (
        P("ctx"),
        P(None, "dp"),
        P("dp"),
        P("ctx", "dp"),
        P("ctx", "dp"),
        P("ctx", "dp"),
        P(None, None, "dp"),
        P("dp", None),
        P("dp", None),
        P("dp"),
        P("ctx", "dp"),
    )
    n_ctx, n_dp = mesh.shape["ctx"], mesh.shape["dp"]

    def body(*args):
        ids, table, w_query = args[0], args[1], args[3]
        fits = (
            n_ctx == SUBLANES
            and n_ctx == 2 * n_dp
            and w_query.shape[1] == n_ctx * LANES
            and table.shape[1] == 2 * w_query.shape[0]
            and table.shape[0] % LANES == 0
            and table.shape[0] < SUBLANES * LANES
            and ids.shape[0] % LANES == 0
            and ids.shape[0] < SUBLANES * LANES
        )
        if fits:
            return by_channel(n_ctx, n_dp, *args)
        return shards(*args)

    return jax.shard_map(
        body, mesh=mesh, in_specs=placed, out_specs=P("ctx", "dp"), check_vma=False
    )
```

```python
import math

import jax
import jax.numpy as jnp
from jax import lax

from jax.experimental import pallas as pl
from jax.experimental.pallas import tpu as pltpu
from jax.sharding import PartitionSpec as P

MESH = pl.DeviceIdType.MESH
LANES = 128
SUBLANES = 8
VMEM_BYTES = 56 << 20


def shifted(value, axis, steps):
    count = lax.axis_size(axis)
    initial, last = (max(0, -steps), min(count, count - steps))
    return lax.ppermute(value, axis, [(source, source + steps) for source in range(initial, last)])


def entering_2(value, axis, combine, identity):
    peers, index = (lax.axis_size(axis), lax.axis_index(axis))
    everything = jax.tree.map(lambda part: lax.all_gather(part, axis), value)
    start = jax.tree.map(
        lambda part, zero: jnp.broadcast_to(jnp.asarray(zero, part.dtype), part.shape),
        value,
        identity,
    )

    def turn(k, before):
        reached = k < index
        new = combine(before, jax.tree.map(lambda part: part[k], everything))
        return jax.tree.map(lambda a, b: jnp.where(reached, a, b), new, before)

    return lax.fori_loop(0, peers, turn, start)


def shards(
    ids,
    embed_table,
    norm_gain,
    w_query,
    w_key,
    w_value,
    short_filter,
    pole_rate,
    residue,
    skip_gain,
    w_out,
):
    highest = lax.Precision.HIGHEST
    vocab = embed_table.shape[0]
    channels = w_query.shape[1]
    one_hot = (ids[:, None] == jnp.arange(vocab, dtype=jnp.int32)[None, :]).astype(jnp.bfloat16)
    embedded = jnp.dot(one_hot, embed_table, preferred_element_type=jnp.float32).astype(
        jnp.bfloat16
    )
    full_rows, full_gain = (
        lax.all_gather(embedded, "dp", axis=1, tiled=True),
        lax.all_gather(norm_gain, "dp", axis=0, tiled=True),
    )
    floated = full_rows.astype(jnp.float32)
    scale = lax.rsqrt(jnp.mean(floated * floated, axis=1, keepdims=True) + 1e-06)
    normed = (floated * scale * full_gain.astype(jnp.float32)[None, :]).astype(jnp.bfloat16)
    tok_rows = normed.shape[0]

    def add_rows(piece):
        return jnp.dot(normed, piece, preferred_element_type=jnp.float32)

    query_proj = add_rows(lax.all_gather(w_query, "ctx", axis=0, tiled=True))
    key_proj = add_rows(lax.all_gather(w_key, "ctx", axis=0, tiled=True))
    value_proj = add_rows(lax.all_gather(w_value, "ctx", axis=0, tiled=True))
    projected = jnp.concatenate([query_proj, key_proj, value_proj], axis=1).astype(jnp.bfloat16)
    taps = short_filter.shape[0]
    previous = shifted(projected[tok_rows - (taps - 1) :], "ctx", 1)
    extended = jnp.concatenate([previous, projected], axis=0).astype(jnp.float32)
    filt_rows = short_filter.reshape(taps, 3 * channels)
    convolved = jnp.zeros((tok_rows, 3 * channels), jnp.float32)
    for tap in range(taps):
        convolved = (
            convolved
            + filt_rows[tap][None, :] * extended[taps - 1 - tap : taps - 1 - tap + tok_rows]
        )
    query_conv = convolved[:, :channels]
    gated = convolved[:, channels : 2 * channels] * convolved[:, 2 * channels :]
    sub_len = math.gcd(tok_rows, 64)
    blocks = tok_rows // sub_len
    lag_index = jnp.arange(sub_len, dtype=jnp.int32)
    lags = lag_index.astype(jnp.float32)
    strength = residue * jnp.sqrt(2.0 * pole_rate)
    kernel = jnp.einsum(
        "lck,ck->lc", jnp.exp(-pole_rate[None] * lags[:, None, None]), strength, precision=highest
    )
    offsets = lag_index[:, None] - lag_index[None, :]
    toeplitz = jnp.where((offsets >= 0)[:, :, None], kernel[jnp.maximum(offsets, 0)], 0.0)
    pieces = gated.reshape(blocks, sub_len, channels)
    inside = jnp.einsum("tsc,bsc->btc", toeplitz, pieces, precision=highest)
    tail_decay = jnp.exp(-pole_rate[None] * (sub_len - 1.0 - lags)[:, None, None])
    block_ends = jnp.einsum("sck,bsc->bck", tail_decay, pieces, precision=highest)
    step_decay = jnp.exp(-pole_rate * float(sub_len))

    def advance(state, block_end):
        return (step_decay * state + block_end, state)

    device_end, entering = lax.scan(advance, jnp.zeros_like(step_decay), block_ends)
    device_decay = jnp.exp(-pole_rate * float(tok_rows))

    def combine(earlier, later):
        return (earlier[0] * later[0], later[0] * earlier[1] + later[1])

    decay_total, incoming = entering_2(
        (device_decay, device_end),
        "ctx",
        combine,
        (jnp.ones_like(device_decay), jnp.zeros_like(device_end)),
    )
    block_pos = jnp.arange(blocks, dtype=jnp.float32) * float(sub_len)
    states_in = entering + jnp.exp(-pole_rate[None] * block_pos[:, None, None]) * incoming[None]
    lead = jnp.exp(-pole_rate[None] * (lags + 1.0)[:, None, None]) * strength[None]
    carried = jnp.einsum("tck,bck->btc", lead, states_in, precision=highest)
    long_conv = (inside + carried).reshape(tok_rows, channels) + skip_gain[None, :] * gated
    mixed = (query_conv * long_conv).astype(jnp.bfloat16)
    all_mixed = lax.all_gather(mixed, "dp", axis=1, tiled=True)
    output = jnp.dot(
        all_mixed,
        lax.all_gather(w_out, "ctx", axis=0, tiled=True),
        preferred_element_type=jnp.float32,
    )
    return (embedded.astype(jnp.float32) + output).astype(jnp.bfloat16)


def remote(src, dst, send, recv, **where):
    return pltpu.make_async_remote_copy(
        src_ref=src,
        dst_ref=dst,
        send_sem=send,
        recv_sem=recv,
        device_id=where,
        device_id_type=MESH,
    )


def greet(ctx_peers, dp_peers):
    barrier = pltpu.get_barrier_semaphore()
    for peer in ctx_peers:
        pl.semaphore_signal(barrier, inc=1, device_id={"ctx": peer}, device_id_type=MESH)
    for peer in dp_peers:
        pl.semaphore_signal(barrier, inc=1, device_id={"dp": peer}, device_id_type=MESH)
    return lambda: pl.semaphore_wait(barrier, len(ctx_peers) + len(dp_peers))


def flip(index, bit):
    return index + bit - 2 * bit * (lax.rem(index // bit, 2))


def block_kernel(
    n_ctx,
    n_dp,
    ids_ref,
    gain_ref,
    filt_ref,
    rate_ref,
    residue_ref,
    skip_ref,
    table_ref,
    wq_ref,
    wk_ref,
    wv_ref,
    wo_ref,
    out_ref,
    all_ids,
    tab,
    own,
    weights,
    first_out,
    first_in,
    hold,
    second_out,
    second_in,
    mine,
    sums,
    scales,
    gains,
    rows,
    params,
    hot,
    proj,
    gated,
    query,
    mixed,
    gathered,
    w_all,
    acc,
    z_send,
    z_recv,
    core_send,
    core_recv,
    w_send,
    w_recv,
    id_send,
    id_recv,
    sum_send,
    sum_recv,
    gain_send,
    gain_recv,
    first_send,
    first_recv,
    second_send,
    second_recv,
    dup_send,
    dup_recv,
    a_send,
    a_recv,
    y_send,
    y_recv,
    o_send,
    o_recv,
    q_send,
    q_recv,
    c_send,
    c_recv,
    local,
):
    me, at = lax.axis_index("ctx"), lax.axis_index("dp")
    vocab, width = table_ref.shape
    depth = wq_ref.shape[0]
    lanes = wq_ref.shape[1] // n_ctx
    span = 3 * lanes
    chunks = first_send.shape[1]
    part_rows = vocab // chunks
    side_rows = part_rows // 2
    hops = z_send.shape[1]
    hop_rows = vocab // hops
    half_rows = hop_rows // 2
    segments, steps = n_ctx, out_ref.shape[0]
    turns = a_send.shape[1]
    turn_rows = steps // turns
    taps = filt_ref.shape[0]
    modes = rate_ref.shape[0]
    pieces = o_send.shape[1]
    piece_rows = depth // pieces
    chip, core = me // 2, lax.rem(me, 2)
    partner, side, up = flip(me, 1), flip(me, 2), flip(me, 4)
    across = flip(side, 4)
    relatives = [me, side, up, across]
    ctx_peers = [lax.rem(me + d, n_ctx) for d in range(1, n_ctx)]
    dp_peers = [lax.rem(at + d, n_dp) for d in range(1, n_dp)]
    source, above, below = at == chip, at > chip, at < chip
    low = at < n_dp // 2
    outer = (at == 0) | (at == n_dp - 1)
    inner = jnp.logical_not(outer)
    plane_outer = jnp.where(low, 0, n_dp - 1)
    plane_inner = jnp.where(low, 1, n_dp - 2)
    far_inner = jnp.where(low, n_dp - 2, 1)
    far_outer = jnp.where(low, n_dp - 1, 0)
    channels = pl.ds(pl.multiple_of(me * lanes, lanes), lanes)

    everyone_in = greet(ctx_peers, dp_peers)
    loads = [
        pltpu.make_async_copy(table_ref, own, local.at[0]),
        pltpu.make_async_copy(
            wo_ref, w_all.at[pl.ds(pl.multiple_of(me * depth, depth), depth)], local.at[1]
        ),
    ]
    for r, peer in enumerate(relatives):
        for w, weight in enumerate((wq_ref, wk_ref, wv_ref)):
            column = pl.multiple_of(peer * lanes, lanes)
            loads.append(
                pltpu.make_async_copy(
                    weight.at[:, pl.ds(column, lanes)],
                    weights.at[
                        pl.ds(pl.multiple_of(core * depth, depth), depth),
                        pl.ds((r * 3 + w) * lanes, lanes),
                    ],
                    local.at[2 + r * 3 + w],
                )
            )
    for copy in loads:
        copy.start()
    all_ids[me] = jnp.concatenate(
        [ids_ref[...], jnp.zeros((SUBLANES - ids_ref.shape[0], LANES), ids_ref.dtype)], axis=0
    )
    params[0, :modes, :] = rate_ref[:, channels]
    params[0, modes : 2 * modes, :] = residue_ref[:, channels]
    for tap in range(taps):
        params[0, 2 * modes + 3 * tap : 2 * modes + 3 * tap + 3, :] = filt_ref[tap, :, channels]
    skip_row = 2 * modes + 3 * taps
    params[0, skip_row : skip_row + 1, :] = skip_ref[:, channels]

    @pl.when(source)
    def _():
        wide = gain_ref[...].astype(jnp.float32).reshape(1, width)
        gains[...] = jnp.concatenate(
            [wide[:, r * LANES : (r + 1) * LANES] for r in range(width // LANES)], axis=0
        )

    everyone_in()

    def gain_copy(d):
        return remote(gains, gains, gain_send.at[d], gain_recv.at[0], dp=dp_peers[d])

    @pl.when(source)
    def _():
        for d in range(n_dp - 1):
            gain_copy(d).start()

    sends = []

    def send(copy):
        copy.start()
        sends.append(copy)

    def half(k, which):
        return pl.ds(pl.multiple_of(k * hop_rows + which * half_rows, half_rows), half_rows)

    def z_copy(src, k, way, peer):
        piece = half(k, core)
        return remote(src.at[piece], tab.at[piece], z_send.at[way, k], z_recv.at[k], dp=peer)

    def core_copy(k):
        piece = half(k, core)
        return remote(tab.at[piece], tab.at[piece], core_send.at[k], core_recv.at[k], ctx=partner)

    def core_arrival(k):
        piece = half(k, 1 - core)
        return remote(tab.at[piece], tab.at[piece], core_send.at[k], core_recv.at[k], ctx=partner)

    can_up, can_down = at < n_dp - 1, at > 0
    def depart(k):
        @pl.when(source & can_up)
        def _():
            z_copy(table_ref, k, 0, at + 1).start()

        @pl.when(source & can_down)
        def _():
            z_copy(table_ref, k, 1, at - 1).start()

    early = min(2, hops)
    for k in range(early):
        depart(k)
    swaps = []
    for r, peer in enumerate(relatives):
        for w, weight in enumerate((wq_ref, wk_ref, wv_ref)):
            column = pl.multiple_of(flip(peer, 1) * lanes, lanes)
            swaps.append(
                remote(
                    weight.at[:, pl.ds(column, lanes)],
                    weights.at[
                        pl.ds(pl.multiple_of(core * depth, depth), depth),
                        pl.ds((r * 3 + w) * lanes, lanes),
                    ],
                    w_send.at[r * 3 + w],
                    w_recv.at[r * 3 + w],
                    ctx=partner,
                )
            )
            send(swaps[-1])

    loads[0].wait()
    groups = vocab // LANES
    lines = []
    for g in range(groups):
        block = own[g * LANES : (g + 1) * LANES, :].astype(jnp.float32)
        total = jnp.sum(block * block, axis=1, keepdims=True)
        lines.append(jnp.broadcast_to(total, (LANES, LANES)).T[:1, :])
    lines.append(jnp.zeros((SUBLANES - groups, LANES), jnp.float32))
    sums[at] = jnp.concatenate(lines, axis=0)

    for d, peer in enumerate(dp_peers):
        send(remote(sums.at[at], sums.at[at], sum_send.at[d], sum_recv.at[at], dp=peer))

    for k in range(early, hops):
        depart(k)

    @pl.when(source)
    def _():
        tab[...] = own[...]

    for d, peer in enumerate(ctx_peers):
        send(remote(all_ids.at[me], all_ids.at[me], id_send.at[d], id_recv.at[me], ctx=peer))

    def piece_of(owner, p):
        start = pl.multiple_of(owner * depth + p * piece_rows, piece_rows)
        return w_all.at[pl.ds(start, piece_rows)]

    def own_piece(way, p):
        return remote(
            wo_ref.at[pl.ds(p * piece_rows, piece_rows)],
            piece_of(me, p),
            o_send.at[way, p],
            o_recv.at[way, p],
            ctx=(side, up)[way],
        )

    def pass_piece(p):
        owner, peer = ((side, up), (up, side))[p % 2]
        return remote(piece_of(owner, p), piece_of(owner, p), q_send.at[p], q_recv.at[p], ctx=peer)

    def core_piece(which, p):
        owner = (side, up, across)[which]
        return remote(
            piece_of(owner, p), piece_of(owner, p), c_send.at[which, p], c_recv.at[which, p], ctx=partner
        )

    whole_mine = pl.ds(pl.multiple_of(me * depth, depth), depth)
    to_partner = remote(wo_ref, w_all.at[whole_mine], c_send.at[3, 0], c_recv.at[3, 0], ctx=partner)

    def offer(p):
        for way in range(2):
            send(own_piece(way, p))

    offer(0)
    offer(1)
    send(to_partner)

    def arrive(h):
        @pl.when(above)
        def _():
            z_copy(tab, h, 0, at).wait_recv()

            @pl.when(can_up)
            def _():
                z_copy(tab, h, 0, at + 1).start()

        @pl.when(below)
        def _():
            z_copy(tab, h, 1, at).wait_recv()

            @pl.when(can_down)
            def _():
                z_copy(tab, h, 1, at - 1).start()

        @pl.when(jnp.logical_not(source))
        def _():
            core_copy(h).start()

    def settle():
        for peer in dp_peers:
            remote(sums.at[peer], sums.at[peer], sum_send.at[0], sum_recv.at[peer], dp=peer).wait_recv()
        total = sums[0]
        for b in range(1, n_dp):
            total = total + sums[b]
        scale = lax.rsqrt(total / (n_dp * width) + 1e-06)
        for g in range(groups):
            scales[g * LANES : (g + 1) * LANES, :] = jnp.broadcast_to(
                scale[g : g + 1, :], (LANES, LANES)
            ).T

        @pl.when(jnp.logical_not(source))
        def _():
            gain_copy(0).wait_recv()

        for copy in loads[2:]:
            copy.wait()
        for copy in swaps:
            copy.wait_recv()

    def sides(k, way):
        start = k * part_rows + way * side_rows
        return slice(start, start + side_rows)

    def first(k, way):
        piece = pl.ds(k * part_rows + way * side_rows, side_rows)
        return remote(
            first_out.at[piece],
            first_in.at[piece],
            first_send.at[way, k],
            first_recv.at[way, k],
            ctx=(side, up)[way],
        )

    def second(k, way):
        piece = pl.ds(k * part_rows + way * side_rows, side_rows)
        return remote(
            second_out.at[piece],
            second_in.at[piece],
            second_send.at[way, k],
            second_recv.at[way, k],
            ctx=(up, side)[way],
        )

    def relay(k):
        for way in range(2):
            first(k, way).wait_recv()
            piece = sides(k, way)
            second_out[piece, :] = (
                hold[piece, :] + first_in[piece, span:].astype(jnp.float32)
            ).astype(jnp.bfloat16)
            send(second(k, way))

    for k in range(chunks):
        for h in range(k * hops // chunks, (k + 1) * hops // chunks):
            arrive(h)
        for h in range(k * hops // chunks, (k + 1) * hops // chunks):

            @pl.when(jnp.logical_not(source))
            def _():
                core_arrival(h).wait_recv()

        if k == 0:
            settle()
            gain = jnp.concatenate([gains[r : r + 1, :] for r in range(width // LANES)], axis=1)
        piece = slice(k * part_rows, (k + 1) * part_rows)
        by_row = jnp.concatenate([scales[piece, :]] * (width // LANES), axis=1)
        normed = (tab[piece, :].astype(jnp.float32) * by_row * gain).astype(jnp.bfloat16)

        def product(r):
            return jnp.dot(
                normed, weights[:, r * span : (r + 1) * span], preferred_element_type=jnp.float32
            )

        cuts = [slice(0, side_rows), slice(side_rows, part_rows)]
        diagonal = product(3).astype(jnp.bfloat16)
        for way in range(2):
            along = product(1 + way)
            first_out[sides(k, way), :span] = along[cuts[way], :].astype(jnp.bfloat16)
            first_out[sides(k, way), span:] = diagonal[cuts[way], :]
            hold[sides(k, 1 - way), :] = along[cuts[1 - way], :]
            send(first(k, way))
        mine[piece, :] = product(0)
        if k > 0:
            relay(k - 1)
    relay(chunks - 1)

    for peer in ctx_peers:
        remote(all_ids.at[peer], all_ids.at[peer], id_send.at[0], id_recv.at[peer], ctx=peer).wait_recv()
    names = lax.broadcasted_iota(jnp.int32, (lanes, vocab), 1)
    for s in range(segments):
        columns = jnp.concatenate(
            [all_ids[s].astype(jnp.float32), jnp.zeros((lanes - SUBLANES, lanes), jnp.float32)], axis=0
        ).T.astype(jnp.int32)
        for p in range(steps // lanes):
            start = s * steps + p * lanes
            hot[start : start + lanes, :] = (
                (columns[:, p : p + 1] == names).astype(jnp.float32).astype(jnp.bfloat16)
            )

    def dup_copy(k):
        piece = pl.ds(k * part_rows, part_rows)
        return remote(
            rows.at[0, piece], rows.at[1, piece], dup_send.at[k], dup_recv.at[k], dp=plane_outer
        )

    dup_params = remote(
        params.at[0], params.at[1], dup_send.at[chunks], dup_recv.at[chunks], dp=plane_outer
    )
    for k in range(chunks):
        for way in range(2):
            second(k, way).wait_recv()
            piece = sides(k, way)
            rows[0, piece, :] = (
                mine[piece, :]
                + first_in[piece, :span].astype(jnp.float32)
                + second_in[piece, :].astype(jnp.float32)
            ).astype(jnp.bfloat16)

        @pl.when(inner)
        def _():
            dup_copy(k).start()
            if k == 0:
                dup_params.start()

    lead = proj.shape[1] - segments * steps
    place_of = lax.broadcasted_iota(jnp.int32, (segments, lanes), 0)

    def later(value, by):
        return jnp.where(place_of >= by, pltpu.roll(value, by, 0), 0.0)

    def spread_rows(row):
        return jnp.broadcast_to(row, (segments, lanes))

    unroll = 4

    def turn_copy(m, plane, k, d, peer):
        piece = pl.ds(k * turn_rows, turn_rows)
        return remote(
            mixed.at[m, peer, piece],
            gathered.at[plane, piece, channels],
            a_send.at[m, k, d],
            a_recv.at[m, k, me],
            ctx=peer,
        )

    def turn_arrival(m, plane, k, peer):
        piece = pl.ds(k * turn_rows, turn_rows)
        theirs = gathered.at[plane, piece, pl.ds(pl.multiple_of(peer * lanes, lanes), lanes)]
        return remote(theirs, theirs, a_send.at[m, k, 0], a_recv.at[m, k, peer], ctx=peer)

    def mix(m, plane, between, arrived):
        for s in range(segments):
            picked = jnp.dot(
                hot[s * steps : (s + 1) * steps, :], rows[m], preferred_element_type=jnp.float32
            )
            for w in range(3):
                proj[w, pl.ds(lead + s, steps, stride=segments), :] = picked[
                    :, w * lanes : (w + 1) * lanes
                ]
        end = proj.shape[1]
        for tap in range(1, taps):
            for w in range(3):
                tail = proj[w, end - tap * segments : end - (tap - 1) * segments, :]
                proj[w, lead - tap * segments : lead - (tap - 1) * segments, :] = later(tail, 1)
        size = lanes

        def convolve(n, carry):
            start = n * size + lead
            conv = [jnp.zeros((size, lanes), jnp.float32) for _ in range(3)]
            for tap in range(taps):
                here = pl.ds(pl.multiple_of(start - tap * segments, segments), size)
                for w in range(3):
                    line = 2 * modes + 3 * tap + w
                    conv[w] = conv[w] + params[m, line : line + 1, :] * proj[w, here, :]
            there = pl.ds(pl.multiple_of(n * size, size), size)
            query[there, :] = conv[0]
            gated[there, :] = conv[1] * conv[2]
            return carry

        lax.fori_loop(0, segments * steps // size, convolve, 0)
        rate, residue = params[m, :modes, :], params[m, modes : 2 * modes, :]
        decay = [spread_rows(jnp.exp(-rate[i : i + 1, :])) for i in range(modes)]

        def ends(n, state):
            for u in range(unroll):
                here = pl.ds(pl.multiple_of((n * unroll + u) * segments, segments), segments)
                row = gated[here, :]
                state = tuple(d * s + row for d, s in zip(decay, state))
            return state

        zero = jnp.zeros((segments, lanes), jnp.float32)
        state = lax.fori_loop(0, steps // unroll, ends, (zero,) * modes)
        entering = []
        for i in range(modes):
            value = later(state[i], 1)
            by = 1
            while by < segments:
                jump = jnp.exp(-rate[i : i + 1, :] * float(steps * by))
                value = value + jump * later(value, by)
                by *= 2
            entering.append(value)
        strength = [
            spread_rows(residue[i : i + 1, :] * jnp.sqrt(2.0 * rate[i : i + 1, :]))
            for i in range(modes)
        ]
        skip = spread_rows(params[m, skip_row : skip_row + 1, :])

        def advance(n, state):
            for u in range(unroll):
                here = pl.ds(pl.multiple_of((n * unroll + u) * segments, segments), segments)
                row = gated[here, :]
                total = [skip * row, None]
                new = []
                for i in range(modes):
                    now = decay[i] * state[i] + row
                    new.append(now)
                    term = strength[i] * now
                    total[i % 2] = term if total[i % 2] is None else total[i % 2] + term
                state = tuple(new)
                query[here, :] = query[here, :] * (total[0] + total[1])
            return state

        state = tuple(entering)
        between()
        for k in range(turns):
            first_step = k * turn_rows // unroll
            state = lax.fori_loop(first_step, first_step + turn_rows // unroll, advance, state)
            piece = slice(k * turn_rows, (k + 1) * turn_rows)
            for s in range(segments):
                mixed[m, s, piece, :] = query[
                    pl.ds(k * turn_rows * segments + s, turn_rows, stride=segments), :
                ].astype(jnp.bfloat16)
            for d, peer in enumerate(ctx_peers):
                turn_copy(m, plane, k, d, peer).start()
            gathered[plane, piece, channels] = mixed[m, me, piece, :]
            if k > 0:
                arrived(k - 1)
        arrived(turns - 1)

    def y_copy(slot, plane, k, peer):
        block = gathered.at[plane, pl.ds(k * turn_rows, turn_rows)]
        return remote(block, block, y_send.at[slot, k], y_recv.at[slot, k], dp=peer)

    def arrival(m, plane, k):
        for peer in ctx_peers:
            turn_arrival(m, plane, k, peer).wait_recv()

    def nothing(*_):
        pass

    def own_inner(k):
        @pl.when(inner)
        def _():
            arrival(0, at, k)
            y_copy(1, plane_inner, k, far_inner).start()

    def own_outer():
        for k in range(turns):
            arrival(0, at, k)
            y_copy(0, plane_outer, k, plane_inner).start()

    def take(p):
        for way in range(2):
            own_piece(way, p).wait_recv()
        send(pass_piece(p))
        for way in range(2):
            send(core_piece(way, p))

    mix(0, at, nothing, own_inner)
    offer(2)
    offer(3)
    take(0)
    take(1)

    @pl.when(outer)
    def _():
        dup_params.wait_recv()
        for k in range(chunks):
            dup_copy(k).wait_recv()
        mix(1, plane_inner, own_outer, nothing)

    acc[...] = jnp.dot(
        hot[pl.ds(pl.multiple_of(me * steps, steps), steps), :],
        own[...],
        preferred_element_type=jnp.float32,
    )

    @pl.when(inner)
    def _():
        ahead = turns // 2
        for k in range(turns + ahead):
            if k < turns:
                y_copy(1, far_inner, k, far_inner).wait_recv()
                y_copy(3, far_inner, k, plane_outer).start()
            if k >= ahead:
                y_copy(0, plane_outer, k - ahead, plane_outer).wait_recv()
                y_copy(2, plane_outer, k - ahead, far_inner).start()

    for p in range(2, pieces):
        take(p)

    @pl.when(inner)
    def _():
        for k in range(turns):
            y_copy(2, far_outer, k, far_inner).wait_recv()
            y_copy(4, far_outer, k, plane_outer).start()

    @pl.when(outer)
    def _():
        for k in range(turns):
            arrival(1, plane_inner, k)
            y_copy(3, far_inner, k, plane_inner).wait_recv()

    for p in range(pieces):
        pass_piece(p).wait_recv()
        send(core_piece(2, p))
    loads[1].wait()
    to_partner.wait_recv()
    for p in range(pieces):
        for which in range(3):
            core_piece(which, p).wait_recv()

    def weights_of(plane):
        return w_all[pl.ds(pl.multiple_of(plane * width, width), width), :]

    for plane in (plane_outer, plane_inner, far_inner):
        acc[...] += jnp.dot(
            gathered[plane], weights_of(plane), preferred_element_type=jnp.float32
        )
    for k in range(turns):

        @pl.when(outer)
        def _():
            y_copy(4, far_outer, k, plane_inner).wait_recv()

        piece = slice(k * turn_rows, (k + 1) * turn_rows)
        out_ref[piece, :] = (
            acc[piece, :]
            + jnp.dot(
                gathered[far_outer, piece, :],
                weights_of(far_outer),
                preferred_element_type=jnp.float32,
            )
        ).astype(out_ref.dtype)

    for copy in sends:
        copy.wait_send()

    @pl.when(source)
    def _():
        for d in range(n_dp - 1):
            gain_copy(d).wait_send()

    for k in range(hops):

        @pl.when((source | above) & can_up)
        def _():
            z_copy(tab, k, 0, at).wait_send()

        @pl.when((source | below) & can_down)
        def _():
            z_copy(tab, k, 1, at).wait_send()

        @pl.when(jnp.logical_not(source))
        def _():
            core_copy(k).wait_send()

    @pl.when(inner)
    def _():
        dup_params.wait_send()
        for k in range(chunks):
            dup_copy(k).wait_send()
        for k in range(turns):
            for slot, plane in ((1, plane_inner), (2, plane_outer), (3, far_inner), (4, far_outer)):
                y_copy(slot, plane, k, far_inner).wait_send()

    for k in range(turns):
        for d, peer in enumerate(ctx_peers):
            turn_copy(0, at, k, d, peer).wait_send()

    @pl.when(outer)
    def _():
        for k in range(turns):
            y_copy(0, plane_outer, k, plane_inner).wait_send()
            for d, peer in enumerate(ctx_peers):
                turn_copy(1, plane_inner, k, d, peer).wait_send()


def by_channel(
    n_ctx,
    n_dp,
    ids,
    embed_table,
    norm_gain,
    w_query,
    w_key,
    w_value,
    short_filter,
    pole_rate,
    residue,
    skip_gain,
    w_out,
):
    vocab, width = embed_table.shape
    depth, lanes = w_query.shape[0], w_query.shape[1] // n_ctx
    steps, modes, taps = ids.shape[0], pole_rate.shape[1], short_filter.shape[0]
    tokens, span = n_ctx * steps, 3 * lanes
    chips = n_ctx // 2
    chunks = vocab // LANES
    hops = 2 * chunks
    turns, pieces = 4, 4
    kind = w_query.dtype
    lines = 2 * modes + 3 * taps + 1
    lines += -lines % SUBLANES
    far = pl.BlockSpec(memory_space=pltpu.HBM)
    whole = pl.BlockSpec(memory_space=pltpu.VMEM)
    dma = pltpu.SemaphoreType.DMA
    vmem = pltpu.VMEM
    f32 = jnp.float32
    return pl.pallas_call(
        lambda *refs: block_kernel(n_ctx, n_dp, *refs),
        name="block",
        out_shape=jax.ShapeDtypeStruct((steps, w_out.shape[1]), embed_table.dtype),
        in_specs=[whole] * 6 + [far] * 5,
        out_specs=whole,
        scratch_shapes=[
            vmem((n_ctx, SUBLANES, LANES), ids.dtype),
            vmem((vocab, width), kind),
            vmem((vocab, width), kind),
            vmem((2 * depth, chips * span), kind),
            vmem((vocab, 2 * span), kind),
            vmem((vocab, 2 * span), kind),
            vmem((vocab, span), f32),
            vmem((vocab, span), kind),
            vmem((vocab, span), kind),
            vmem((vocab, span), f32),
            vmem((n_dp, SUBLANES, LANES), f32),
            vmem((vocab, LANES), f32),
            vmem((width // LANES, LANES), f32),
            vmem((2, vocab, span), kind),
            vmem((2, lines, LANES), f32),
            vmem((tokens, vocab), kind),
            vmem((3, n_ctx * (taps - 1) + tokens, lanes), f32),
            vmem((tokens, lanes), f32),
            vmem((tokens, lanes), f32),
            vmem((2, n_ctx, steps, lanes), kind),
            vmem((n_dp, steps, n_ctx * lanes), kind),
            vmem((n_ctx * depth, w_out.shape[1]), kind),
            vmem((steps, w_out.shape[1]), f32),
            dma((2, hops)),
            dma((hops,)),
            dma((hops,)),
            dma((hops,)),
            dma((chips * 3,)),
            dma((chips * 3,)),
            dma((n_ctx - 1,)),
            dma((n_ctx,)),
            dma((n_dp - 1,)),
            dma((n_dp,)),
            dma((n_dp - 1,)),
            dma((1,)),
            dma((2, chunks)),
            dma((2, chunks)),
            dma((2, chunks)),
            dma((2, chunks)),
            dma((chunks + 1,)),
            dma((chunks + 1,)),
            dma((2, turns, n_ctx - 1)),
            dma((2, turns, n_ctx)),
            dma((5, turns)),
            dma((5, turns)),
            dma((2, pieces)),
            dma((2, pieces)),
            dma((pieces,)),
            dma((pieces,)),
            dma((4, pieces)),
            dma((4, pieces)),
            dma((2 + chips * 3,)),
        ],
        compiler_params=pltpu.CompilerParams(
            collective_id=0, has_side_effects=True, vmem_limit_bytes=VMEM_BYTES
        ),
    )(
        ids.reshape(-1, LANES),
        norm_gain,
        short_filter,
        pole_rate.T,
        residue.T,
        skip_gain[None, :],
        embed_table,
        w_query,
        w_key,
        w_value,
        w_out,
    )


def solution(mesh):
    placed = (
        P("ctx"),
        P(None, "dp"),
        P("dp"),
        P("ctx", "dp"),
        P("ctx", "dp"),
        P("ctx", "dp"),
        P(None, None, "dp"),
        P("dp", None),
        P("dp", None),
        P("dp"),
        P("ctx", "dp"),
    )
    n_ctx, n_dp = mesh.shape["ctx"], mesh.shape["dp"]

    def body(*args):
        ids, table, w_query = args[0], args[1], args[3]
        fits = (
            n_ctx == SUBLANES
            and n_ctx == 2 * n_dp
            and w_query.shape[1] == n_ctx * LANES
            and table.shape[1] == 2 * w_query.shape[0]
            and table.shape[0] % LANES == 0
            and table.shape[0] < SUBLANES * LANES
            and ids.shape[0] % LANES == 0
            and ids.shape[0] < SUBLANES * LANES
        )
        if fits:
            return by_channel(n_ctx, n_dp, *args)
        return shards(*args)

    return jax.shard_map(
        body, mesh=mesh, in_specs=placed, out_specs=P("ctx", "dp"), check_vma=False
    )
```

```python
import math

import jax
import jax.numpy as jnp
from jax import lax

from jax.experimental import pallas as pl
from jax.experimental.pallas import tpu as pltpu
from jax.sharding import PartitionSpec as P

MESH = pl.DeviceIdType.MESH
LANES = 128
SUBLANES = 8
VMEM_BYTES = 56 << 20


def shifted(value, axis, steps):
    count = lax.axis_size(axis)
    initial, last = (max(0, -steps), min(count, count - steps))
    return lax.ppermute(value, axis, [(source, source + steps) for source in range(initial, last)])


def entering_2(value, axis, combine, identity):
    peers, index = (lax.axis_size(axis), lax.axis_index(axis))
    everything = jax.tree.map(lambda part: lax.all_gather(part, axis), value)
    start = jax.tree.map(
        lambda part, zero: jnp.broadcast_to(jnp.asarray(zero, part.dtype), part.shape),
        value,
        identity,
    )

    def turn(k, before):
        reached = k < index
        new = combine(before, jax.tree.map(lambda part: part[k], everything))
        return jax.tree.map(lambda a, b: jnp.where(reached, a, b), new, before)

    return lax.fori_loop(0, peers, turn, start)


def shards(
    ids,
    embed_table,
    norm_gain,
    w_query,
    w_key,
    w_value,
    short_filter,
    pole_rate,
    residue,
    skip_gain,
    w_out,
):
    highest = lax.Precision.HIGHEST
    vocab = embed_table.shape[0]
    channels = w_query.shape[1]
    one_hot = (ids[:, None] == jnp.arange(vocab, dtype=jnp.int32)[None, :]).astype(jnp.bfloat16)
    embedded = jnp.dot(one_hot, embed_table, preferred_element_type=jnp.float32).astype(
        jnp.bfloat16
    )
    full_rows, full_gain = (
        lax.all_gather(embedded, "dp", axis=1, tiled=True),
        lax.all_gather(norm_gain, "dp", axis=0, tiled=True),
    )
    floated = full_rows.astype(jnp.float32)
    scale = lax.rsqrt(jnp.mean(floated * floated, axis=1, keepdims=True) + 1e-06)
    normed = (floated * scale * full_gain.astype(jnp.float32)[None, :]).astype(jnp.bfloat16)
    tok_rows = normed.shape[0]

    def add_rows(piece):
        return jnp.dot(normed, piece, preferred_element_type=jnp.float32)

    query_proj = add_rows(lax.all_gather(w_query, "ctx", axis=0, tiled=True))
    key_proj = add_rows(lax.all_gather(w_key, "ctx", axis=0, tiled=True))
    value_proj = add_rows(lax.all_gather(w_value, "ctx", axis=0, tiled=True))
    projected = jnp.concatenate([query_proj, key_proj, value_proj], axis=1).astype(jnp.bfloat16)
    taps = short_filter.shape[0]
    previous = shifted(projected[tok_rows - (taps - 1) :], "ctx", 1)
    extended = jnp.concatenate([previous, projected], axis=0).astype(jnp.float32)
    filt_rows = short_filter.reshape(taps, 3 * channels)
    convolved = jnp.zeros((tok_rows, 3 * channels), jnp.float32)
    for tap in range(taps):
        convolved = (
            convolved
            + filt_rows[tap][None, :] * extended[taps - 1 - tap : taps - 1 - tap + tok_rows]
        )
    query_conv = convolved[:, :channels]
    gated = convolved[:, channels : 2 * channels] * convolved[:, 2 * channels :]
    sub_len = math.gcd(tok_rows, 64)
    blocks = tok_rows // sub_len
    lag_index = jnp.arange(sub_len, dtype=jnp.int32)
    lags = lag_index.astype(jnp.float32)
    strength = residue * jnp.sqrt(2.0 * pole_rate)
    kernel = jnp.einsum(
        "lck,ck->lc", jnp.exp(-pole_rate[None] * lags[:, None, None]), strength, precision=highest
    )
    offsets = lag_index[:, None] - lag_index[None, :]
    toeplitz = jnp.where((offsets >= 0)[:, :, None], kernel[jnp.maximum(offsets, 0)], 0.0)
    pieces = gated.reshape(blocks, sub_len, channels)
    inside = jnp.einsum("tsc,bsc->btc", toeplitz, pieces, precision=highest)
    tail_decay = jnp.exp(-pole_rate[None] * (sub_len - 1.0 - lags)[:, None, None])
    block_ends = jnp.einsum("sck,bsc->bck", tail_decay, pieces, precision=highest)
    step_decay = jnp.exp(-pole_rate * float(sub_len))

    def advance(state, block_end):
        return (step_decay * state + block_end, state)

    device_end, entering = lax.scan(advance, jnp.zeros_like(step_decay), block_ends)
    device_decay = jnp.exp(-pole_rate * float(tok_rows))

    def combine(earlier, later):
        return (earlier[0] * later[0], later[0] * earlier[1] + later[1])

    decay_total, incoming = entering_2(
        (device_decay, device_end),
        "ctx",
        combine,
        (jnp.ones_like(device_decay), jnp.zeros_like(device_end)),
    )
    block_pos = jnp.arange(blocks, dtype=jnp.float32) * float(sub_len)
    states_in = entering + jnp.exp(-pole_rate[None] * block_pos[:, None, None]) * incoming[None]
    lead = jnp.exp(-pole_rate[None] * (lags + 1.0)[:, None, None]) * strength[None]
    carried = jnp.einsum("tck,bck->btc", lead, states_in, precision=highest)
    long_conv = (inside + carried).reshape(tok_rows, channels) + skip_gain[None, :] * gated
    mixed = (query_conv * long_conv).astype(jnp.bfloat16)
    all_mixed = lax.all_gather(mixed, "dp", axis=1, tiled=True)
    output = jnp.dot(
        all_mixed,
        lax.all_gather(w_out, "ctx", axis=0, tiled=True),
        preferred_element_type=jnp.float32,
    )
    return (embedded.astype(jnp.float32) + output).astype(jnp.bfloat16)


def remote(src, dst, send, recv, **where):
    return pltpu.make_async_remote_copy(
        src_ref=src,
        dst_ref=dst,
        send_sem=send,
        recv_sem=recv,
        device_id=where,
        device_id_type=MESH,
    )


def greet(ctx_peers, dp_peers):
    barrier = pltpu.get_barrier_semaphore()
    for peer in ctx_peers:
        pl.semaphore_signal(barrier, inc=1, device_id={"ctx": peer}, device_id_type=MESH)
    for peer in dp_peers:
        pl.semaphore_signal(barrier, inc=1, device_id={"dp": peer}, device_id_type=MESH)
    return lambda: pl.semaphore_wait(barrier, len(ctx_peers) + len(dp_peers))


def flip(index, bit):
    return index + bit - 2 * bit * (lax.rem(index // bit, 2))


def block_kernel(
    n_ctx,
    n_dp,
    ids_ref,
    gain_ref,
    filt_ref,
    rate_ref,
    residue_ref,
    skip_ref,
    table_ref,
    wq_ref,
    wk_ref,
    wv_ref,
    wo_ref,
    out_ref,
    all_ids,
    tab,
    own,
    weights,
    first_out,
    first_in,
    hold,
    second_out,
    second_in,
    mine,
    sums,
    scales,
    gains,
    rows,
    params,
    hot,
    proj,
    gated,
    query,
    mixed,
    gathered,
    w_all,
    acc,
    z_send,
    z_recv,
    core_send,
    core_recv,
    w_send,
    w_recv,
    id_send,
    id_recv,
    sum_send,
    sum_recv,
    gain_send,
    gain_recv,
    first_send,
    first_recv,
    second_send,
    second_recv,
    dup_send,
    dup_recv,
    a_send,
    a_recv,
    y_send,
    y_recv,
    o_send,
    o_recv,
    q_send,
    q_recv,
    c_send,
    c_recv,
    local,
):
    me, at = lax.axis_index("ctx"), lax.axis_index("dp")
    vocab, width = table_ref.shape
    depth = wq_ref.shape[0]
    lanes = wq_ref.shape[1] // n_ctx
    span = 3 * lanes
    chunks = first_send.shape[1]
    part_rows = vocab // chunks
    side_rows = part_rows // 2
    hops = z_send.shape[1]
    hop_rows = vocab // hops
    half_rows = hop_rows // 2
    segments, steps = n_ctx, out_ref.shape[0]
    turns = a_send.shape[1]
    chips = n_ctx // 2
    turn_rows = steps // turns
    taps = filt_ref.shape[0]
    modes = rate_ref.shape[0]
    pieces = o_send.shape[1]
    piece_rows = depth // pieces
    chip, core = me // 2, lax.rem(me, 2)
    partner, side, up = flip(me, 1), flip(me, 2), flip(me, 4)
    across = flip(side, 4)
    relatives = [me, side, up, across]
    ctx_peers = [lax.rem(me + d, n_ctx) for d in range(1, n_ctx)]
    dp_peers = [lax.rem(at + d, n_dp) for d in range(1, n_dp)]
    source, above, below = at == chip, at > chip, at < chip
    low = at < n_dp // 2
    outer = (at == 0) | (at == n_dp - 1)
    inner = jnp.logical_not(outer)
    plane_outer = jnp.where(low, 0, n_dp - 1)
    plane_inner = jnp.where(low, 1, n_dp - 2)
    far_inner = jnp.where(low, n_dp - 2, 1)
    far_outer = jnp.where(low, n_dp - 1, 0)
    channels = pl.ds(pl.multiple_of(me * lanes, lanes), lanes)

    everyone_in = greet(ctx_peers, dp_peers)
    loads = [
        pltpu.make_async_copy(table_ref, own, local.at[0]),
        pltpu.make_async_copy(
            wo_ref, w_all.at[pl.ds(pl.multiple_of(me * depth, depth), depth)], local.at[1]
        ),
    ]
    for r, peer in enumerate(relatives):
        for w, weight in enumerate((wq_ref, wk_ref, wv_ref)):
            column = pl.multiple_of(peer * lanes, lanes)
            loads.append(
                pltpu.make_async_copy(
                    weight.at[:, pl.ds(column, lanes)],
                    weights.at[
                        pl.ds(pl.multiple_of(core * depth, depth), depth),
                        pl.ds((r * 3 + w) * lanes, lanes),
                    ],
                    local.at[2 + r * 3 + w],
                )
            )
    for copy in loads:
        copy.start()
    all_ids[me] = jnp.concatenate(
        [ids_ref[...], jnp.zeros((SUBLANES - ids_ref.shape[0], LANES), ids_ref.dtype)], axis=0
    )
    params[0, :modes, :] = rate_ref[:, channels]
    params[0, modes : 2 * modes, :] = residue_ref[:, channels]
    for tap in range(taps):
        params[0, 2 * modes + 3 * tap : 2 * modes + 3 * tap + 3, :] = filt_ref[tap, :, channels]
    skip_row = 2 * modes + 3 * taps
    params[0, skip_row : skip_row + 1, :] = skip_ref[:, channels]

    @pl.when(source)
    def _():
        wide = gain_ref[...].astype(jnp.float32).reshape(1, width)
        gains[...] = jnp.concatenate(
            [wide[:, r * LANES : (r + 1) * LANES] for r in range(width // LANES)], axis=0
        )

    everyone_in()

    def gain_copy(d):
        return remote(gains, gains, gain_send.at[d], gain_recv.at[0], dp=dp_peers[d])

    @pl.when(source)
    def _():
        for d in range(n_dp - 1):
            gain_copy(d).start()

    sends = []

    def send(copy):
        copy.start()
        sends.append(copy)

    def half(k, which):
        return pl.ds(pl.multiple_of(k * hop_rows + which * half_rows, half_rows), half_rows)

    def z_copy(src, k, way, peer):
        piece = half(k, core)
        return remote(src.at[piece], tab.at[piece], z_send.at[way, k], z_recv.at[k], dp=peer)

    def core_copy(k):
        piece = half(k, core)
        return remote(tab.at[piece], tab.at[piece], core_send.at[k], core_recv.at[k], ctx=partner)

    def core_arrival(k):
        piece = half(k, 1 - core)
        return remote(tab.at[piece], tab.at[piece], core_send.at[k], core_recv.at[k], ctx=partner)

    can_up, can_down = at < n_dp - 1, at > 0
    def depart(k):
        @pl.when(source & can_up)
        def _():
            z_copy(table_ref, k, 0, at + 1).start()

        @pl.when(source & can_down)
        def _():
            z_copy(table_ref, k, 1, at - 1).start()

    early = min(2, hops)
    for k in range(early):
        depart(k)
    swaps = []
    for r, peer in enumerate(relatives):
        for w, weight in enumerate((wq_ref, wk_ref, wv_ref)):
            column = pl.multiple_of(flip(peer, 1) * lanes, lanes)
            swaps.append(
                remote(
                    weight.at[:, pl.ds(column, lanes)],
                    weights.at[
                        pl.ds(pl.multiple_of(core * depth, depth), depth),
                        pl.ds((r * 3 + w) * lanes, lanes),
                    ],
                    w_send.at[r * 3 + w],
                    w_recv.at[r * 3 + w],
                    ctx=partner,
                )
            )
            send(swaps[-1])

    loads[0].wait()
    groups = vocab // LANES
    lines = []
    for g in range(groups):
        block = own[g * LANES : (g + 1) * LANES, :].astype(jnp.float32)
        total = jnp.sum(block * block, axis=1, keepdims=True)
        lines.append(jnp.broadcast_to(total, (LANES, LANES)).T[:1, :])
    lines.append(jnp.zeros((SUBLANES - groups, LANES), jnp.float32))
    sums[at] = jnp.concatenate(lines, axis=0)

    for d, peer in enumerate(dp_peers):
        send(remote(sums.at[at], sums.at[at], sum_send.at[d], sum_recv.at[at], dp=peer))

    for k in range(early, hops):
        depart(k)

    @pl.when(source)
    def _():
        tab[...] = own[...]

    for d, peer in enumerate(ctx_peers):
        send(remote(all_ids.at[me], all_ids.at[me], id_send.at[d], id_recv.at[me], ctx=peer))

    def piece_of(owner, p):
        start = pl.multiple_of(owner * depth + p * piece_rows, piece_rows)
        return w_all.at[pl.ds(start, piece_rows)]

    def own_piece(way, p):
        return remote(
            wo_ref.at[pl.ds(p * piece_rows, piece_rows)],
            piece_of(me, p),
            o_send.at[way, p],
            o_recv.at[way, p],
            ctx=(side, up)[way],
        )

    def pass_piece(p):
        owner, peer = ((side, up), (up, side))[p % 2]
        return remote(piece_of(owner, p), piece_of(owner, p), q_send.at[p], q_recv.at[p], ctx=peer)

    def core_piece(which, p):
        owner = (side, up, across)[which]
        return remote(
            piece_of(owner, p), piece_of(owner, p), c_send.at[which, p], c_recv.at[which, p], ctx=partner
        )

    whole_mine = pl.ds(pl.multiple_of(me * depth, depth), depth)
    to_partner = remote(wo_ref, w_all.at[whole_mine], c_send.at[3, 0], c_recv.at[3, 0], ctx=partner)

    def offer(p):
        for way in range(2):
            send(own_piece(way, p))

    offer(0)
    offer(1)
    send(to_partner)

    def arrive(h):
        @pl.when(above)
        def _():
            z_copy(tab, h, 0, at).wait_recv()

            @pl.when(can_up)
            def _():
                z_copy(tab, h, 0, at + 1).start()

        @pl.when(below)
        def _():
            z_copy(tab, h, 1, at).wait_recv()

            @pl.when(can_down)
            def _():
                z_copy(tab, h, 1, at - 1).start()

        @pl.when(jnp.logical_not(source))
        def _():
            core_copy(h).start()

    def settle():
        for peer in dp_peers:
            remote(sums.at[peer], sums.at[peer], sum_send.at[0], sum_recv.at[peer], dp=peer).wait_recv()
        total = sums[0]
        for b in range(1, n_dp):
            total = total + sums[b]
        scale = lax.rsqrt(total / (n_dp * width) + 1e-06)
        for g in range(groups):
            scales[g * LANES : (g + 1) * LANES, :] = jnp.broadcast_to(
                scale[g : g + 1, :], (LANES, LANES)
            ).T

        @pl.when(jnp.logical_not(source))
        def _():
            gain_copy(0).wait_recv()

        for copy in loads[2:]:
            copy.wait()
        for copy in swaps:
            copy.wait_recv()

    def sides(k, way):
        start = k * part_rows + way * side_rows
        return slice(start, start + side_rows)

    def first(k, way):
        piece = pl.ds(k * part_rows + way * side_rows, side_rows)
        return remote(
            first_out.at[piece],
            first_in.at[piece],
            first_send.at[way, k],
            first_recv.at[way, k],
            ctx=(side, up)[way],
        )

    def second(k, way):
        piece = pl.ds(k * part_rows + way * side_rows, side_rows)
        return remote(
            second_out.at[piece],
            second_in.at[piece],
            second_send.at[way, k],
            second_recv.at[way, k],
            ctx=(up, side)[way],
        )

    def relay(k):
        for way in range(2):
            first(k, way).wait_recv()
            piece = sides(k, way)
            second_out[piece, :] = (
                hold[piece, :] + first_in[piece, span:].astype(jnp.float32)
            ).astype(jnp.bfloat16)
            send(second(k, way))

    each = hops // chunks
    for h in range(each):
        arrive(h)
    for k in range(chunks):
        for h in range(k * hops // chunks, (k + 1) * hops // chunks):

            @pl.when(jnp.logical_not(source))
            def _():
                core_arrival(h).wait_recv()

        if k == 0:
            settle()
            gain = jnp.concatenate([gains[r : r + 1, :] for r in range(width // LANES)], axis=1)
        piece = slice(k * part_rows, (k + 1) * part_rows)
        by_row = jnp.concatenate([scales[piece, :]] * (width // LANES), axis=1)
        normed = (tab[piece, :].astype(jnp.float32) * by_row * gain).astype(jnp.bfloat16)

        def product(r):
            return jnp.dot(
                normed, weights[:, r * span : (r + 1) * span], preferred_element_type=jnp.float32
            )

        cuts = [slice(0, side_rows), slice(side_rows, part_rows)]
        diagonal = product(3).astype(jnp.bfloat16)
        for way in range(2):
            along = product(1 + way)
            first_out[sides(k, way), :span] = along[cuts[way], :].astype(jnp.bfloat16)
            first_out[sides(k, way), span:] = diagonal[cuts[way], :]
            hold[sides(k, 1 - way), :] = along[cuts[1 - way], :]
            send(first(k, way))
            if way == 0 and k + 1 < chunks:
                arrive((k + 1) * each)
        if k + 1 < chunks:
            for h in range(1, each):
                arrive((k + 1) * each + h)
        if k > 0:
            relay(k - 1)
        mine[piece, :] = product(0)
    relay(chunks - 1)

    for peer in ctx_peers:
        remote(all_ids.at[peer], all_ids.at[peer], id_send.at[0], id_recv.at[peer], ctx=peer).wait_recv()
    names = lax.broadcasted_iota(jnp.int32, (lanes, vocab), 1)
    for s in range(segments):
        columns = jnp.concatenate(
            [all_ids[s].astype(jnp.float32), jnp.zeros((lanes - SUBLANES, lanes), jnp.float32)], axis=0
        ).T.astype(jnp.int32)
        for p in range(steps // lanes):
            start = s * steps + p * lanes
            hot[start : start + lanes, :] = (
                (columns[:, p : p + 1] == names).astype(jnp.float32).astype(jnp.bfloat16)
            )

    def dup_copy(k):
        piece = pl.ds(k * part_rows, part_rows)
        return remote(
            rows.at[0, piece], rows.at[1, piece], dup_send.at[k], dup_recv.at[k], dp=plane_outer
        )

    dup_params = remote(
        params.at[0], params.at[1], dup_send.at[chunks], dup_recv.at[chunks], dp=plane_outer
    )
    for k in range(chunks):
        for way in range(2):
            second(k, way).wait_recv()
            piece = sides(k, way)
            rows[0, piece, :] = (
                mine[piece, :]
                + first_in[piece, :span].astype(jnp.float32)
                + second_in[piece, :].astype(jnp.float32)
            ).astype(jnp.bfloat16)

        @pl.when(inner)
        def _():
            dup_copy(k).start()
            if k == 0:
                dup_params.start()

    lead = proj.shape[1] - segments * steps
    place_of = lax.broadcasted_iota(jnp.int32, (segments, lanes), 0)

    def later(value, by):
        return jnp.where(place_of >= by, pltpu.roll(value, by, 0), 0.0)

    def spread_rows(row):
        return jnp.broadcast_to(row, (segments, lanes))

    unroll = 4
    lag = turns // 2

    def turn_copy(m, plane, k, d, peer):
        piece = pl.ds(k * turn_rows, turn_rows)
        return remote(
            mixed.at[m, peer, piece],
            gathered.at[plane, piece, channels],
            a_send.at[m, k, d],
            a_recv.at[m, k, me],
            ctx=peer,
        )

    def turn_arrival(m, plane, k, peer):
        piece = pl.ds(k * turn_rows, turn_rows)
        theirs = gathered.at[plane, piece, pl.ds(pl.multiple_of(peer * lanes, lanes), lanes)]
        return remote(theirs, theirs, a_send.at[m, k, 0], a_recv.at[m, k, peer], ctx=peer)

    def mix(m, plane, between, arrived):
        for s in range(segments):
            picked = jnp.dot(
                hot[s * steps : (s + 1) * steps, :], rows[m], preferred_element_type=jnp.float32
            )
            for w in range(3):
                proj[w, pl.ds(lead + s, steps, stride=segments), :] = picked[
                    :, w * lanes : (w + 1) * lanes
                ]
        end = proj.shape[1]
        for tap in range(1, taps):
            for w in range(3):
                tail = proj[w, end - tap * segments : end - (tap - 1) * segments, :]
                proj[w, lead - tap * segments : lead - (tap - 1) * segments, :] = later(tail, 1)
        size = lanes

        def convolve(n, carry):
            start = n * size + lead
            conv = [jnp.zeros((size, lanes), jnp.float32) for _ in range(3)]
            for tap in range(taps):
                here = pl.ds(pl.multiple_of(start - tap * segments, segments), size)
                for w in range(3):
                    line = 2 * modes + 3 * tap + w
                    conv[w] = conv[w] + params[m, line : line + 1, :] * proj[w, here, :]
            there = pl.ds(pl.multiple_of(n * size, size), size)
            query[there, :] = conv[0]
            gated[there, :] = conv[1] * conv[2]
            return carry

        lax.fori_loop(0, segments * steps // size, convolve, 0)
        rate, residue = params[m, :modes, :], params[m, modes : 2 * modes, :]
        decay = [spread_rows(jnp.exp(-rate[i : i + 1, :])) for i in range(modes)]

        def ends(n, state):
            for u in range(unroll):
                here = pl.ds(pl.multiple_of((n * unroll + u) * segments, segments), segments)
                row = gated[here, :]
                state = tuple(d * s + row for d, s in zip(decay, state))
            return state

        zero = jnp.zeros((segments, lanes), jnp.float32)
        state = lax.fori_loop(0, steps // unroll, ends, (zero,) * modes)
        entering = []
        for i in range(modes):
            value = later(state[i], 1)
            by = 1
            while by < segments:
                jump = jnp.exp(-rate[i : i + 1, :] * float(steps * by))
                value = value + jump * later(value, by)
                by *= 2
            entering.append(value)
        strength = [
            spread_rows(residue[i : i + 1, :] * jnp.sqrt(2.0 * rate[i : i + 1, :]))
            for i in range(modes)
        ]
        skip = spread_rows(params[m, skip_row : skip_row + 1, :])

        def advance(n, state):
            for u in range(unroll):
                here = pl.ds(pl.multiple_of((n * unroll + u) * segments, segments), segments)
                row = gated[here, :]
                total = [skip * row, None]
                new = []
                for i in range(modes):
                    now = decay[i] * state[i] + row
                    new.append(now)
                    term = strength[i] * now
                    total[i % 2] = term if total[i % 2] is None else total[i % 2] + term
                state = tuple(new)
                query[here, :] = query[here, :] * (total[0] + total[1])
            return state

        state = tuple(entering)
        between()
        for k in range(turns):
            first_step = k * turn_rows // unroll
            state = lax.fori_loop(first_step, first_step + turn_rows // unroll, advance, state)
            piece = slice(k * turn_rows, (k + 1) * turn_rows)
            for s in range(segments):
                mixed[m, s, piece, :] = query[
                    pl.ds(k * turn_rows * segments + s, turn_rows, stride=segments), :
                ].astype(jnp.bfloat16)
            for d, peer in enumerate(ctx_peers):
                turn_copy(m, plane, k, d, peer).start()
            gathered[plane, piece, channels] = mixed[m, me, piece, :]
            if k >= lag:
                arrived(k - lag)
        for k in range(turns - lag, turns):
            arrived(k)

    def y_copy(slot, plane, k, peer):
        block = gathered.at[plane, pl.ds(k * turn_rows, turn_rows)]
        return remote(block, block, y_send.at[slot, k], y_recv.at[slot, k], dp=peer)

    def arrival(m, plane, k):
        for peer in ctx_peers:
            turn_arrival(m, plane, k, peer).wait_recv()

    def nothing(*_):
        pass

    def own_inner(k):
        @pl.when(inner)
        def _():
            arrival(0, at, k)
            y_copy(1, plane_inner, k, far_inner).start()

    def own_outer():
        for k in range(turns):
            arrival(0, at, k)
            y_copy(0, plane_outer, k, plane_inner).start()

    def take(p):
        for way in range(2):
            own_piece(way, p).wait_recv()
        send(pass_piece(p))
        for way in range(2):
            send(core_piece(way, p))

    take(0)
    take(1)
    mix(0, at, nothing, own_inner)
    offer(2)
    offer(3)

    @pl.when(outer)
    def _():
        dup_params.wait_recv()
        for k in range(chunks):
            dup_copy(k).wait_recv()
        mix(1, plane_inner, own_outer, nothing)

    acc[...] = jnp.dot(
        hot[pl.ds(pl.multiple_of(me * steps, steps), steps), :],
        own[...],
        preferred_element_type=jnp.float32,
    )

    @pl.when(inner)
    def _():
        ahead = turns // 2
        for k in range(turns + ahead):
            if k < turns:
                y_copy(1, far_inner, k, far_inner).wait_recv()
                y_copy(3, far_inner, k, plane_outer).start()
            if k >= ahead:
                y_copy(0, plane_outer, k - ahead, plane_outer).wait_recv()
                y_copy(2, plane_outer, k - ahead, far_inner).start()

    for p in range(2, pieces):
        take(p)

    @pl.when(outer)
    def _():
        for k in range(turns):
            arrival(1, plane_inner, k)
            y_copy(3, far_inner, k, plane_inner).wait_recv()

    loads[1].wait()
    to_partner.wait_recv()

    def weights_of(plane):
        return w_all[pl.ds(pl.multiple_of(plane * width, width), width), :]

    for r, peer in enumerate(relatives):

        @pl.when(inner)
        def _():
            for k in range(r * turns // chips, (r + 1) * turns // chips):
                y_copy(2, far_outer, k, far_inner).wait_recv()
                y_copy(4, far_outer, k, plane_outer).start()

        if r == 2:
            for p in range(pieces):
                pass_piece(p).wait_recv()
                send(core_piece(2, p))
        if r > 0:
            for p in range(pieces):
                core_piece(r - 1, p).wait_recv()
        plane = peer // 2

        @pl.when(plane != far_outer)
        def _():
            acc[...] += jnp.dot(
                gathered[plane], weights_of(plane), preferred_element_type=jnp.float32
            )

    for k in range(turns):

        @pl.when(outer)
        def _():
            y_copy(4, far_outer, k, plane_inner).wait_recv()

        piece = slice(k * turn_rows, (k + 1) * turn_rows)
        out_ref[piece, :] = (
            acc[piece, :]
            + jnp.dot(
                gathered[far_outer, piece, :],
                weights_of(far_outer),
                preferred_element_type=jnp.float32,
            )
        ).astype(out_ref.dtype)

    for copy in sends:
        copy.wait_send()

    @pl.when(source)
    def _():
        for d in range(n_dp - 1):
            gain_copy(d).wait_send()

    for k in range(hops):

        @pl.when((source | above) & can_up)
        def _():
            z_copy(tab, k, 0, at).wait_send()

        @pl.when((source | below) & can_down)
        def _():
            z_copy(tab, k, 1, at).wait_send()

        @pl.when(jnp.logical_not(source))
        def _():
            core_copy(k).wait_send()

    @pl.when(inner)
    def _():
        dup_params.wait_send()
        for k in range(chunks):
            dup_copy(k).wait_send()
        for k in range(turns):
            for slot, plane in ((1, plane_inner), (2, plane_outer), (3, far_inner), (4, far_outer)):
                y_copy(slot, plane, k, far_inner).wait_send()

    for k in range(turns):
        for d, peer in enumerate(ctx_peers):
            turn_copy(0, at, k, d, peer).wait_send()

    @pl.when(outer)
    def _():
        for k in range(turns):
            y_copy(0, plane_outer, k, plane_inner).wait_send()
            for d, peer in enumerate(ctx_peers):
                turn_copy(1, plane_inner, k, d, peer).wait_send()


def by_channel(
    n_ctx,
    n_dp,
    ids,
    embed_table,
    norm_gain,
    w_query,
    w_key,
    w_value,
    short_filter,
    pole_rate,
    residue,
    skip_gain,
    w_out,
):
    vocab, width = embed_table.shape
    depth, lanes = w_query.shape[0], w_query.shape[1] // n_ctx
    steps, modes, taps = ids.shape[0], pole_rate.shape[1], short_filter.shape[0]
    tokens, span = n_ctx * steps, 3 * lanes
    chips = n_ctx // 2
    chunks = vocab // LANES
    hops = 2 * chunks
    turns, pieces = 4, 4
    kind = w_query.dtype
    lines = 2 * modes + 3 * taps + 1
    lines += -lines % SUBLANES
    far = pl.BlockSpec(memory_space=pltpu.HBM)
    whole = pl.BlockSpec(memory_space=pltpu.VMEM)
    dma = pltpu.SemaphoreType.DMA
    vmem = pltpu.VMEM
    f32 = jnp.float32
    return pl.pallas_call(
        lambda *refs: block_kernel(n_ctx, n_dp, *refs),
        name="block",
        out_shape=jax.ShapeDtypeStruct((steps, w_out.shape[1]), embed_table.dtype),
        in_specs=[whole] * 6 + [far] * 5,
        out_specs=whole,
        scratch_shapes=[
            vmem((n_ctx, SUBLANES, LANES), ids.dtype),
            vmem((vocab, width), kind),
            vmem((vocab, width), kind),
            vmem((2 * depth, chips * span), kind),
            vmem((vocab, 2 * span), kind),
            vmem((vocab, 2 * span), kind),
            vmem((vocab, span), f32),
            vmem((vocab, span), kind),
            vmem((vocab, span), kind),
            vmem((vocab, span), f32),
            vmem((n_dp, SUBLANES, LANES), f32),
            vmem((vocab, LANES), f32),
            vmem((width // LANES, LANES), f32),
            vmem((2, vocab, span), kind),
            vmem((2, lines, LANES), f32),
            vmem((tokens, vocab), kind),
            vmem((3, n_ctx * (taps - 1) + tokens, lanes), f32),
            vmem((tokens, lanes), f32),
            vmem((tokens, lanes), f32),
            vmem((2, n_ctx, steps, lanes), kind),
            vmem((n_dp, steps, n_ctx * lanes), kind),
            vmem((n_ctx * depth, w_out.shape[1]), kind),
            vmem((steps, w_out.shape[1]), f32),
            dma((2, hops)),
            dma((hops,)),
            dma((hops,)),
            dma((hops,)),
            dma((chips * 3,)),
            dma((chips * 3,)),
            dma((n_ctx - 1,)),
            dma((n_ctx,)),
            dma((n_dp - 1,)),
            dma((n_dp,)),
            dma((n_dp - 1,)),
            dma((1,)),
            dma((2, chunks)),
            dma((2, chunks)),
            dma((2, chunks)),
            dma((2, chunks)),
            dma((chunks + 1,)),
            dma((chunks + 1,)),
            dma((2, turns, n_ctx - 1)),
            dma((2, turns, n_ctx)),
            dma((5, turns)),
            dma((5, turns)),
            dma((2, pieces)),
            dma((2, pieces)),
            dma((pieces,)),
            dma((pieces,)),
            dma((4, pieces)),
            dma((4, pieces)),
            dma((2 + chips * 3,)),
        ],
        compiler_params=pltpu.CompilerParams(
            collective_id=0, has_side_effects=True, vmem_limit_bytes=VMEM_BYTES
        ),
    )(
        ids.reshape(-1, LANES),
        norm_gain,
        short_filter,
        pole_rate.T,
        residue.T,
        skip_gain[None, :],
        embed_table,
        w_query,
        w_key,
        w_value,
        w_out,
    )


def solution(mesh):
    placed = (
        P("ctx"),
        P(None, "dp"),
        P("dp"),
        P("ctx", "dp"),
        P("ctx", "dp"),
        P("ctx", "dp"),
        P(None, None, "dp"),
        P("dp", None),
        P("dp", None),
        P("dp"),
        P("ctx", "dp"),
    )
    n_ctx, n_dp = mesh.shape["ctx"], mesh.shape["dp"]

    def body(*args):
        ids, table, w_query = args[0], args[1], args[3]
        fits = (
            n_ctx == SUBLANES
            and n_ctx == 2 * n_dp
            and w_query.shape[1] == n_ctx * LANES
            and table.shape[1] == 2 * w_query.shape[0]
            and table.shape[0] % LANES == 0
            and table.shape[0] < SUBLANES * LANES
            and ids.shape[0] % LANES == 0
            and ids.shape[0] < SUBLANES * LANES
        )
        if fits:
            return by_channel(n_ctx, n_dp, *args)
        return shards(*args)

    return jax.shard_map(
        body, mesh=mesh, in_specs=placed, out_specs=P("ctx", "dp"), check_vma=False
    )
```

```python
import math

import jax
import jax.numpy as jnp
from jax import lax

from jax.experimental import pallas as pl
from jax.experimental.pallas import tpu as pltpu
from jax.sharding import PartitionSpec as P

MESH = pl.DeviceIdType.MESH
LANES = 128
SUBLANES = 8
VMEM_BYTES = 56 << 20


def shifted(value, axis, steps):
    count = lax.axis_size(axis)
    initial, last = (max(0, -steps), min(count, count - steps))
    return lax.ppermute(value, axis, [(source, source + steps) for source in range(initial, last)])


def entering_2(value, axis, combine, identity):
    peers, index = (lax.axis_size(axis), lax.axis_index(axis))
    everything = jax.tree.map(lambda part: lax.all_gather(part, axis), value)
    start = jax.tree.map(
        lambda part, zero: jnp.broadcast_to(jnp.asarray(zero, part.dtype), part.shape),
        value,
        identity,
    )

    def turn(k, before):
        reached = k < index
        new = combine(before, jax.tree.map(lambda part: part[k], everything))
        return jax.tree.map(lambda a, b: jnp.where(reached, a, b), new, before)

    return lax.fori_loop(0, peers, turn, start)


def shards(
    ids,
    embed_table,
    norm_gain,
    w_query,
    w_key,
    w_value,
    short_filter,
    pole_rate,
    residue,
    skip_gain,
    w_out,
):
    highest = lax.Precision.HIGHEST
    vocab = embed_table.shape[0]
    channels = w_query.shape[1]
    one_hot = (ids[:, None] == jnp.arange(vocab, dtype=jnp.int32)[None, :]).astype(jnp.bfloat16)
    embedded = jnp.dot(one_hot, embed_table, preferred_element_type=jnp.float32).astype(
        jnp.bfloat16
    )
    full_rows, full_gain = (
        lax.all_gather(embedded, "dp", axis=1, tiled=True),
        lax.all_gather(norm_gain, "dp", axis=0, tiled=True),
    )
    floated = full_rows.astype(jnp.float32)
    scale = lax.rsqrt(jnp.mean(floated * floated, axis=1, keepdims=True) + 1e-06)
    normed = (floated * scale * full_gain.astype(jnp.float32)[None, :]).astype(jnp.bfloat16)
    tok_rows = normed.shape[0]

    def add_rows(piece):
        return jnp.dot(normed, piece, preferred_element_type=jnp.float32)

    query_proj = add_rows(lax.all_gather(w_query, "ctx", axis=0, tiled=True))
    key_proj = add_rows(lax.all_gather(w_key, "ctx", axis=0, tiled=True))
    value_proj = add_rows(lax.all_gather(w_value, "ctx", axis=0, tiled=True))
    projected = jnp.concatenate([query_proj, key_proj, value_proj], axis=1).astype(jnp.bfloat16)
    taps = short_filter.shape[0]
    previous = shifted(projected[tok_rows - (taps - 1) :], "ctx", 1)
    extended = jnp.concatenate([previous, projected], axis=0).astype(jnp.float32)
    filt_rows = short_filter.reshape(taps, 3 * channels)
    convolved = jnp.zeros((tok_rows, 3 * channels), jnp.float32)
    for tap in range(taps):
        convolved = (
            convolved
            + filt_rows[tap][None, :] * extended[taps - 1 - tap : taps - 1 - tap + tok_rows]
        )
    query_conv = convolved[:, :channels]
    gated = convolved[:, channels : 2 * channels] * convolved[:, 2 * channels :]
    sub_len = math.gcd(tok_rows, 64)
    blocks = tok_rows // sub_len
    lag_index = jnp.arange(sub_len, dtype=jnp.int32)
    lags = lag_index.astype(jnp.float32)
    strength = residue * jnp.sqrt(2.0 * pole_rate)
    kernel = jnp.einsum(
        "lck,ck->lc", jnp.exp(-pole_rate[None] * lags[:, None, None]), strength, precision=highest
    )
    offsets = lag_index[:, None] - lag_index[None, :]
    toeplitz = jnp.where((offsets >= 0)[:, :, None], kernel[jnp.maximum(offsets, 0)], 0.0)
    pieces = gated.reshape(blocks, sub_len, channels)
    inside = jnp.einsum("tsc,bsc->btc", toeplitz, pieces, precision=highest)
    tail_decay = jnp.exp(-pole_rate[None] * (sub_len - 1.0 - lags)[:, None, None])
    block_ends = jnp.einsum("sck,bsc->bck", tail_decay, pieces, precision=highest)
    step_decay = jnp.exp(-pole_rate * float(sub_len))

    def advance(state, block_end):
        return (step_decay * state + block_end, state)

    device_end, entering = lax.scan(advance, jnp.zeros_like(step_decay), block_ends)
    device_decay = jnp.exp(-pole_rate * float(tok_rows))

    def combine(earlier, later):
        return (earlier[0] * later[0], later[0] * earlier[1] + later[1])

    decay_total, incoming = entering_2(
        (device_decay, device_end),
        "ctx",
        combine,
        (jnp.ones_like(device_decay), jnp.zeros_like(device_end)),
    )
    block_pos = jnp.arange(blocks, dtype=jnp.float32) * float(sub_len)
    states_in = entering + jnp.exp(-pole_rate[None] * block_pos[:, None, None]) * incoming[None]
    lead = jnp.exp(-pole_rate[None] * (lags + 1.0)[:, None, None]) * strength[None]
    carried = jnp.einsum("tck,bck->btc", lead, states_in, precision=highest)
    long_conv = (inside + carried).reshape(tok_rows, channels) + skip_gain[None, :] * gated
    mixed = (query_conv * long_conv).astype(jnp.bfloat16)
    all_mixed = lax.all_gather(mixed, "dp", axis=1, tiled=True)
    output = jnp.dot(
        all_mixed,
        lax.all_gather(w_out, "ctx", axis=0, tiled=True),
        preferred_element_type=jnp.float32,
    )
    return (embedded.astype(jnp.float32) + output).astype(jnp.bfloat16)


def remote(src, dst, send, recv, **where):
    return pltpu.make_async_remote_copy(
        src_ref=src,
        dst_ref=dst,
        send_sem=send,
        recv_sem=recv,
        device_id=where,
        device_id_type=MESH,
    )


def greet(ctx_peers, dp_peers):
    barrier = pltpu.get_barrier_semaphore()
    for peer in ctx_peers:
        pl.semaphore_signal(barrier, inc=1, device_id={"ctx": peer}, device_id_type=MESH)
    for peer in dp_peers:
        pl.semaphore_signal(barrier, inc=1, device_id={"dp": peer}, device_id_type=MESH)
    return lambda: pl.semaphore_wait(barrier, len(ctx_peers) + len(dp_peers))


def flip(index, bit):
    return index + bit - 2 * bit * (lax.rem(index // bit, 2))


def block_kernel(
    n_ctx,
    n_dp,
    ids_ref,
    gain_ref,
    filt_ref,
    rate_ref,
    residue_ref,
    skip_ref,
    table_ref,
    wq_ref,
    wk_ref,
    wv_ref,
    wo_ref,
    out_ref,
    all_ids,
    tab,
    own,
    weights,
    first_out,
    first_in,
    hold,
    second_out,
    second_in,
    mine,
    sums,
    scales,
    gains,
    rows,
    params,
    hot,
    proj,
    gated,
    query,
    mixed,
    gathered,
    w_all,
    acc,
    result,
    z_send,
    z_recv,
    core_send,
    core_recv,
    w_send,
    w_recv,
    id_send,
    id_recv,
    sum_send,
    sum_recv,
    gain_send,
    gain_recv,
    first_send,
    first_recv,
    second_send,
    second_recv,
    dup_send,
    dup_recv,
    a_send,
    a_recv,
    y_send,
    y_recv,
    o_send,
    o_recv,
    q_send,
    q_recv,
    c_send,
    c_recv,
    local,
    leave,
):
    me, at = lax.axis_index("ctx"), lax.axis_index("dp")
    vocab, width = table_ref.shape
    depth = wq_ref.shape[0]
    lanes = wq_ref.shape[1] // n_ctx
    span = 3 * lanes
    chunks = first_send.shape[1]
    part_rows = vocab // chunks
    side_rows = part_rows // 2
    hops = z_send.shape[1]
    hop_rows = vocab // hops
    half_rows = hop_rows // 2
    segments, steps = n_ctx, out_ref.shape[0]
    turns = a_send.shape[1]
    chips = n_ctx // 2
    turn_rows = steps // turns
    taps = filt_ref.shape[0]
    modes = rate_ref.shape[0]
    pieces = o_send.shape[1]
    piece_rows = depth // pieces
    chip, core = me // 2, lax.rem(me, 2)
    partner, side, up = flip(me, 1), flip(me, 2), flip(me, 4)
    across = flip(side, 4)
    relatives = [me, side, up, across]
    ctx_peers = [lax.rem(me + d, n_ctx) for d in range(1, n_ctx)]
    dp_peers = [lax.rem(at + d, n_dp) for d in range(1, n_dp)]
    source, above, below = at == chip, at > chip, at < chip
    low = at < n_dp // 2
    outer = (at == 0) | (at == n_dp - 1)
    inner = jnp.logical_not(outer)
    plane_outer = jnp.where(low, 0, n_dp - 1)
    plane_inner = jnp.where(low, 1, n_dp - 2)
    far_inner = jnp.where(low, n_dp - 2, 1)
    far_outer = jnp.where(low, n_dp - 1, 0)
    channels = pl.ds(pl.multiple_of(me * lanes, lanes), lanes)

    everyone_in = greet(ctx_peers, dp_peers)
    loads = [
        pltpu.make_async_copy(table_ref, own, local.at[0]),
        pltpu.make_async_copy(
            wo_ref, w_all.at[pl.ds(pl.multiple_of(me * depth, depth), depth)], local.at[1]
        ),
    ]
    for r, peer in enumerate(relatives):
        for w, weight in enumerate((wq_ref, wk_ref, wv_ref)):
            column = pl.multiple_of(peer * lanes, lanes)
            loads.append(
                pltpu.make_async_copy(
                    weight.at[:, pl.ds(column, lanes)],
                    weights.at[
                        pl.ds(pl.multiple_of(core * depth, depth), depth),
                        pl.ds((r * 3 + w) * lanes, lanes),
                    ],
                    local.at[2 + r * 3 + w],
                )
            )
    for copy in loads:
        copy.start()
    all_ids[me] = jnp.concatenate(
        [ids_ref[...], jnp.zeros((SUBLANES - ids_ref.shape[0], LANES), ids_ref.dtype)], axis=0
    )
    params[0, :modes, :] = rate_ref[:, channels]
    params[0, modes : 2 * modes, :] = residue_ref[:, channels]
    for tap in range(taps):
        params[0, 2 * modes + 3 * tap : 2 * modes + 3 * tap + 3, :] = filt_ref[tap, :, channels]
    skip_row = 2 * modes + 3 * taps
    params[0, skip_row : skip_row + 1, :] = skip_ref[:, channels]

    @pl.when(source)
    def _():
        wide = gain_ref[...].astype(jnp.float32).reshape(1, width)
        gains[...] = jnp.concatenate(
            [wide[:, r * LANES : (r + 1) * LANES] for r in range(width // LANES)], axis=0
        )

    everyone_in()

    def gain_copy(d):
        return remote(gains, gains, gain_send.at[d], gain_recv.at[0], dp=dp_peers[d])

    @pl.when(source)
    def _():
        for d in range(n_dp - 1):
            gain_copy(d).start()

    sends = []

    def send(copy):
        copy.start()
        sends.append(copy)

    def half(k, which):
        return pl.ds(pl.multiple_of(k * hop_rows + which * half_rows, half_rows), half_rows)

    def z_copy(src, k, way, peer):
        piece = half(k, core)
        return remote(src.at[piece], tab.at[piece], z_send.at[way, k], z_recv.at[k], dp=peer)

    def core_copy(k):
        piece = half(k, core)
        return remote(tab.at[piece], tab.at[piece], core_send.at[k], core_recv.at[k], ctx=partner)

    def core_arrival(k):
        piece = half(k, 1 - core)
        return remote(tab.at[piece], tab.at[piece], core_send.at[k], core_recv.at[k], ctx=partner)

    can_up, can_down = at < n_dp - 1, at > 0
    def depart(k):
        @pl.when(source & can_up)
        def _():
            z_copy(table_ref, k, 0, at + 1).start()

        @pl.when(source & can_down)
        def _():
            z_copy(table_ref, k, 1, at - 1).start()

    early = min(2, hops)
    for k in range(early):
        depart(k)
    swaps = []
    for r, peer in enumerate(relatives):
        for w, weight in enumerate((wq_ref, wk_ref, wv_ref)):
            column = pl.multiple_of(flip(peer, 1) * lanes, lanes)
            swaps.append(
                remote(
                    weight.at[:, pl.ds(column, lanes)],
                    weights.at[
                        pl.ds(pl.multiple_of(core * depth, depth), depth),
                        pl.ds((r * 3 + w) * lanes, lanes),
                    ],
                    w_send.at[r * 3 + w],
                    w_recv.at[r * 3 + w],
                    ctx=partner,
                )
            )
            send(swaps[-1])

    loads[0].wait()
    groups = vocab // LANES
    lines = []
    for g in range(groups):
        block = own[g * LANES : (g + 1) * LANES, :].astype(jnp.float32)
        total = jnp.sum(block * block, axis=1, keepdims=True)
        lines.append(jnp.broadcast_to(total, (LANES, LANES)).T[:1, :])
    lines.append(jnp.zeros((SUBLANES - groups, LANES), jnp.float32))
    sums[at] = jnp.concatenate(lines, axis=0)

    for d, peer in enumerate(dp_peers):
        send(remote(sums.at[at], sums.at[at], sum_send.at[d], sum_recv.at[at], dp=peer))

    for k in range(early, hops):
        depart(k)

    @pl.when(source)
    def _():
        tab[...] = own[...]

    for d, peer in enumerate(ctx_peers):
        send(remote(all_ids.at[me], all_ids.at[me], id_send.at[d], id_recv.at[me], ctx=peer))

    def piece_of(owner, p):
        start = pl.multiple_of(owner * depth + p * piece_rows, piece_rows)
        return w_all.at[pl.ds(start, piece_rows)]

    def own_piece(way, p):
        return remote(
            wo_ref.at[pl.ds(p * piece_rows, piece_rows)],
            piece_of(me, p),
            o_send.at[way, p],
            o_recv.at[way, p],
            ctx=(side, up)[way],
        )

    def pass_piece(p):
        owner, peer = ((side, up), (up, side))[p % 2]
        return remote(piece_of(owner, p), piece_of(owner, p), q_send.at[p], q_recv.at[p], ctx=peer)

    def core_piece(which, p):
        owner = (side, up, across)[which]
        return remote(
            piece_of(owner, p), piece_of(owner, p), c_send.at[which, p], c_recv.at[which, p], ctx=partner
        )

    whole_mine = pl.ds(pl.multiple_of(me * depth, depth), depth)
    to_partner = remote(wo_ref, w_all.at[whole_mine], c_send.at[3, 0], c_recv.at[3, 0], ctx=partner)

    def offer(p):
        for way in range(2):
            send(own_piece(way, p))

    offer(0)
    offer(1)
    send(to_partner)

    def arrive(h):
        @pl.when(above)
        def _():
            z_copy(tab, h, 0, at).wait_recv()

            @pl.when(can_up)
            def _():
                z_copy(tab, h, 0, at + 1).start()

        @pl.when(below)
        def _():
            z_copy(tab, h, 1, at).wait_recv()

            @pl.when(can_down)
            def _():
                z_copy(tab, h, 1, at - 1).start()

        @pl.when(jnp.logical_not(source))
        def _():
            core_copy(h).start()

    def settle():
        for peer in dp_peers:
            remote(sums.at[peer], sums.at[peer], sum_send.at[0], sum_recv.at[peer], dp=peer).wait_recv()
        total = sums[0]
        for b in range(1, n_dp):
            total = total + sums[b]
        scale = lax.rsqrt(total / (n_dp * width) + 1e-06)
        for g in range(groups):
            scales[g * LANES : (g + 1) * LANES, :] = jnp.broadcast_to(
                scale[g : g + 1, :], (LANES, LANES)
            ).T

        @pl.when(jnp.logical_not(source))
        def _():
            gain_copy(0).wait_recv()

        for copy in loads[2:]:
            copy.wait()
        for copy in swaps:
            copy.wait_recv()

    def sides(k, way):
        start = k * part_rows + way * side_rows
        return slice(start, start + side_rows)

    def first(k, way):
        piece = pl.ds(k * part_rows + way * side_rows, side_rows)
        return remote(
            first_out.at[piece],
            first_in.at[piece],
            first_send.at[way, k],
            first_recv.at[way, k],
            ctx=(side, up)[way],
        )

    def second(k, way):
        piece = pl.ds(k * part_rows + way * side_rows, side_rows)
        return remote(
            second_out.at[piece],
            second_in.at[piece],
            second_send.at[way, k],
            second_recv.at[way, k],
            ctx=(up, side)[way],
        )

    def relay(k):
        for way in range(2):
            first(k, way).wait_recv()
            piece = sides(k, way)
            second_out[piece, :] = (
                hold[piece, :] + first_in[piece, span:].astype(jnp.float32)
            ).astype(jnp.bfloat16)
            send(second(k, way))

    each = hops // chunks
    for h in range(each):
        arrive(h)
    for k in range(chunks):
        for h in range(k * hops // chunks, (k + 1) * hops // chunks):

            @pl.when(jnp.logical_not(source))
            def _():
                core_arrival(h).wait_recv()

        if k == 0:
            settle()
            gain = jnp.concatenate([gains[r : r + 1, :] for r in range(width // LANES)], axis=1)
        piece = slice(k * part_rows, (k + 1) * part_rows)
        by_row = jnp.concatenate([scales[piece, :]] * (width // LANES), axis=1)
        normed = (tab[piece, :].astype(jnp.float32) * by_row * gain).astype(jnp.bfloat16)

        def product(r):
            return jnp.dot(
                normed, weights[:, r * span : (r + 1) * span], preferred_element_type=jnp.float32
            )

        cuts = [slice(0, side_rows), slice(side_rows, part_rows)]
        diagonal = product(3).astype(jnp.bfloat16)
        for way in range(2):
            along = product(1 + way)
            first_out[sides(k, way), :span] = along[cuts[way], :].astype(jnp.bfloat16)
            first_out[sides(k, way), span:] = diagonal[cuts[way], :]
            hold[sides(k, 1 - way), :] = along[cuts[1 - way], :]
            send(first(k, way))
            if way == 0 and k + 1 < chunks:
                arrive((k + 1) * each)
        if k + 1 < chunks:
            for h in range(1, each):
                arrive((k + 1) * each + h)
        if k > 0:
            relay(k - 1)
        mine[piece, :] = product(0)
    relay(chunks - 1)

    for peer in ctx_peers:
        remote(all_ids.at[peer], all_ids.at[peer], id_send.at[0], id_recv.at[peer], ctx=peer).wait_recv()
    names = lax.broadcasted_iota(jnp.int32, (lanes, vocab), 1)
    for s in range(segments):
        columns = jnp.concatenate(
            [all_ids[s].astype(jnp.float32), jnp.zeros((lanes - SUBLANES, lanes), jnp.float32)], axis=0
        ).T.astype(jnp.int32)
        for p in range(steps // lanes):
            start = s * steps + p * lanes
            hot[start : start + lanes, :] = (
                (columns[:, p : p + 1] == names).astype(jnp.float32).astype(jnp.bfloat16)
            )

    def dup_copy(k):
        piece = pl.ds(k * part_rows, part_rows)
        return remote(
            rows.at[0, piece], rows.at[1, piece], dup_send.at[k], dup_recv.at[k], dp=plane_outer
        )

    dup_params = remote(
        params.at[0], params.at[1], dup_send.at[chunks], dup_recv.at[chunks], dp=plane_outer
    )
    for k in range(chunks):
        for way in range(2):
            second(k, way).wait_recv()
            piece = sides(k, way)
            rows[0, piece, :] = (
                mine[piece, :]
                + first_in[piece, :span].astype(jnp.float32)
                + second_in[piece, :].astype(jnp.float32)
            ).astype(jnp.bfloat16)

        @pl.when(inner)
        def _():
            dup_copy(k).start()
            if k == 0:
                dup_params.start()

    lead = proj.shape[1] - segments * steps
    place_of = lax.broadcasted_iota(jnp.int32, (segments, lanes), 0)

    def later(value, by):
        return jnp.where(place_of >= by, pltpu.roll(value, by, 0), 0.0)

    def spread_rows(row):
        return jnp.broadcast_to(row, (segments, lanes))

    unroll = 8
    lag = turns - 1

    def turn_copy(m, plane, k, d, peer):
        piece = pl.ds(k * turn_rows, turn_rows)
        return remote(
            mixed.at[m, peer, piece],
            gathered.at[plane, piece, channels],
            a_send.at[m, k, d],
            a_recv.at[m, k, me],
            ctx=peer,
        )

    def turn_arrival(m, plane, k, peer):
        piece = pl.ds(k * turn_rows, turn_rows)
        theirs = gathered.at[plane, piece, pl.ds(pl.multiple_of(peer * lanes, lanes), lanes)]
        return remote(theirs, theirs, a_send.at[m, k, 0], a_recv.at[m, k, peer], ctx=peer)

    def mix(m, plane, between, arrived):
        for s in range(segments):
            picked = jnp.dot(
                hot[s * steps : (s + 1) * steps, :], rows[m], preferred_element_type=jnp.float32
            )
            for w in range(3):
                proj[w, pl.ds(lead + s, steps, stride=segments), :] = picked[
                    :, w * lanes : (w + 1) * lanes
                ]
        end = proj.shape[1]
        for tap in range(1, taps):
            for w in range(3):
                tail = proj[w, end - tap * segments : end - (tap - 1) * segments, :]
                proj[w, lead - tap * segments : lead - (tap - 1) * segments, :] = later(tail, 1)
        size = lanes

        def convolve(n, carry):
            start = n * size + lead
            conv = [jnp.zeros((size, lanes), jnp.float32) for _ in range(3)]
            for tap in range(taps):
                here = pl.ds(pl.multiple_of(start - tap * segments, segments), size)
                for w in range(3):
                    line = 2 * modes + 3 * tap + w
                    conv[w] = conv[w] + params[m, line : line + 1, :] * proj[w, here, :]
            there = pl.ds(pl.multiple_of(n * size, size), size)
            query[there, :] = conv[0]
            gated[there, :] = conv[1] * conv[2]
            return carry

        lax.fori_loop(0, segments * steps // size, convolve, 0)
        rate, residue = params[m, :modes, :], params[m, modes : 2 * modes, :]
        decay = [spread_rows(jnp.exp(-rate[i : i + 1, :])) for i in range(modes)]

        def ends(n, state):
            for u in range(unroll):
                here = pl.ds(pl.multiple_of((n * unroll + u) * segments, segments), segments)
                row = gated[here, :]
                state = tuple(d * s + row for d, s in zip(decay, state))
            return state

        zero = jnp.zeros((segments, lanes), jnp.float32)
        state = lax.fori_loop(0, steps // unroll, ends, (zero,) * modes)
        entering = []
        for i in range(modes):
            value = later(state[i], 1)
            by = 1
            while by < segments:
                jump = jnp.exp(-rate[i : i + 1, :] * float(steps * by))
                value = value + jump * later(value, by)
                by *= 2
            entering.append(value)
        strength = [
            spread_rows(residue[i : i + 1, :] * jnp.sqrt(2.0 * rate[i : i + 1, :]))
            for i in range(modes)
        ]
        skip = spread_rows(params[m, skip_row : skip_row + 1, :])

        def advance(n, state):
            for u in range(unroll):
                here = pl.ds(pl.multiple_of((n * unroll + u) * segments, segments), segments)
                row = gated[here, :]
                total = [skip * row, None]
                new = []
                for i in range(modes):
                    now = decay[i] * state[i] + row
                    new.append(now)
                    term = strength[i] * now
                    total[i % 2] = term if total[i % 2] is None else total[i % 2] + term
                state = tuple(new)
                query[here, :] = query[here, :] * (total[0] + total[1])
            return state

        state = tuple(entering)
        between()
        for k in range(turns):
            first_step = k * turn_rows // unroll
            state = lax.fori_loop(first_step, first_step + turn_rows // unroll, advance, state)
            piece = slice(k * turn_rows, (k + 1) * turn_rows)
            for s in range(segments):
                mixed[m, s, piece, :] = query[
                    pl.ds(k * turn_rows * segments + s, turn_rows, stride=segments), :
                ].astype(jnp.bfloat16)
            for d, peer in enumerate(ctx_peers):
                turn_copy(m, plane, k, d, peer).start()
            gathered[plane, piece, channels] = mixed[m, me, piece, :]
            if k >= lag:
                arrived(k - lag)
        for k in range(turns - lag, turns):
            arrived(k)

    def y_copy(slot, plane, k, peer):
        block = gathered.at[plane, pl.ds(k * turn_rows, turn_rows)]
        return remote(block, block, y_send.at[slot, k], y_recv.at[slot, k], dp=peer)

    def arrival(m, plane, k):
        for peer in ctx_peers:
            turn_arrival(m, plane, k, peer).wait_recv()

    def nothing(*_):
        pass

    def own_inner(k):
        @pl.when(inner)
        def _():
            arrival(0, at, k)
            y_copy(1, plane_inner, k, far_inner).start()

    def own_outer():
        for k in range(turns):
            arrival(0, at, k)
            y_copy(0, plane_outer, k, plane_inner).start()

    def take(p):
        for way in range(2):
            own_piece(way, p).wait_recv()
        send(pass_piece(p))
        for way in range(2):
            send(core_piece(way, p))

    take(0)
    take(1)
    mix(0, at, nothing, own_inner)
    offer(2)
    offer(3)

    @pl.when(outer)
    def _():
        dup_params.wait_recv()
        for k in range(chunks):
            dup_copy(k).wait_recv()
        mix(1, plane_inner, own_outer, nothing)

    acc[...] = jnp.dot(
        hot[pl.ds(pl.multiple_of(me * steps, steps), steps), :],
        own[...],
        preferred_element_type=jnp.float32,
    )

    @pl.when(inner)
    def _():
        ahead = turns // 2
        for k in range(turns + ahead):
            if k < turns:
                y_copy(1, far_inner, k, far_inner).wait_recv()
                y_copy(3, far_inner, k, plane_outer).start()
            if k >= ahead:
                y_copy(0, plane_outer, k - ahead, plane_outer).wait_recv()
                y_copy(2, plane_outer, k - ahead, far_inner).start()

    for p in range(2, pieces):
        take(p)

    @pl.when(outer)
    def _():
        for k in range(turns):
            arrival(1, plane_inner, k)
            y_copy(3, far_inner, k, plane_inner).wait_recv()

    loads[1].wait()
    to_partner.wait_recv()

    def weights_of(plane):
        return w_all[pl.ds(pl.multiple_of(plane * width, width), width), :]

    for r, peer in enumerate(relatives):

        @pl.when(inner)
        def _():
            for k in range(r * turns // chips, (r + 1) * turns // chips):
                y_copy(2, far_outer, k, far_inner).wait_recv()
                y_copy(4, far_outer, k, plane_outer).start()

        if r == 2:
            for p in range(pieces):
                pass_piece(p).wait_recv()
                send(core_piece(2, p))
        if r > 0:
            for p in range(pieces):
                core_piece(r - 1, p).wait_recv()
        plane = peer // 2

        @pl.when(plane != far_outer)
        def _():
            acc[...] += jnp.dot(
                gathered[plane], weights_of(plane), preferred_element_type=jnp.float32
            )

    leaving = []
    for k in range(turns):

        @pl.when(outer)
        def _():
            y_copy(4, far_outer, k, plane_inner).wait_recv()

        piece = pl.ds(k * turn_rows, turn_rows)
        result[piece, :] = (
            acc[piece, :]
            + jnp.dot(
                gathered[far_outer, piece, :],
                weights_of(far_outer),
                preferred_element_type=jnp.float32,
            )
        ).astype(out_ref.dtype)
        leaving.append(
            pltpu.make_async_copy(result.at[piece], out_ref.at[piece], leave.at[k])
        )
        leaving[-1].start()

    for copy in sends:
        copy.wait_send()
    for copy in leaving:
        copy.wait()

    @pl.when(source)
    def _():
        for d in range(n_dp - 1):
            gain_copy(d).wait_send()

    for k in range(hops):

        @pl.when((source | above) & can_up)
        def _():
            z_copy(tab, k, 0, at).wait_send()

        @pl.when((source | below) & can_down)
        def _():
            z_copy(tab, k, 1, at).wait_send()

        @pl.when(jnp.logical_not(source))
        def _():
            core_copy(k).wait_send()

    @pl.when(inner)
    def _():
        dup_params.wait_send()
        for k in range(chunks):
            dup_copy(k).wait_send()
        for k in range(turns):
            for slot, plane in ((1, plane_inner), (2, plane_outer), (3, far_inner), (4, far_outer)):
                y_copy(slot, plane, k, far_inner).wait_send()

    for k in range(turns):
        for d, peer in enumerate(ctx_peers):
            turn_copy(0, at, k, d, peer).wait_send()

    @pl.when(outer)
    def _():
        for k in range(turns):
            y_copy(0, plane_outer, k, plane_inner).wait_send()
            for d, peer in enumerate(ctx_peers):
                turn_copy(1, plane_inner, k, d, peer).wait_send()


def by_channel(
    n_ctx,
    n_dp,
    ids,
    embed_table,
    norm_gain,
    w_query,
    w_key,
    w_value,
    short_filter,
    pole_rate,
    residue,
    skip_gain,
    w_out,
):
    vocab, width = embed_table.shape
    depth, lanes = w_query.shape[0], w_query.shape[1] // n_ctx
    steps, modes, taps = ids.shape[0], pole_rate.shape[1], short_filter.shape[0]
    tokens, span = n_ctx * steps, 3 * lanes
    chips = n_ctx // 2
    chunks = vocab // LANES
    hops = 2 * chunks
    turns, pieces = 4, 4
    kind = w_query.dtype
    lines = 2 * modes + 3 * taps + 1
    lines += -lines % SUBLANES
    far = pl.BlockSpec(memory_space=pltpu.HBM)
    whole = pl.BlockSpec(memory_space=pltpu.VMEM)
    dma = pltpu.SemaphoreType.DMA
    vmem = pltpu.VMEM
    f32 = jnp.float32
    return pl.pallas_call(
        lambda *refs: block_kernel(n_ctx, n_dp, *refs),
        name="block",
        out_shape=jax.ShapeDtypeStruct((steps, w_out.shape[1]), embed_table.dtype),
        in_specs=[whole] * 6 + [far] * 5,
        out_specs=pl.BlockSpec(memory_space=pl.ANY),
        scratch_shapes=[
            vmem((n_ctx, SUBLANES, LANES), ids.dtype),
            vmem((vocab, width), kind),
            vmem((vocab, width), kind),
            vmem((2 * depth, chips * span), kind),
            vmem((vocab, 2 * span), kind),
            vmem((vocab, 2 * span), kind),
            vmem((vocab, span), f32),
            vmem((vocab, span), kind),
            vmem((vocab, span), kind),
            vmem((vocab, span), f32),
            vmem((n_dp, SUBLANES, LANES), f32),
            vmem((vocab, LANES), f32),
            vmem((width // LANES, LANES), f32),
            vmem((2, vocab, span), kind),
            vmem((2, lines, LANES), f32),
            vmem((tokens, vocab), kind),
            vmem((3, n_ctx * (taps - 1) + tokens, lanes), f32),
            vmem((tokens, lanes), f32),
            vmem((tokens, lanes), f32),
            vmem((2, n_ctx, steps, lanes), kind),
            vmem((n_dp, steps, n_ctx * lanes), kind),
            vmem((n_ctx * depth, w_out.shape[1]), kind),
            vmem((steps, w_out.shape[1]), f32),
            vmem((steps, w_out.shape[1]), embed_table.dtype),
            dma((2, hops)),
            dma((hops,)),
            dma((hops,)),
            dma((hops,)),
            dma((chips * 3,)),
            dma((chips * 3,)),
            dma((n_ctx - 1,)),
            dma((n_ctx,)),
            dma((n_dp - 1,)),
            dma((n_dp,)),
            dma((n_dp - 1,)),
            dma((1,)),
            dma((2, chunks)),
            dma((2, chunks)),
            dma((2, chunks)),
            dma((2, chunks)),
            dma((chunks + 1,)),
            dma((chunks + 1,)),
            dma((2, turns, n_ctx - 1)),
            dma((2, turns, n_ctx)),
            dma((5, turns)),
            dma((5, turns)),
            dma((2, pieces)),
            dma((2, pieces)),
            dma((pieces,)),
            dma((pieces,)),
            dma((4, pieces)),
            dma((4, pieces)),
            dma((2 + chips * 3,)),
            dma((turns,)),
        ],
        compiler_params=pltpu.CompilerParams(
            collective_id=0, has_side_effects=True, vmem_limit_bytes=VMEM_BYTES
        ),
    )(
        ids.reshape(-1, LANES),
        norm_gain,
        short_filter,
        pole_rate.T,
        residue.T,
        skip_gain[None, :],
        embed_table,
        w_query,
        w_key,
        w_value,
        w_out,
    )


def solution(mesh):
    placed = (
        P("ctx"),
        P(None, "dp"),
        P("dp"),
        P("ctx", "dp"),
        P("ctx", "dp"),
        P("ctx", "dp"),
        P(None, None, "dp"),
        P("dp", None),
        P("dp", None),
        P("dp"),
        P("ctx", "dp"),
    )
    n_ctx, n_dp = mesh.shape["ctx"], mesh.shape["dp"]

    def body(*args):
        ids, table, w_query = args[0], args[1], args[3]
        fits = (
            n_ctx == SUBLANES
            and n_ctx == 2 * n_dp
            and w_query.shape[1] == n_ctx * LANES
            and table.shape[1] == 2 * w_query.shape[0]
            and table.shape[0] % LANES == 0
            and table.shape[0] < SUBLANES * LANES
            and ids.shape[0] % LANES == 0
            and ids.shape[0] < SUBLANES * LANES
        )
        if fits:
            return by_channel(n_ctx, n_dp, *args)
        return shards(*args)

    return jax.shard_map(
        body, mesh=mesh, in_specs=placed, out_specs=P("ctx", "dp"), check_vma=False
    )
```
